32 devices in a mesh: section: 4 (over x, core), ctx: 8 (over z, y).
Axes of the slice: x: 2, y: 2, z: 4, core: 2. Of those that a mesh axis runs over, the one named last changes fastest.
Arguments:
- block_order: int32 [8], replicated, may hold values from 0 to 7, each once
- queries: bfloat16 [4, 64, 2560], P('section', 'ctx'), may hold values from -400 to 400
- cache_keys: bfloat16 [1024, 2560], P('ctx', 'section'), may hold values from -6 to 6
- cache_values: bfloat16 [1024, 2560], P('ctx', 'section'), may hold values from -6 to 6
- attention_out: bfloat16 [4, 64, 2560], P('section', 'ctx'), may hold values from -6 to 6
- output_grad: bfloat16 [4, 64, 2560], P('section', 'ctx'), may hold values from -192 to 192
Outputs:
- grad_queries: bfloat16 [4, 64, 2560], P('section', 'ctx')
- grad_keys: bfloat16 [1024, 2560], P('ctx', 'section')
- grad_values: bfloat16 [1024, 2560], P('ctx', 'section')
The draws below stay inside these ranges and needn't reach their ends.
Inputs may be any that keep to these rules, and one draw needn't show every extreme that they name: `block_order`: every block number once.
All inputs are finite; a program needn't handle non-finite values.
Results may differ from the reference program's by a relative error of at most 0.012.
Values may be sent and summed in bfloat16 or wider, within the bound.
No kernel may reach another device: no remote copies, remote signals or barrier semaphores. Data moves between devices by JAX's collectives and lax.ppermute only.
A program may use at most 64 MiB of HBM per device.

```python
import jax
import jax.numpy as jnp
from jax import lax

HEADS = 20
HEAD_DIM = 128
KV_DEV = 128
QR = 8
KV_LEN = 1024
QW = 64
LAYERS = 4
N_SECTION = 4
N_CTX = 8


def shared_plan(key):
    base_key = jax.random.fold_in(key, 101)
    key_total = KV_DEV * N_CTX
    features = HEADS * HEAD_DIM
    key_a = jax.random.fold_in(base_key, 0)
    cache_keys = jax.random.truncated_normal(key_a, -6.0, 6.0, (key_total, features))
    return cache_keys


def draw_cache_keys(key, part):
    cache_keys = shared_plan(key)
    return cache_keys.astype(jnp.bfloat16)


def draw_queries(key, part):
    base_key = jax.random.fold_in(key, 202)
    shape = (N_SECTION, QR * N_CTX, HEADS * HEAD_DIM)
    values = jax.random.truncated_normal(base_key, -6.0, 6.0, shape)
    return values.astype(jnp.bfloat16)


def draw_output_grad(key, part):
    base_key = jax.random.fold_in(key, 303)
    spread = KV_DEV * N_CTX / 32.0
    shape = (N_SECTION, QR * N_CTX, HEADS * HEAD_DIM)
    values = jax.random.truncated_normal(base_key, -6.0, 6.0, shape) * spread
    return values.astype(jnp.bfloat16)


def steps_of(stream_key, dims, pieces, least, high):
    loudness, own = 1.0, jax.random.fold_in(stream_key, 6)
    for axis_at, parts in pieces:
        steps = jnp.exp(jax.random.uniform(jax.random.fold_in(own, axis_at), (parts,), jnp.float32, least / len(pieces), high / len(pieces)))
        loudness = loudness * jnp.repeat(steps, dims[axis_at] // parts).reshape([-1 if axis == axis_at else 1 for axis in range(len(dims))])
    return loudness


def scatter_about(stream_key, extent, scale, limit, shards=(), kind=jnp.bfloat16):
    values = scale * jax.random.normal(stream_key, extent, jnp.float32)
    if shards:
        values = values * steps_of(stream_key, extent, shards, -0.22, 0.18)
    return jnp.clip(values, -limit, limit).astype(kind)


def setup_inputs(seed: int = 0) -> dict:
    key_of = jax.random.split(jax.random.key(seed), 7)
    return {
        "block_order": jax.random.permutation(key_of[0], N_CTX).astype(jnp.int32),
        "queries": draw_queries(jax.random.fold_in(key_of[6], 71), 0),
        "cache_keys": draw_cache_keys(jax.random.fold_in(key_of[6], 71), 0),
        "cache_values": scatter_about(key_of[3], (KV_LEN, HEADS * HEAD_DIM), 1.0, 6.0, ((0, 8), (1, 4))),
        "attention_out": scatter_about(key_of[4], (LAYERS, QW, HEADS * HEAD_DIM), 1.0, 6.0, ((0, 4), (1, 8))),
        "output_grad": draw_output_grad(jax.random.fold_in(key_of[6], 71), 0),
    }


masked_score = -1e30


def reference(block_order, queries, cache_keys, cache_values, attention_out, output_grad):
    key_total = cache_keys.shape[0]
    query_count = queries.shape[1]
    features = cache_keys.shape[1]
    scaling = HEAD_DIM ** -0.5
    key_rows = jnp.arange(key_total, dtype=jnp.int32)
    key_pos = block_order[key_rows // KV_DEV].astype(jnp.int32) * KV_DEV + key_rows % KV_DEV
    query_pos = key_total - query_count + jnp.arange(query_count, dtype=jnp.int32)
    visible = key_pos[None, :] <= query_pos[:, None]
    key_heads = cache_keys.reshape(key_total, HEADS, HEAD_DIM).transpose(1, 0, 2)
    value_heads = cache_values.reshape(key_total, HEADS, HEAD_DIM).transpose(1, 0, 2)

    def layer_step(running, layer_data):
        query_one, grad_one, out_one = layer_data
        delta_terms = jnp.sum((grad_one.astype(jnp.float32) * out_one.astype(jnp.float32)).reshape(query_count, HEADS, HEAD_DIM), axis=2).T
        query_heads = query_one.reshape(query_count, HEADS, HEAD_DIM).transpose(1, 0, 2)
        grad_heads = grad_one.reshape(query_count, HEADS, HEAD_DIM).transpose(1, 0, 2)

        def head_step(packed):
            query_head, grad_head, delta_head, key_head, value_head = packed
            scores = jnp.dot(query_head, key_head.T, preferred_element_type=jnp.float32) * scaling
            scores = jnp.where(visible, scores, masked_score)
            row_max = jnp.max(scores, axis=1, keepdims=True)
            row_sum = jnp.sum(jnp.where(visible, jnp.exp(scores - row_max), 0.0), axis=1, keepdims=True)
            log_total = row_max + jnp.log(row_sum)
            prob = jnp.where(visible, jnp.exp(scores - log_total), 0.0)
            prob_b = prob.astype(jnp.bfloat16)
            value_grad = jnp.dot(prob_b.T, grad_head, preferred_element_type=jnp.float32)
            prob_grad = jnp.dot(grad_head, value_head.T, preferred_element_type=jnp.float32)
            score_grad = (prob * (prob_grad - delta_head[:, None]) * scaling).astype(jnp.bfloat16)
            query_grad = jnp.dot(score_grad, key_head, preferred_element_type=jnp.float32)
            key_grad = jnp.dot(score_grad.T, query_head, preferred_element_type=jnp.float32)
            return query_grad, key_grad, value_grad

        query_grad, key_grad, value_grad = lax.map(head_step, (query_heads, grad_heads, delta_terms, key_heads, value_heads))
        return (running[0] + key_grad, running[1] + value_grad), query_grad

    zeros = jnp.zeros((HEADS, key_total, HEAD_DIM), jnp.float32)
    sums, query_grads = lax.scan(layer_step, (zeros, zeros), (queries, output_grad, attention_out))
    grad_queries = query_grads.transpose(0, 2, 1, 3).reshape(queries.shape[0], query_count, features).astype(jnp.bfloat16)
    grad_keys = sums[0].transpose(1, 0, 2).reshape(key_total, features).astype(jnp.bfloat16)
    grad_values = sums[1].transpose(1, 0, 2).reshape(key_total, features).astype(jnp.bfloat16)
    return grad_queries, grad_keys, grad_values
```

```python
import jax
import jax.numpy as jnp
from jax import lax
from jax.experimental import pallas as pl
from jax.experimental.pallas import tpu as pltpu
from jax.sharding import PartitionSpec as P

HEAD_DIM = 128
LANES = 128
masked_score = -1e30
BF = jnp.bfloat16
F32 = jnp.float32


def nt(a, b):
    return lax.dot_general(a, b, (((1,), (1,)), ((), ())), preferred_element_type=F32)


def nn(a, b):
    return lax.dot_general(a, b, (((1,), (0,)), ((), ())), preferred_element_type=F32)


def tn(a, b):
    return lax.dot_general(a, b, (((0,), (0,)), ((), ())), preferred_element_type=F32)


def split3(x):
    hi = x.astype(BF)
    rest = x - hi.astype(F32)
    mid = rest.astype(BF)
    low = (rest - mid.astype(F32)).astype(BF)
    return hi, mid, low


def pack(queries, grads, outs, sections, copies):
    rows, features = queries.shape
    here = features // sections
    heads = here // HEAD_DIM
    width = 2 * here + LANES

    def body(q_ref, g_ref, o_ref, out_ref):
        lane = lax.broadcasted_iota(jnp.int32, (rows, LANES), 1)
        for s in range(sections):
            extra = jnp.zeros((rows, LANES), F32)
            for h in range(heads):
                at = pl.ds(s * here + h * HEAD_DIM, HEAD_DIM)
                terms = g_ref[:, at].astype(F32) * o_ref[:, at].astype(F32)
                delta = jnp.sum(terms, axis=1, keepdims=True)
                for part, value in enumerate(split3(delta)):
                    extra = jnp.where(lane == part * heads + h, value.astype(F32), extra)
            q = q_ref[:, pl.ds(s * here, here)]
            g = g_ref[:, pl.ds(s * here, here)]
            e = extra.astype(BF)

            @pl.loop(0, copies)
            def _(c):
                out_ref[s, c, :, pl.ds(0, here)] = q
                out_ref[s, c, :, pl.ds(here, here)] = g
                out_ref[s, c, :, pl.ds(2 * here, LANES)] = e

    return pl.pallas_call(
        body,
        out_shape=jax.ShapeDtypeStruct((sections, copies, rows, width), BF),
        name="pack",
    )(queries, grads, outs)


def visible_of(start_ref, shape, row_count, key_total):
    key_pos = start_ref[0] + lax.broadcasted_iota(jnp.int32, shape, 0)
    row = lax.broadcasted_iota(jnp.int32, shape, 1) % row_count
    return key_pos <= key_total - row_count + row


def stats_kernel(start, packed, keys, row_count, key_total, heads):
    m = packed.shape[0]
    key_count = keys.shape[0]
    scaling = HEAD_DIM ** (-0.5)

    def body(start_ref, q_ref, k_ref, out_ref):
        h = pl.program_id(0)
        shape = (key_count, m)
        visible = visible_of(start_ref, shape, row_count, key_total)
        s = jnp.where(visible, nt(k_ref[...], q_ref[...]) * scaling, masked_score)
        top = jnp.max(s, axis=0, keepdims=True)
        total = jnp.sum(jnp.where(visible, jnp.exp(s - top), 0.0), axis=0, keepdims=True)

        @pl.when(h == 0)
        def _():
            out_ref[...] = jnp.ones_like(out_ref)

        out_ref[0, pl.ds(h, 1), :] = top
        out_ref[1, pl.ds(h, 1), :] = total

    return pl.pallas_call(
        body,
        grid_spec=pltpu.PrefetchScalarGridSpec(
            num_scalar_prefetch=1,
            grid=(heads,),
            in_specs=[
                pl.BlockSpec((m, HEAD_DIM), lambda h, s: (0, h)),
                pl.BlockSpec((key_count, HEAD_DIM), lambda h, s: (0, h)),
            ],
            out_specs=pl.BlockSpec((2, 8, m), lambda h, s: (0, 0, 0)),
        ),
        out_shape=jax.ShapeDtypeStruct((2, 8, m), F32),
        name="stats",
    )(start, packed, keys)


def gradient_kernel(start, packed, keys, values, log_total, row_count, key_total, heads):
    m = packed.shape[0]
    key_count, here = keys.shape
    scaling = HEAD_DIM ** (-0.5)

    def body(start_ref, q_ref, g_ref, e_ref, k_ref, v_ref, l_ref, u_ref, dk_ref, dv_ref):
        h = pl.program_id(0)
        shape = (key_count, m)
        visible = visible_of(start_ref, shape, row_count, key_total)
        q, g, k, v = q_ref[...], g_ref[...], k_ref[...], v_ref[...]
        lane = lax.broadcasted_iota(jnp.int32, (8, LANES), 1)
        pick = (lane == h) | (lane == heads + h) | (lane == 2 * heads + h)
        delta = nt(jnp.where(pick, 1.0, 0.0).astype(BF), e_ref[...])[0:1, :]
        s = nt(k, q) * scaling
        prob = jnp.where(visible, jnp.exp(s - l_ref[pl.ds(h, 1), :]), 0.0)
        ds = (prob * (nt(v, g) - delta) * scaling).astype(BF)
        dv_ref[...] = nn(prob.astype(BF), g).astype(BF)
        dk_ref[...] = nn(ds, q).astype(BF)
        u_ref[...] = tn(ds, k).astype(BF)

    return pl.pallas_call(
        body,
        grid_spec=pltpu.PrefetchScalarGridSpec(
            num_scalar_prefetch=1,
            grid=(heads,),
            in_specs=[
                pl.BlockSpec((m, HEAD_DIM), lambda h, s: (0, h)),
                pl.BlockSpec((m, HEAD_DIM), lambda h, s: (0, heads + h)),
                pl.BlockSpec((m, LANES), lambda h, s: (0, 2 * heads)),
                pl.BlockSpec((key_count, HEAD_DIM), lambda h, s: (0, h)),
                pl.BlockSpec((key_count, HEAD_DIM), lambda h, s: (0, h)),
                pl.BlockSpec((8, m), lambda h, s: (0, 0)),
            ],
            out_specs=[
                pl.BlockSpec((m, HEAD_DIM), lambda h, s: (0, h)),
                pl.BlockSpec((key_count, HEAD_DIM), lambda h, s: (0, h)),
                pl.BlockSpec((key_count, HEAD_DIM), lambda h, s: (0, h)),
            ],
        ),
        out_shape=[
            jax.ShapeDtypeStruct((m, here), BF),
            jax.ShapeDtypeStruct((key_count, here), BF),
            jax.ShapeDtypeStruct((key_count, here), BF),
        ],
        name="gradients",
    )(start, packed, packed, packed, keys, values, log_total)


def merge_stats(stats, axis, count):
    step = count // 2
    while step:
        other = lax.ppermute(stats, axis, [(i, i ^ step) for i in range(count)])
        top = jnp.maximum(stats[0], other[0])
        total = stats[1] * jnp.exp(stats[0] - top) + other[1] * jnp.exp(other[0] - top)
        stats = jnp.stack([top, total])
        step //= 2
    return stats


def local(block_order, queries, cache_keys, cache_values, attention_out, output_grad):
    sections = lax.axis_size("section")
    ctx_count = lax.axis_size("ctx")
    assert ctx_count & (ctx_count - 1) == 0
    layers, rows, features = queries.shape
    assert layers == 1
    key_count, here = cache_keys.shape
    heads = here // HEAD_DIM
    row_count = rows * ctx_count
    key_total = key_count * ctx_count
    start = (block_order[lax.axis_index("ctx")] * key_count).reshape(1)

    sent = pack(queries[0], output_grad[0], attention_out[0], sections, ctx_count)
    width = sent.shape[-1]
    sent = sent.reshape(sections * ctx_count, rows, width)
    packed = lax.all_to_all(sent, ("section", "ctx"), 0, 0, tiled=True)
    packed = packed.reshape(sections * row_count, width)

    stats = stats_kernel(start, packed, cache_keys, row_count, key_total, heads)
    stats = merge_stats(stats, "ctx", ctx_count)
    log_total = stats[0] + jnp.log(stats[1])
    part, grad_keys, grad_values = gradient_kernel(
        start, packed, cache_keys, cache_values, log_total, row_count, key_total, heads
    )
    part = part.reshape(sections * ctx_count, rows, here)
    part = lax.all_to_all(part, ("section", "ctx"), 0, 0, tiled=True)
    part = part.reshape(sections, ctx_count, rows, here).astype(F32).sum(axis=1)
    grad_queries = part.transpose(1, 0, 2).reshape(1, rows, features).astype(BF)
    return (grad_queries, grad_keys, grad_values)


def solution(mesh):
    in_specs = (
        P(),
        P("section", "ctx", None),
        P("ctx", "section"),
        P("ctx", "section"),
        P("section", "ctx", None),
        P("section", "ctx", None),
    )
    out_specs = (P("section", "ctx", None), P("ctx", "section"), P("ctx", "section"))
    return jax.shard_map(local, mesh=mesh, in_specs=in_specs, out_specs=out_specs, check_vma=False)
```

```python
import jax
import jax.numpy as jnp
from jax import lax
from jax.experimental import pallas as pl
from jax.experimental.pallas import tpu as pltpu
from jax.sharding import PartitionSpec as P


HEAD_DIM = 128
LANES = 128
masked_score = -1e30
BF = jnp.bfloat16
F32 = jnp.float32


def nt(a, b):
    return lax.dot_general(a, b, (((1,), (1,)), ((), ())), preferred_element_type=F32)


def nn(a, b):
    return lax.dot_general(a, b, (((1,), (0,)), ((), ())), preferred_element_type=F32)


def tn(a, b):
    return lax.dot_general(a, b, (((0,), (0,)), ((), ())), preferred_element_type=F32)


def split3(x):
    hi = x.astype(BF)
    rest = x - hi.astype(F32)
    mid = rest.astype(BF)
    low = (rest - mid.astype(F32)).astype(BF)
    return hi, mid, low


def in_vmem(count):
    return [pl.BlockSpec(memory_space=pltpu.VMEM) for _ in range(count)]


def in_smem():
    return pl.BlockSpec(memory_space=pltpu.SMEM)


def head_of(h):
    return pl.ds(h * HEAD_DIM, HEAD_DIM)


def pack_grads(grads, outs, sections):
    rows, features = grads.shape
    here = features // sections
    heads = here // HEAD_DIM

    def body(g_ref, o_ref, out_ref):
        lane = lax.broadcasted_iota(jnp.int32, (rows, LANES), 1)
        for s in range(sections):
            extra = jnp.zeros((rows, LANES), F32)
            for h in range(heads):
                at = head_of(s * heads + h)
                terms = g_ref[:, at].astype(F32) * o_ref[:, at].astype(F32)
                delta = jnp.sum(terms, axis=1, keepdims=True)
                for part, value in enumerate(split3(delta)):
                    extra = jnp.where(lane == part * heads + h, value.astype(F32), extra)
            out_ref[s, :, pl.ds(0, here)] = g_ref[:, pl.ds(s * here, here)]
            out_ref[s, :, pl.ds(here, LANES)] = extra.astype(BF)

    return pl.pallas_call(
        body,
        in_specs=in_vmem(2),
        out_specs=in_vmem(1)[0],
        out_shape=jax.ShapeDtypeStruct((sections, rows, here + LANES), BF),
        name="pack_grads",
    )(grads, outs)


def visible_of(start_ref, shape, row_count, key_total):
    key_pos = start_ref[0] + lax.broadcasted_iota(jnp.int32, shape, 0)
    row = lax.broadcasted_iota(jnp.int32, shape, 1) % row_count
    return key_pos <= key_total - row_count + row


def stats_kernel(start, queries, keys, row_count, key_total):
    m, here = queries.shape
    key_count = keys.shape[0]
    heads = here // HEAD_DIM
    slots = -(-heads // 8) * 8
    scaling = HEAD_DIM ** (-0.5)

    def body(start_ref, q_ref, k_ref, out_ref):
        visible = visible_of(start_ref, (key_count, m), row_count, key_total)
        out_ref[...] = jnp.ones_like(out_ref)
        for h in range(heads):
            at = head_of(h)
            s = jnp.where(visible, nt(k_ref[:, at], q_ref[:, at]) * scaling, masked_score)
            top = jnp.max(s, axis=0, keepdims=True)
            total = jnp.sum(jnp.where(visible, jnp.exp(s - top), 0.0), axis=0, keepdims=True)
            out_ref[0, pl.ds(h, 1), :] = top
            out_ref[1, pl.ds(h, 1), :] = total

    return pl.pallas_call(
        body,
        in_specs=[in_smem(), *in_vmem(2)],
        out_specs=in_vmem(1)[0],
        out_shape=jax.ShapeDtypeStruct((2, slots, m), F32),
        name="stats",
    )(start, queries, keys)


def query_kernel(start, queries, grads, keys, values, stats, row_count, key_total):
    m = queries.shape[0]
    key_count, here = keys.shape
    heads = here // HEAD_DIM
    scaling = HEAD_DIM ** (-0.5)

    def body(start_ref, q_ref, g_ref, k_ref, v_ref, l_ref, u_ref, p_ref, ds_ref):
        visible = visible_of(start_ref, (key_count, m), row_count, key_total)
        extra = g_ref[:, pl.ds(here, LANES)]
        slot = lax.broadcasted_iota(jnp.int32, (l_ref.shape[1], LANES), 0)
        lane = lax.broadcasted_iota(jnp.int32, (l_ref.shape[1], LANES), 1)
        pick = (lane % heads == slot) & (lane < 3 * heads)
        delta = nt(jnp.where(pick, 1.0, 0.0).astype(BF), extra)
        log_total = l_ref[0] + jnp.log(l_ref[1])
        for h in range(heads):
            at = head_of(h)
            k = k_ref[:, at]
            s = nt(k, q_ref[:, at]) * scaling
            prob = jnp.where(visible, jnp.exp(s - log_total[h : h + 1, :]), 0.0)
            ds = prob * (nt(v_ref[:, at], g_ref[:, at]) - delta[h : h + 1, :]) * scaling
            ds = ds.astype(BF)
            u_ref[:, at] = tn(ds, k).astype(BF)
            p_ref[h] = prob.astype(BF)
            ds_ref[h] = ds

    return pl.pallas_call(
        body,
        in_specs=[in_smem(), *in_vmem(5)],
        out_specs=in_vmem(3),
        out_shape=[
            jax.ShapeDtypeStruct((m, here), BF),
            jax.ShapeDtypeStruct((heads, key_count, m), BF),
            jax.ShapeDtypeStruct((heads, key_count, m), BF),
        ],
        name="query_gradients",
    )(start, queries, grads, keys, values, stats)


def cache_kernel(queries, grads, probs, score_grads):
    here = queries.shape[1]
    heads, key_count, _ = probs.shape

    def body(q_ref, g_ref, p_ref, ds_ref, dk_ref, dv_ref):
        for h in range(heads):
            at = head_of(h)
            dk_ref[:, at] = nn(ds_ref[h], q_ref[:, at]).astype(BF)
            dv_ref[:, at] = nn(p_ref[h], g_ref[:, at]).astype(BF)

    return pl.pallas_call(
        body,
        in_specs=in_vmem(4),
        out_specs=in_vmem(2),
        out_shape=[jax.ShapeDtypeStruct((key_count, here), BF)] * 2,
        name="cache_gradients",
    )(queries, grads, probs, score_grads)


def merge_stats(stats, axis, count):
    step = count // 2
    while step:
        other = lax.ppermute(stats, axis, [(i, i ^ step) for i in range(count)])
        top = jnp.maximum(stats[0], other[0])
        total = stats[1] * jnp.exp(stats[0] - top) + other[1] * jnp.exp(other[0] - top)
        stats = jnp.stack([top, total])
        step //= 2
    return stats


def flip(value, axis, bit):
    count = lax.axis_size(axis)
    return lax.ppermute(value, axis, [(i, i ^ bit) for i in range(count)])


def ordered(mine, other, upper, axis):
    first = jnp.where(upper, other, mine)
    second = jnp.where(upper, mine, other)
    return jnp.stack([first, second], axis)


def swap_blocks(blocks, axis):
    count = lax.axis_size(axis)
    bits = count.bit_length() - 1
    rest = blocks.shape[1:]
    blocks = blocks.reshape((2,) * bits + rest)
    for i in range(bits):
        upper = (lax.axis_index(axis) >> i) % 2 == 1
        first = lax.index_in_dim(blocks, 0, bits - 1, keepdims=False)
        second = lax.index_in_dim(blocks, 1, bits - 1, keepdims=False)
        mine = jnp.where(upper, second, first)
        other = flip(jnp.where(upper, first, second), axis, 1 << i)
        blocks = ordered(mine, other, upper, 0)
    return blocks.reshape((count,) + rest)


def spread_blocks(blocks, axis):
    count = lax.axis_size(axis)
    bits = count.bit_length() - 1
    lead, rest = blocks.shape[0], blocks.shape[1:]
    for i in range(bits):
        bit = count >> (i + 1)
        upper = lax.axis_index(axis) & bit != 0
        blocks = ordered(blocks, flip(blocks, axis, bit), upper, i + 1)
    return blocks.reshape((lead, count) + rest)


def exchange(blocks):
    return lax.all_to_all(blocks, ("section", "ctx"), 0, 0, tiled=True)


def compute(block_order, queries, cache_keys, cache_values, attention_out, output_grad):
    sections = lax.axis_size("section")
    ctx_count = lax.axis_size("ctx")
    assert ctx_count & (ctx_count - 1) == 0
    assert sections & (sections - 1) == 0
    layers, rows, features = queries.shape
    assert layers == 1
    key_count, here = cache_keys.shape
    row_count = rows * ctx_count
    key_total = key_count * ctx_count
    peers = sections * ctx_count
    start = (block_order[lax.axis_index("ctx")] * key_count).reshape(1)

    sent = queries.reshape(rows, sections, here).transpose(1, 0, 2)[:, None]
    sent = jnp.broadcast_to(sent, (sections, ctx_count, rows, here))
    query_all = exchange(sent.reshape(peers, rows, here)).reshape(-1, here)

    sent = pack_grads(output_grad[0], attention_out[0], sections)
    sent = spread_blocks(swap_blocks(sent, "section"), "ctx")
    grad_all = sent.reshape(peers * rows, -1)

    stats = stats_kernel(start, query_all, cache_keys, row_count, key_total)
    stats = merge_stats(stats, "ctx", ctx_count)
    part, probs, score_grads = query_kernel(
        start, query_all, grad_all, cache_keys, cache_values, stats, row_count, key_total
    )
    part = exchange(part.reshape(peers, rows, here))
    grad_keys, grad_values = cache_kernel(query_all, grad_all, probs, score_grads)
    part = part.reshape(sections, ctx_count, rows, here).astype(F32).sum(axis=1)
    grad_queries = part.transpose(1, 0, 2).reshape(1, rows, features).astype(BF)
    return (grad_queries, grad_keys, grad_values)


def solution(mesh):
    in_specs = (
        P(),
        P("section", "ctx", None),
        P("ctx", "section"),
        P("ctx", "section"),
        P("section", "ctx", None),
        P("section", "ctx", None),
    )
    out_specs = (P("section", "ctx", None), P("ctx", "section"), P("ctx", "section"))
    return jax.shard_map(compute, mesh=mesh, in_specs=in_specs, out_specs=out_specs, check_vma=False)
```

```python
import math

import jax
import jax.numpy as jnp
from jax import lax
from jax.experimental import pallas as pl
from jax.experimental.pallas import tpu as pltpu
from jax.sharding import PartitionSpec as P


HEAD_DIM = 128
LANES = 128
ON_CHIP_BYTES = 1 << 20
masked_score = -1e30
BF = jnp.bfloat16
F32 = jnp.float32


def nt(a, b):
    return lax.dot_general(a, b, (((1,), (1,)), ((), ())), preferred_element_type=F32)


def nn(a, b):
    return lax.dot_general(a, b, (((1,), (0,)), ((), ())), preferred_element_type=F32)


def tn(a, b):
    return lax.dot_general(a, b, (((0,), (0,)), ((), ())), preferred_element_type=F32)


def split3(x):
    hi = x.astype(BF)
    rest = x - hi.astype(F32)
    mid = rest.astype(BF)
    low = (rest - mid.astype(F32)).astype(BF)
    return hi, mid, low


def in_vmem(count):
    return [pl.BlockSpec(memory_space=pltpu.VMEM) for _ in range(count)]


def small(shape, dtype):
    return math.prod(shape) * jnp.dtype(dtype).itemsize <= ON_CHIP_BYTES


def vmem(value):
    if small(value.shape, value.dtype):
        return pltpu.with_memory_space_constraint(value, pltpu.VMEM)
    return value


def held(shape, dtype):
    if small(shape, dtype):
        return pltpu.VMEM(shape, dtype)
    return jax.ShapeDtypeStruct(shape, dtype)


def in_smem():
    return pl.BlockSpec(memory_space=pltpu.SMEM)


def head_of(h):
    return pl.ds(h * HEAD_DIM, HEAD_DIM)


def pack(queries, grads, outs, sections, copies):
    rows, features = queries.shape
    here = features // sections
    heads = here // HEAD_DIM

    def body(q_ref, g_ref, o_ref, sent_ref, out_ref):
        for s in range(sections):
            q = q_ref[:, pl.ds(s * here, here)]

            @pl.loop(0, copies, unroll=copies <= 8)
            def _(c):
                sent_ref[s, c] = q

        lane = lax.broadcasted_iota(jnp.int32, (rows, LANES), 1)
        for s in range(sections):
            extra = jnp.zeros((rows, LANES), F32)
            for h in range(heads):
                at = head_of(s * heads + h)
                terms = g_ref[:, at].astype(F32) * o_ref[:, at].astype(F32)
                delta = jnp.sum(terms, axis=1, keepdims=True)
                for part, value in enumerate(split3(delta)):
                    extra = jnp.where(lane == part * heads + h, value.astype(F32), extra)
            out_ref[s, :, pl.ds(0, here)] = g_ref[:, pl.ds(s * here, here)]
            out_ref[s, :, pl.ds(here, LANES)] = extra.astype(BF)

    return pl.pallas_call(
        body,
        in_specs=in_vmem(3),
        out_specs=in_vmem(2),
        out_shape=[
            jax.ShapeDtypeStruct((sections, copies, rows, here), BF),
            held((sections, rows, here + LANES), BF),
        ],
        name="pack",
    )(queries, grads, outs)


def visible_of(start_ref, shape, row_count, key_total):
    key_pos = start_ref[0] + lax.broadcasted_iota(jnp.int32, shape, 0)
    row = lax.broadcasted_iota(jnp.int32, shape, 1) % row_count
    return key_pos <= key_total - row_count + row


def stats_kernel(start, queries, keys, row_count, key_total):
    m, here = queries.shape
    key_count = keys.shape[0]
    heads = here // HEAD_DIM
    slots = -(-heads // 8) * 8
    scaling = HEAD_DIM ** (-0.5)

    def body(start_ref, q_ref, k_ref, out_ref):
        visible = visible_of(start_ref, (key_count, m), row_count, key_total)
        out_ref[...] = jnp.ones_like(out_ref)
        for h in range(heads):
            at = head_of(h)
            s = jnp.where(visible, nt(k_ref[:, at], q_ref[:, at]) * scaling, masked_score)
            top = jnp.max(s, axis=0, keepdims=True)
            total = jnp.sum(jnp.where(visible, jnp.exp(s - top), 0.0), axis=0, keepdims=True)
            out_ref[0, pl.ds(h, 1), :] = top
            out_ref[1, pl.ds(h, 1), :] = total

    return pl.pallas_call(
        body,
        in_specs=[in_smem(), *in_vmem(2)],
        out_specs=in_vmem(1)[0],
        out_shape=held((2, slots, m), F32),
        name="stats",
    )(start, vmem(queries), vmem(keys))


def query_kernel(start, queries, grads, keys, values, stats, row_count, key_total):
    m = queries.shape[0]
    key_count, here = keys.shape
    heads = here // HEAD_DIM
    scaling = HEAD_DIM ** (-0.5)

    def body(start_ref, q_ref, g_ref, k_ref, v_ref, l_ref, u_ref, p_ref, ds_ref):
        visible = visible_of(start_ref, (key_count, m), row_count, key_total)
        extra = g_ref[:, pl.ds(here, LANES)]
        slot = lax.broadcasted_iota(jnp.int32, (l_ref.shape[1], LANES), 0)
        lane = lax.broadcasted_iota(jnp.int32, (l_ref.shape[1], LANES), 1)
        pick = (lane % heads == slot) & (lane < 3 * heads)
        delta = nt(jnp.where(pick, 1.0, 0.0).astype(BF), extra)
        log_total = l_ref[0] + jnp.log(l_ref[1])
        for h in range(heads):
            at = head_of(h)
            k = k_ref[:, at]
            s = nt(k, q_ref[:, at]) * scaling
            prob = jnp.where(visible, jnp.exp(s - log_total[h : h + 1, :]), 0.0)
            ds = prob * (nt(v_ref[:, at], g_ref[:, at]) - delta[h : h + 1, :]) * scaling
            ds = ds.astype(BF)
            u_ref[:, at] = tn(ds, k).astype(BF)
            p_ref[h] = prob.astype(BF)
            ds_ref[h] = ds

    return pl.pallas_call(
        body,
        in_specs=[in_smem(), *in_vmem(5)],
        out_specs=in_vmem(3),
        out_shape=[
            jax.ShapeDtypeStruct((m, here), BF),
            held((heads, key_count, m), BF),
            held((heads, key_count, m), BF),
        ],
        name="query_gradients",
    )(start, vmem(queries), vmem(grads), vmem(keys), vmem(values), vmem(stats))


def cache_kernel(queries, grads, probs, score_grads):
    here = queries.shape[1]
    heads, key_count, _ = probs.shape

    def body(q_ref, g_ref, p_ref, ds_ref, dk_ref, dv_ref):
        for h in range(heads):
            at = head_of(h)
            dk_ref[:, at] = nn(ds_ref[h], q_ref[:, at]).astype(BF)
            dv_ref[:, at] = nn(p_ref[h], g_ref[:, at]).astype(BF)

    return pl.pallas_call(
        body,
        in_specs=in_vmem(4),
        out_specs=in_vmem(2),
        out_shape=[jax.ShapeDtypeStruct((key_count, here), BF)] * 2,
        name="cache_gradients",
    )(vmem(queries), vmem(grads), vmem(probs), vmem(score_grads))


def merge_stats(stats, axis, count):
    for i in range(count.bit_length() - 1):
        other = flip(stats, axis, count >> (i + 1))
        top = jnp.maximum(stats[0], other[0])
        total = stats[1] * jnp.exp(stats[0] - top) + other[1] * jnp.exp(other[0] - top)
        stats = jnp.stack([top, total])
    return stats


def flip(value, axis, bit):
    count = lax.axis_size(axis)
    return lax.ppermute(value, axis, [(i, i ^ bit) for i in range(count)])


def ordered(mine, other, upper, axis):
    first = jnp.where(upper, other, mine)
    second = jnp.where(upper, mine, other)
    return jnp.stack([first, second], axis)


def swap_blocks(blocks, axis):
    count = lax.axis_size(axis)
    bits = count.bit_length() - 1
    rest = blocks.shape[1:]
    blocks = blocks.reshape((2,) * bits + rest)
    for i in range(bits):
        upper = (lax.axis_index(axis) >> i) % 2 == 1
        first = lax.index_in_dim(blocks, 0, bits - 1, keepdims=False)
        second = lax.index_in_dim(blocks, 1, bits - 1, keepdims=False)
        mine = jnp.where(upper, second, first)
        other = flip(jnp.where(upper, first, second), axis, 1 << i)
        blocks = ordered(mine, other, upper, 0)
    return blocks.reshape((count,) + rest)


def spread_blocks(blocks, axis):
    count = lax.axis_size(axis)
    bits = count.bit_length() - 1
    lead, rest = blocks.shape[0], blocks.shape[1:]
    for i in range(bits):
        bit = count >> (i + 1)
        upper = lax.axis_index(axis) & bit != 0
        other = flip(blocks, axis, bit)
        blocks = ordered(blocks, other, upper, i + 1)
    return blocks.reshape((lead, count) + rest)


def exchange(blocks):
    return lax.all_to_all(blocks, ("section", "ctx"), 0, 0, tiled=True)


def compute(block_order, queries, cache_keys, cache_values, attention_out, output_grad):
    sections = lax.axis_size("section")
    ctx_count = lax.axis_size("ctx")
    assert ctx_count & (ctx_count - 1) == 0
    assert sections & (sections - 1) == 0
    layers, rows, features = queries.shape
    assert layers == 1
    key_count, here = cache_keys.shape
    row_count = rows * ctx_count
    key_total = key_count * ctx_count
    peers = sections * ctx_count
    start = (block_order[lax.axis_index("ctx")] * key_count).reshape(1)

    sent, own = pack(queries[0], output_grad[0], attention_out[0], sections, ctx_count)
    query_all = exchange(sent.reshape(peers, rows, here)).reshape(-1, here)
    own = spread_blocks(swap_blocks(own, "section"), "ctx")
    grad_all = own.reshape(peers * rows, -1)

    stats = stats_kernel(start, query_all, cache_keys, row_count, key_total)
    stats = merge_stats(stats, "ctx", ctx_count)
    part, probs, score_grads = query_kernel(
        start, query_all, grad_all, cache_keys, cache_values, stats, row_count, key_total
    )
    part = exchange(part.reshape(peers, rows, here))
    grad_keys, grad_values = cache_kernel(query_all, grad_all, probs, score_grads)
    part = part.reshape(sections, ctx_count, rows, here).astype(F32).sum(axis=1)
    grad_queries = part.transpose(1, 0, 2).reshape(1, rows, features).astype(BF)
    return (grad_queries, grad_keys, grad_values)


def solution(mesh):
    in_specs = (
        P(),
        P("section", "ctx", None),
        P("ctx", "section"),
        P("ctx", "section"),
        P("section", "ctx", None),
        P("section", "ctx", None),
    )
    out_specs = (P("section", "ctx", None), P("ctx", "section"), P("ctx", "section"))
    return jax.shard_map(compute, mesh=mesh, in_specs=in_specs, out_specs=out_specs, check_vma=False)
```

```python
import math

import jax
import jax.numpy as jnp
from jax import lax
from jax.experimental import pallas as pl
from jax.experimental.pallas import tpu as pltpu
from jax.sharding import PartitionSpec as P


HEAD_DIM = 128
LANES = 128
ON_CHIP_BYTES = 1 << 20
masked_score = -1e30
BF = jnp.bfloat16
F32 = jnp.float32


def nt(a, b):
    return lax.dot_general(a, b, (((1,), (1,)), ((), ())), preferred_element_type=F32)


def nn(a, b):
    return lax.dot_general(a, b, (((1,), (0,)), ((), ())), preferred_element_type=F32)


def tn(a, b):
    return lax.dot_general(a, b, (((0,), (0,)), ((), ())), preferred_element_type=F32)


def split3(x):
    hi = x.astype(BF)
    rest = x - hi.astype(F32)
    mid = rest.astype(BF)
    low = (rest - mid.astype(F32)).astype(BF)
    return hi, mid, low


def in_vmem(count):
    return [pl.BlockSpec(memory_space=pltpu.VMEM) for _ in range(count)]


def small(shape, dtype):
    return math.prod(shape) * jnp.dtype(dtype).itemsize <= ON_CHIP_BYTES


def vmem(value):
    if small(value.shape, value.dtype):
        return pltpu.with_memory_space_constraint(value, pltpu.VMEM)
    return value


def held(shape, dtype):
    if small(shape, dtype):
        return pltpu.VMEM(shape, dtype)
    return jax.ShapeDtypeStruct(shape, dtype)


def in_smem():
    return pl.BlockSpec(memory_space=pltpu.SMEM)


def head_of(h):
    return pl.ds(h * HEAD_DIM, HEAD_DIM)


def pack(grads, outs, sections):
    rows, features = grads.shape
    here = features // sections
    heads = here // HEAD_DIM

    def body(g_ref, o_ref, out_ref):
        lane = lax.broadcasted_iota(jnp.int32, (rows, LANES), 1)
        for s in range(sections):
            extra = jnp.zeros((rows, LANES), F32)
            for h in range(heads):
                at = head_of(s * heads + h)
                terms = g_ref[:, at].astype(F32) * o_ref[:, at].astype(F32)
                delta = jnp.sum(terms, axis=1, keepdims=True)
                for part, value in enumerate(split3(delta)):
                    extra = jnp.where(lane == part * heads + h, value.astype(F32), extra)
            out_ref[s, :, pl.ds(0, here)] = g_ref[:, pl.ds(s * here, here)]
            out_ref[s, :, pl.ds(here, LANES)] = extra.astype(BF)

    return pl.pallas_call(
        body,
        in_specs=in_vmem(2),
        out_specs=in_vmem(1)[0],
        out_shape=held((sections, rows, here + LANES), BF),
        name="pack",
    )(grads, outs)


def visible_of(start_ref, shape, row_count, key_total):
    key_pos = start_ref[0] + lax.broadcasted_iota(jnp.int32, shape, 0)
    row = lax.broadcasted_iota(jnp.int32, shape, 1) % row_count
    return key_pos <= key_total - row_count + row


def stats_kernel(start, queries, keys, values, row_count, key_total):
    m, here = queries.shape
    key_count = keys.shape[0]
    heads = here // HEAD_DIM
    slots = -(-heads // 8) * 8
    scaling = HEAD_DIM ** (-0.5)

    def body(start_ref, q_ref, k_ref, _, out_ref):
        visible = visible_of(start_ref, (key_count, m), row_count, key_total)
        out_ref[...] = jnp.ones_like(out_ref)
        for h in range(heads):
            at = head_of(h)
            s = jnp.where(visible, nt(k_ref[:, at], q_ref[:, at]) * scaling, masked_score)
            top = jnp.max(s, axis=0, keepdims=True)
            total = jnp.sum(jnp.where(visible, jnp.exp(s - top), 0.0), axis=0, keepdims=True)
            out_ref[0, pl.ds(h, 1), :] = top
            out_ref[1, pl.ds(h, 1), :] = total

    return pl.pallas_call(
        body,
        in_specs=[in_smem(), *in_vmem(3)],
        out_specs=in_vmem(1)[0],
        out_shape=held((2, slots, m), F32),
        name="stats",
    )(start, vmem(queries), vmem(keys), vmem(values))


def query_kernel(start, queries, grads, keys, values, stats, row_count, key_total):
    m = queries.shape[0]
    key_count, here = keys.shape
    heads = here // HEAD_DIM
    slots = stats.shape[1]
    scaling = HEAD_DIM ** (-0.5)

    def body(start_ref, q_ref, g_ref, k_ref, v_ref, l_ref, u_ref, p_ref, ds_ref):
        visible = visible_of(start_ref, (key_count, m), row_count, key_total)
        extra = g_ref[:, pl.ds(here, LANES)]
        slot = lax.broadcasted_iota(jnp.int32, (slots, LANES), 0)
        lane = lax.broadcasted_iota(jnp.int32, (slots, LANES), 1)
        pick = (lane % heads == slot) & (lane < 3 * heads)
        delta = nt(jnp.where(pick, 1.0, 0.0).astype(BF), extra)
        tops = l_ref[0]
        for h in range(heads):
            at = head_of(h)
            k = k_ref[:, at]
            s = nt(k, q_ref[:, at]) * scaling
            prob = jnp.where(visible, jnp.exp(s - tops[h : h + 1, :]), 0.0)
            ds = prob * (nt(v_ref[:, at], g_ref[:, at]) - delta[h : h + 1, :]) * scaling
            ds = ds.astype(BF)
            u_ref[:, at] = tn(ds, k).astype(BF)
            p_ref[h] = prob.astype(BF)
            ds_ref[h] = ds
        sent = jnp.zeros((m, LANES), F32)
        for i in range(2):
            for part, value in enumerate(split3(l_ref[i])):
                at = (3 * i + part) * heads
                place = (lane == at + slot) & (slot < heads)
                sent += tn(value, jnp.where(place, 1.0, 0.0).astype(BF))
        u_ref[:, pl.ds(here, LANES)] = sent.astype(BF)

    return pl.pallas_call(
        body,
        in_specs=[in_smem(), *in_vmem(5)],
        out_specs=in_vmem(3),
        out_shape=[
            jax.ShapeDtypeStruct((m, here + LANES), BF),
            held((heads, key_count, m), BF),
            held((heads, key_count, m), BF),
        ],
        name="query_gradients",
    )(start, vmem(queries), vmem(grads), vmem(keys), vmem(values), vmem(stats))


def cache_kernel(queries, grads, probs, score_grads, own, merged):
    here = queries.shape[1]
    heads, key_count, _ = probs.shape

    def body(q_ref, g_ref, p_ref, ds_ref, own_ref, all_ref, dk_ref, dv_ref):
        share = jnp.exp(own_ref[0] - all_ref[0]) / all_ref[1]
        for h in range(heads):
            at = head_of(h)
            row = share[h : h + 1, :]
            ds = (ds_ref[h].astype(F32) * row).astype(BF)
            prob = (p_ref[h].astype(F32) * row).astype(BF)
            dk_ref[:, at] = nn(ds, q_ref[:, at]).astype(BF)
            dv_ref[:, at] = nn(prob, g_ref[:, at]).astype(BF)

    return pl.pallas_call(
        body,
        in_specs=in_vmem(6),
        out_specs=in_vmem(2),
        out_shape=[jax.ShapeDtypeStruct((key_count, here), BF)] * 2,
        name="cache_gradients",
    )(vmem(queries), vmem(grads), vmem(probs), vmem(score_grads), vmem(own), vmem(merged))


def combine_kernel(parts):
    sections, holders, rows, width = parts.shape
    here = width - LANES
    heads = here // HEAD_DIM

    def body(p_ref, out_ref):
        def stats_of(s, c):
            e = p_ref[s, c, :, pl.ds(here, LANES)].astype(F32)
            e += pltpu.roll(e, LANES - heads, 1) + pltpu.roll(e, LANES - 2 * heads, 1)
            return e, pltpu.roll(e, LANES - 3 * heads, 1)

        for s in range(sections):
            top = jnp.full((rows, LANES), -jnp.inf, F32)
            for c in range(holders):
                top = jnp.maximum(top, stats_of(s, c)[0])
            total = jnp.zeros((rows, LANES), F32)
            for c in range(holders):
                own, count = stats_of(s, c)
                total += jnp.exp(own - top) * count
            sums = [jnp.zeros((rows, HEAD_DIM), F32) for _ in range(heads)]
            for c in range(holders):
                share = jnp.exp(stats_of(s, c)[0] - top) / total
                for h in range(heads):
                    value = p_ref[s, c, :, head_of(h)].astype(F32)
                    sums[h] += share[:, h : h + 1] * value
            for h in range(heads):
                out_ref[:, head_of(s * heads + h)] = sums[h].astype(BF)

    return pl.pallas_call(
        body,
        in_specs=in_vmem(1),
        out_specs=in_vmem(1)[0],
        out_shape=jax.ShapeDtypeStruct((rows, sections * here), BF),
        name="combine",
    )(vmem(parts))


def merge_stats(stats, axis, count):
    for i in range(count.bit_length() - 1):
        other = flip(stats, axis, count >> (i + 1))
        top = jnp.maximum(stats[0], other[0])
        total = stats[1] * jnp.exp(stats[0] - top) + other[1] * jnp.exp(other[0] - top)
        stats = jnp.stack([top, total])
    return stats


def flip(value, axis, bit):
    count = lax.axis_size(axis)
    return lax.ppermute(value, axis, [(i, i ^ bit) for i in range(count)])


def ordered(mine, other, upper, axis):
    first = jnp.where(upper, other, mine)
    second = jnp.where(upper, mine, other)
    return jnp.stack([first, second], axis)


def swap_blocks(blocks, axis):
    count = lax.axis_size(axis)
    bits = count.bit_length() - 1
    rest = blocks.shape[1:]
    blocks = blocks.reshape((2,) * bits + rest)
    for i in range(bits):
        upper = (lax.axis_index(axis) >> i) % 2 == 1
        first = lax.index_in_dim(blocks, 0, bits - 1, keepdims=False)
        second = lax.index_in_dim(blocks, 1, bits - 1, keepdims=False)
        mine = jnp.where(upper, second, first)
        other = jnp.where(upper, first, second)
        other = flip(other, axis, 1 << i)
        blocks = ordered(mine, other, upper, 0)
    return blocks.reshape((count,) + rest)


def spread_blocks(blocks, axis, order):
    count = lax.axis_size(axis)
    lead, rest = blocks.shape[0], blocks.shape[1:]
    done = []
    for bit in order:
        upper = lax.axis_index(axis) & (1 << bit) != 0
        other = flip(blocks, axis, 1 << bit)
        blocks = ordered(blocks, other, upper, 1 + sum(b > bit for b in done))
        done.append(bit)
    return blocks.reshape((lead, count) + rest)


def exchange(blocks):
    return lax.all_to_all(blocks, ("section", "ctx"), 0, 0, tiled=True)


def compute(block_order, queries, cache_keys, cache_values, attention_out, output_grad):
    sections = lax.axis_size("section")
    ctx_count = lax.axis_size("ctx")
    assert ctx_count & (ctx_count - 1) == 0
    assert sections & (sections - 1) == 0
    layers, rows, _ = queries.shape
    assert layers == 1
    key_count, here = cache_keys.shape
    row_count = rows * ctx_count
    key_total = key_count * ctx_count
    peers = sections * ctx_count
    start = (block_order[lax.axis_index("ctx")] * key_count).reshape(1)

    ctx_bits = ctx_count.bit_length() - 1
    down = list(range(ctx_bits))[::-1]

    sent = queries.reshape(rows, sections, here).transpose(1, 0, 2)
    sent = swap_blocks(sent, "section")
    query_all = spread_blocks(sent, "ctx", down)
    query_all = query_all.reshape(peers * rows, here)
    sent = pack(output_grad[0], attention_out[0], sections)
    sent = swap_blocks(sent, "section")
    grad_all = spread_blocks(sent, "ctx", down[:1] + down[1:][::-1])
    grad_all = grad_all.reshape(peers * rows, here + LANES)

    own = stats_kernel(start, query_all, cache_keys, cache_values, row_count, key_total)
    merged = merge_stats(own, "ctx", ctx_count)
    part, probs, score_grads = query_kernel(
        start, query_all, grad_all, cache_keys, cache_values, own, row_count, key_total
    )
    part = exchange(part.reshape(peers, rows, here + LANES))
    grad_keys, grad_values = cache_kernel(query_all, grad_all, probs, score_grads, own, merged)
    grad_queries = combine_kernel(part.reshape(sections, ctx_count, rows, here + LANES))
    return (grad_queries[None], grad_keys, grad_values)


def solution(mesh):
    in_specs = (
        P(),
        P("section", "ctx", None),
        P("ctx", "section"),
        P("ctx", "section"),
        P("section", "ctx", None),
        P("section", "ctx", None),
    )
    out_specs = (P("section", "ctx", None), P("ctx", "section"), P("ctx", "section"))
    return jax.shard_map(compute, mesh=mesh, in_specs=in_specs, out_specs=out_specs, check_vma=False)
```

```python
import math

import jax
import jax.numpy as jnp
from jax import lax
from jax.experimental import pallas as pl
from jax.experimental.pallas import tpu as pltpu
from jax.sharding import PartitionSpec as P


HEAD_DIM = 128
LANES = 128
ON_CHIP_BYTES = 1 << 20
masked_score = -1e30
BF = jnp.bfloat16
F32 = jnp.float32


def nt(a, b):
    return lax.dot_general(a, b, (((1,), (1,)), ((), ())), preferred_element_type=F32)


def nn(a, b):
    return lax.dot_general(a, b, (((1,), (0,)), ((), ())), preferred_element_type=F32)


def tn(a, b):
    return lax.dot_general(a, b, (((0,), (0,)), ((), ())), preferred_element_type=F32)


def split3(x):
    hi = x.astype(BF)
    rest = x - hi.astype(F32)
    mid = rest.astype(BF)
    low = (rest - mid.astype(F32)).astype(BF)
    return hi, mid, low


def in_vmem(count):
    return [pl.BlockSpec(memory_space=pltpu.VMEM) for _ in range(count)]


def small(shape, dtype):
    return math.prod(shape) * jnp.dtype(dtype).itemsize <= ON_CHIP_BYTES


def vmem(value):
    if small(value.shape, value.dtype):
        return pltpu.with_memory_space_constraint(value, pltpu.VMEM)
    return value


def held(shape, dtype):
    if small(shape, dtype):
        return pltpu.VMEM(shape, dtype)
    return jax.ShapeDtypeStruct(shape, dtype)


def in_smem():
    return pl.BlockSpec(memory_space=pltpu.SMEM)


def head_of(h):
    return pl.ds(h * HEAD_DIM, HEAD_DIM)


def pack(block_order, keys, values, grads, outs, sections):
    rows, features = grads.shape
    here = features // sections
    heads = here // HEAD_DIM
    key_count = keys.shape[0]

    def body(order_ref, k_hbm, v_hbm, g_ref, o_ref, out_ref, start_ref, k_ref, v_ref, sems):
        copies = [
            pltpu.make_async_copy(k_hbm, k_ref, sems.at[0]),
            pltpu.make_async_copy(v_hbm, v_ref, sems.at[1]),
        ]
        for copy in copies:
            copy.start()
        block = order_ref[lax.axis_index("ctx")]
        start_ref[...] = jnp.full(start_ref.shape, block * key_count, jnp.int32)
        lane = lax.broadcasted_iota(jnp.int32, (rows, LANES), 1)
        for s in range(sections):
            extra = jnp.zeros((rows, LANES), F32)
            for h in range(heads):
                at = head_of(s * heads + h)
                terms = g_ref[:, at].astype(F32) * o_ref[:, at].astype(F32)
                delta = jnp.sum(terms, axis=1, keepdims=True)
                for part, value in enumerate(split3(delta)):
                    extra = jnp.where(lane == part * heads + h, value.astype(F32), extra)
            out_ref[s, :, pl.ds(0, here)] = g_ref[:, pl.ds(s * here, here)]
            out_ref[s, :, pl.ds(here, LANES)] = extra.astype(BF)
        for copy in copies:
            copy.wait()

    return pl.pallas_call(
        body,
        in_specs=[in_smem(), *[pl.BlockSpec(memory_space=pl.ANY)] * 2, *in_vmem(2)],
        out_specs=in_vmem(4),
        out_shape=[
            held((sections, rows, here + LANES), BF),
            held((8, LANES), jnp.int32),
            held(keys.shape, BF),
            held(values.shape, BF),
        ],
        scratch_shapes=[pltpu.SemaphoreType.DMA((2,))],
        name="pack",
    )(block_order, keys, values, grads, outs)


def visible_of(start_ref, shape, row_count, key_total):
    key_pos = start_ref[0:1, 0:1] + lax.broadcasted_iota(jnp.int32, shape, 0)
    row = lax.broadcasted_iota(jnp.int32, shape, 1) % row_count
    return key_pos <= key_total - row_count + row


def stats_kernel(start, queries, keys, row_count, key_total):
    m, here = queries.shape
    key_count = keys.shape[0]
    heads = here // HEAD_DIM
    slots = -(-heads // 8) * 8
    scaling = HEAD_DIM ** (-0.5)

    def body(start_ref, q_ref, k_ref, out_ref):
        visible = visible_of(start_ref, (key_count, m), row_count, key_total)
        out_ref[...] = jnp.ones_like(out_ref)
        for h in range(heads):
            at = head_of(h)
            s = jnp.where(visible, nt(k_ref[:, at], q_ref[:, at]) * scaling, masked_score)
            top = jnp.max(s, axis=0, keepdims=True)
            total = jnp.sum(jnp.where(visible, jnp.exp(s - top), 0.0), axis=0, keepdims=True)
            out_ref[0, pl.ds(h, 1), :] = top
            out_ref[1, pl.ds(h, 1), :] = total

    return pl.pallas_call(
        body,
        in_specs=in_vmem(3),
        out_specs=in_vmem(1)[0],
        out_shape=held((2, slots, m), F32),
        name="stats",
    )(vmem(start), vmem(queries), vmem(keys))


def query_kernel(start, queries, grads, keys, values, stats, row_count, key_total):
    m = queries.shape[0]
    key_count, here = keys.shape
    heads = here // HEAD_DIM
    slots = stats.shape[1]
    scaling = HEAD_DIM ** (-0.5)

    def body(start_ref, q_ref, g_ref, k_ref, v_ref, l_ref, u_ref, p_ref, ds_ref):
        visible = visible_of(start_ref, (key_count, m), row_count, key_total)
        extra = g_ref[:, pl.ds(here, LANES)]
        slot = lax.broadcasted_iota(jnp.int32, (slots, LANES), 0)
        lane = lax.broadcasted_iota(jnp.int32, (slots, LANES), 1)
        pick = (lane % heads == slot) & (lane < 3 * heads)
        delta = nt(jnp.where(pick, 1.0, 0.0).astype(BF), extra)
        tops = l_ref[0]
        for h in range(heads):
            at = head_of(h)
            k = k_ref[:, at]
            s = nt(k, q_ref[:, at]) * scaling
            prob = jnp.where(visible, jnp.exp(s - tops[h : h + 1, :]), 0.0)
            ds = prob * (nt(v_ref[:, at], g_ref[:, at]) - delta[h : h + 1, :]) * scaling
            ds = ds.astype(BF)
            u_ref[:, at] = tn(ds, k).astype(BF)
            p_ref[h] = prob.astype(BF)
            ds_ref[h] = ds
        sent = jnp.zeros((m, LANES), F32)
        for i in range(2):
            for part, value in enumerate(split3(l_ref[i])):
                at = (3 * i + part) * heads
                place = (lane == at + slot) & (slot < heads)
                sent += tn(value, jnp.where(place, 1.0, 0.0).astype(BF))
        u_ref[:, pl.ds(here, LANES)] = sent.astype(BF)

    return pl.pallas_call(
        body,
        in_specs=in_vmem(6),
        out_specs=in_vmem(3),
        out_shape=[
            jax.ShapeDtypeStruct((m, here + LANES), BF),
            held((heads, key_count, m), BF),
            held((heads, key_count, m), BF),
        ],
        name="query_gradients",
    )(vmem(start), vmem(queries), vmem(grads), vmem(keys), vmem(values), vmem(stats))


def cache_kernel(queries, grads, probs, score_grads, own, merged):
    here = queries.shape[1]
    heads, key_count, _ = probs.shape

    def body(q_ref, g_ref, p_ref, ds_ref, own_ref, all_ref, dk_ref, dv_ref):
        share = jnp.exp(own_ref[0] - all_ref[0]) / all_ref[1]
        for h in range(heads):
            at = head_of(h)
            row = share[h : h + 1, :]
            ds = (ds_ref[h].astype(F32) * row).astype(BF)
            prob = (p_ref[h].astype(F32) * row).astype(BF)
            dk_ref[:, at] = nn(ds, q_ref[:, at]).astype(BF)
            dv_ref[:, at] = nn(prob, g_ref[:, at]).astype(BF)

    return pl.pallas_call(
        body,
        in_specs=in_vmem(6),
        out_specs=in_vmem(2),
        out_shape=[jax.ShapeDtypeStruct((key_count, here), BF)] * 2,
        name="cache_gradients",
    )(vmem(queries), vmem(grads), vmem(probs), vmem(score_grads), vmem(own), vmem(merged))


def combine_kernel(parts):
    sections, holders, rows, width = parts.shape
    here = width - LANES
    heads = here // HEAD_DIM

    def body(p_ref, out_ref):
        def stats_of(s, c):
            e = p_ref[s, c, :, pl.ds(here, LANES)].astype(F32)
            e += pltpu.roll(e, LANES - heads, 1) + pltpu.roll(e, LANES - 2 * heads, 1)
            return e, pltpu.roll(e, LANES - 3 * heads, 1)

        for s in range(sections):
            top = jnp.full((rows, LANES), -jnp.inf, F32)
            for c in range(holders):
                top = jnp.maximum(top, stats_of(s, c)[0])
            total = jnp.zeros((rows, LANES), F32)
            for c in range(holders):
                own, count = stats_of(s, c)
                total += jnp.exp(own - top) * count
            sums = [jnp.zeros((rows, HEAD_DIM), F32) for _ in range(heads)]
            for c in range(holders):
                share = jnp.exp(stats_of(s, c)[0] - top) / total
                for h in range(heads):
                    value = p_ref[s, c, :, head_of(h)].astype(F32)
                    sums[h] += share[:, h : h + 1] * value
            for h in range(heads):
                out_ref[:, head_of(s * heads + h)] = sums[h].astype(BF)

    return pl.pallas_call(
        body,
        in_specs=in_vmem(1),
        out_specs=in_vmem(1)[0],
        out_shape=jax.ShapeDtypeStruct((rows, sections * here), BF),
        name="combine",
    )(vmem(parts))


def merge_stats(stats, axis, count):
    for i in range(count.bit_length() - 1):
        other = flip(stats, axis, count >> (i + 1))
        top = jnp.maximum(stats[0], other[0])
        total = stats[1] * jnp.exp(stats[0] - top) + other[1] * jnp.exp(other[0] - top)
        stats = jnp.stack([top, total])
    return stats


def flip(value, axis, bit):
    count = lax.axis_size(axis)
    return lax.ppermute(value, axis, [(i, i ^ bit) for i in range(count)])


def ordered(mine, other, upper, axis):
    first = jnp.where(upper, other, mine)
    second = jnp.where(upper, mine, other)
    return jnp.stack([first, second], axis)


def swap_blocks(blocks, axis):
    count = lax.axis_size(axis)
    bits = count.bit_length() - 1
    rest = blocks.shape[1:]
    blocks = blocks.reshape((2,) * bits + rest)
    for i in range(bits):
        upper = (lax.axis_index(axis) >> i) % 2 == 1
        first = lax.index_in_dim(blocks, 0, bits - 1, keepdims=False)
        second = lax.index_in_dim(blocks, 1, bits - 1, keepdims=False)
        mine = jnp.where(upper, second, first)
        other = jnp.where(upper, first, second)
        other = flip(other, axis, 1 << i)
        blocks = ordered(mine, other, upper, 0)
    return blocks.reshape((count,) + rest)


def spread_blocks(blocks, axis, order):
    count = lax.axis_size(axis)
    lead, rest = blocks.shape[0], blocks.shape[1:]
    done = []
    for bit in order:
        upper = lax.axis_index(axis) & (1 << bit) != 0
        other = flip(blocks, axis, 1 << bit)
        blocks = ordered(blocks, other, upper, 1 + sum(b > bit for b in done))
        done.append(bit)
    return blocks.reshape((lead, count) + rest)


def exchange(blocks):
    return lax.all_to_all(blocks, ("section", "ctx"), 0, 0, tiled=True)


def compute(block_order, queries, cache_keys, cache_values, attention_out, output_grad):
    sections = lax.axis_size("section")
    ctx_count = lax.axis_size("ctx")
    assert ctx_count & (ctx_count - 1) == 0
    assert sections & (sections - 1) == 0
    layers, rows, _ = queries.shape
    assert layers == 1
    key_count, here = cache_keys.shape
    row_count = rows * ctx_count
    key_total = key_count * ctx_count
    peers = sections * ctx_count

    ctx_bits = ctx_count.bit_length() - 1
    down = list(range(ctx_bits))[::-1]

    sent = queries.reshape(rows, sections, here).transpose(1, 0, 2)
    sent = swap_blocks(sent, "section")
    query_all = spread_blocks(sent, "ctx", down)
    query_all = query_all.reshape(peers * rows, here)
    sent, start, keys, values = pack(
        block_order, cache_keys, cache_values, output_grad[0], attention_out[0], sections
    )
    sent = swap_blocks(sent, "section")
    grad_all = spread_blocks(sent, "ctx", down[:1] + down[1:][::-1])
    grad_all = grad_all.reshape(peers * rows, here + LANES)

    own = stats_kernel(start, query_all, keys, row_count, key_total)
    merged = merge_stats(own, "ctx", ctx_count)
    part, probs, score_grads = query_kernel(
        start, query_all, grad_all, keys, values, own, row_count, key_total
    )
    part = exchange(part.reshape(peers, rows, here + LANES))
    grad_keys, grad_values = cache_kernel(query_all, grad_all, probs, score_grads, own, merged)
    grad_queries = combine_kernel(part.reshape(sections, ctx_count, rows, here + LANES))
    return (grad_queries[None], grad_keys, grad_values)


def solution(mesh):
    in_specs = (
        P(),
        P("section", "ctx", None),
        P("ctx", "section"),
        P("ctx", "section"),
        P("section", "ctx", None),
        P("section", "ctx", None),
    )
    out_specs = (P("section", "ctx", None), P("ctx", "section"), P("ctx", "section"))
    return jax.shard_map(compute, mesh=mesh, in_specs=in_specs, out_specs=out_specs, check_vma=False)
```

```python
import math

import jax
import jax.numpy as jnp
from jax import lax
from jax.experimental import pallas as pl
from jax.experimental.pallas import tpu as pltpu
from jax.sharding import PartitionSpec as P


HEAD_DIM = 128
LANES = 128
ON_CHIP_BYTES = 1 << 20
masked_score = -1e30
BF = jnp.bfloat16
F32 = jnp.float32


def nt(a, b):
    return lax.dot_general(a, b, (((1,), (1,)), ((), ())), preferred_element_type=F32)


def nn(a, b):
    return lax.dot_general(a, b, (((1,), (0,)), ((), ())), preferred_element_type=F32)


def tn(a, b):
    return lax.dot_general(a, b, (((0,), (0,)), ((), ())), preferred_element_type=F32)


def split3(x):
    hi = x.astype(BF)
    rest = x - hi.astype(F32)
    mid = rest.astype(BF)
    low = (rest - mid.astype(F32)).astype(BF)
    return hi, mid, low


def in_vmem(count):
    return [pl.BlockSpec(memory_space=pltpu.VMEM) for _ in range(count)]


def small(shape, dtype):
    return math.prod(shape) * jnp.dtype(dtype).itemsize <= ON_CHIP_BYTES


def vmem(value):
    if small(value.shape, value.dtype):
        return pltpu.with_memory_space_constraint(value, pltpu.VMEM)
    return value


def held(shape, dtype):
    if small(shape, dtype):
        return pltpu.VMEM(shape, dtype)
    return jax.ShapeDtypeStruct(shape, dtype)


def head_of(h):
    return pl.ds(h * HEAD_DIM, HEAD_DIM)


def pack(block_order, keys, values, queries, grads, outs, sections):
    rows, features = grads.shape
    here = features // sections
    heads = here // HEAD_DIM
    key_count = keys.shape[0]
    half = sections // 2

    def body(order_hbm, k_hbm, v_hbm, q_hbm, g_hbm, o_hbm, *refs):
        q_mine, q_other, g_mine, g_other, start_ref, k_ref, v_ref = refs[:7]
        q_ref, g_ref, o_ref, order_ref, sems = refs[7:]
        pairs = [
            (q_hbm, q_ref),
            (g_hbm, g_ref),
            (o_hbm, o_ref),
            (order_hbm, order_ref),
            (k_hbm, k_ref),
            (v_hbm, v_ref),
        ]
        copies = [pltpu.make_async_copy(*pair, sems.at[i]) for i, pair in enumerate(pairs)]
        for copy in copies:
            copy.start()
        odd = lax.axis_index("section") % 2
        lane = lax.broadcasted_iota(jnp.int32, (rows, LANES), 1)

        def at(s, h, count=1):
            return pl.ds(pl.multiple_of(s * here + h * HEAD_DIM, HEAD_DIM), count * HEAD_DIM)

        copies[0].wait()
        for q_out, bit in ((q_mine, odd), (q_other, 1 - odd)):
            for j in range(half):
                q_out[j] = q_ref[:, at(2 * j + bit, 0, heads)]
        copies[1].wait()
        copies[2].wait()
        for g_out, bit in ((g_mine, odd), (g_other, 1 - odd)):
            for j in range(half):
                extra = jnp.zeros((rows, LANES), F32)
                for h in range(heads):
                    g = g_ref[:, at(2 * j + bit, h)]
                    terms = g.astype(F32) * o_ref[:, at(2 * j + bit, h)].astype(F32)
                    delta = jnp.sum(terms, axis=1, keepdims=True)
                    for part, value in enumerate(split3(delta)):
                        extra = jnp.where(lane == part * heads + h, value.astype(F32), extra)
                    g_out[j, :, head_of(h)] = g
                g_out[j, :, pl.ds(here, LANES)] = extra.astype(BF)
        copies[3].wait()
        block = order_ref[lax.axis_index("ctx")]
        start_ref[...] = jnp.full(start_ref.shape, block * key_count, jnp.int32)
        copies[4].wait()
        copies[5].wait()

    query_half = held((half, rows, here), BF)
    grad_half = held((half, rows, here + LANES), BF)
    return pl.pallas_call(
        body,
        in_specs=[pl.BlockSpec(memory_space=pl.ANY)] * 6,
        out_specs=in_vmem(7),
        out_shape=[
            query_half,
            query_half,
            grad_half,
            grad_half,
            held((8, LANES), jnp.int32),
            held(keys.shape, BF),
            held(values.shape, BF),
        ],
        scratch_shapes=[
            pltpu.VMEM((rows, features), BF),
            pltpu.VMEM((rows, features), BF),
            pltpu.VMEM((rows, features), BF),
            pltpu.SMEM(block_order.shape, jnp.int32),
            pltpu.SemaphoreType.DMA((6,)),
        ],
        name="pack",
    )(block_order, keys, values, queries, grads, outs)


def visible_of(start_ref, shape, row_count, key_total):
    key_pos = start_ref[0:1, 0:1] + lax.broadcasted_iota(jnp.int32, shape, 0)
    row = lax.broadcasted_iota(jnp.int32, shape, 1) % row_count
    return key_pos <= key_total - row_count + row


def stats_kernel(start, queries, keys, row_count, key_total):
    m, here = queries.shape
    key_count = keys.shape[0]
    heads = here // HEAD_DIM
    slots = -(-heads // 8) * 8
    scaling = HEAD_DIM ** (-0.5)

    def body(start_ref, q_ref, k_ref, out_ref):
        visible = visible_of(start_ref, (key_count, m), row_count, key_total)
        out_ref[...] = jnp.ones_like(out_ref)
        for h in range(heads):
            at = head_of(h)
            s = jnp.where(visible, nt(k_ref[:, at], q_ref[:, at]) * scaling, masked_score)
            top = jnp.max(s, axis=0, keepdims=True)
            total = jnp.sum(jnp.where(visible, jnp.exp(s - top), 0.0), axis=0, keepdims=True)
            out_ref[0, pl.ds(h, 1), :] = top
            out_ref[1, pl.ds(h, 1), :] = total

    return pl.pallas_call(
        body,
        in_specs=in_vmem(3),
        out_specs=in_vmem(1)[0],
        out_shape=held((2, slots, m), F32),
        name="stats",
    )(vmem(start), vmem(queries), vmem(keys))


def query_kernel(start, queries, grads, keys, values, stats, row_count, key_total):
    m = queries.shape[0]
    key_count, here = keys.shape
    heads = here // HEAD_DIM
    slots = stats.shape[1]
    scaling = HEAD_DIM ** (-0.5)

    def body(start_ref, q_ref, g_ref, k_ref, v_ref, l_ref, u_ref, p_ref, ds_ref):
        visible = visible_of(start_ref, (key_count, m), row_count, key_total)
        extra = g_ref[:, pl.ds(here, LANES)]
        slot = lax.broadcasted_iota(jnp.int32, (slots, LANES), 0)
        lane = lax.broadcasted_iota(jnp.int32, (slots, LANES), 1)
        pick = (lane % heads == slot) & (lane < 3 * heads)
        delta = nt(jnp.where(pick, 1.0, 0.0).astype(BF), extra)
        tops = l_ref[0]
        for h in range(heads):
            at = head_of(h)
            k = k_ref[:, at]
            s = nt(k, q_ref[:, at]) * scaling
            prob = jnp.where(visible, jnp.exp(s - tops[h : h + 1, :]), 0.0)
            ds = prob * (nt(v_ref[:, at], g_ref[:, at]) - delta[h : h + 1, :]) * scaling
            ds = ds.astype(BF)
            u_ref[:, at] = tn(ds, k).astype(BF)
            p_ref[h] = prob.astype(BF)
            ds_ref[h] = ds
        sent = jnp.zeros((m, LANES), F32)
        for i in range(2):
            for part, value in enumerate(split3(l_ref[i])):
                at = (3 * i + part) * heads
                place = (lane == at + slot) & (slot < heads)
                sent += tn(value, jnp.where(place, 1.0, 0.0).astype(BF))
        u_ref[:, pl.ds(here, LANES)] = sent.astype(BF)

    return pl.pallas_call(
        body,
        in_specs=in_vmem(6),
        out_specs=in_vmem(3),
        out_shape=[
            jax.ShapeDtypeStruct((m, here + LANES), BF),
            held((heads, key_count, m), BF),
            held((heads, key_count, m), BF),
        ],
        name="query_gradients",
    )(vmem(start), vmem(queries), vmem(grads), vmem(keys), vmem(values), vmem(stats))


def cache_kernel(queries, grads, probs, score_grads, own, merged):
    here = queries.shape[1]
    heads, key_count, _ = probs.shape

    def body(q_ref, g_ref, p_ref, ds_ref, own_ref, all_ref, dk_ref, dv_ref):
        share = jnp.exp(own_ref[0] - all_ref[0]) / all_ref[1]
        for h in range(heads):
            at = head_of(h)
            row = share[h : h + 1, :]
            ds = (ds_ref[h].astype(F32) * row).astype(BF)
            prob = (p_ref[h].astype(F32) * row).astype(BF)
            dk_ref[:, at] = nn(ds, q_ref[:, at]).astype(BF)
            dv_ref[:, at] = nn(prob, g_ref[:, at]).astype(BF)

    return pl.pallas_call(
        body,
        in_specs=in_vmem(6),
        out_specs=in_vmem(2),
        out_shape=[jax.ShapeDtypeStruct((key_count, here), BF)] * 2,
        name="cache_gradients",
    )(vmem(queries), vmem(grads), vmem(probs), vmem(score_grads), vmem(own), vmem(merged))


def combine_kernel(parts):
    sections, holders, rows, width = parts.shape
    here = width - LANES
    heads = here // HEAD_DIM

    def body(p_ref, out_ref):
        def stats_of(s, c):
            e = p_ref[s, c, :, pl.ds(here, LANES)].astype(F32)
            e += pltpu.roll(e, LANES - heads, 1) + pltpu.roll(e, LANES - 2 * heads, 1)
            return e, pltpu.roll(e, LANES - 3 * heads, 1)

        for s in range(sections):
            top = jnp.full((rows, LANES), -jnp.inf, F32)
            for c in range(holders):
                top = jnp.maximum(top, stats_of(s, c)[0])
            total = jnp.zeros((rows, LANES), F32)
            for c in range(holders):
                own, count = stats_of(s, c)
                total += jnp.exp(own - top) * count
            sums = [jnp.zeros((rows, HEAD_DIM), F32) for _ in range(heads)]
            for c in range(holders):
                share = jnp.exp(stats_of(s, c)[0] - top) / total
                for h in range(heads):
                    value = p_ref[s, c, :, head_of(h)].astype(F32)
                    sums[h] += share[:, h : h + 1] * value
            for h in range(heads):
                out_ref[:, head_of(s * heads + h)] = sums[h].astype(BF)

    return pl.pallas_call(
        body,
        in_specs=in_vmem(1),
        out_specs=in_vmem(1)[0],
        out_shape=jax.ShapeDtypeStruct((rows, sections * here), BF),
        name="combine",
    )(vmem(parts))


def merge_stats(stats, axis, order):
    for bit in order:
        other = flip(stats, axis, 1 << bit)
        top = jnp.maximum(stats[0], other[0])
        total = stats[1] * jnp.exp(stats[0] - top) + other[1] * jnp.exp(other[0] - top)
        stats = jnp.stack([top, total])
    return stats


def flip(value, axis, bit):
    count = lax.axis_size(axis)
    return lax.ppermute(value, axis, [(i, i ^ bit) for i in range(count)])


def ordered(mine, other, upper, axis):
    first = jnp.where(upper, other, mine)
    second = jnp.where(upper, mine, other)
    return jnp.stack([first, second], axis)


def swap_blocks(mine, other, axis):
    count = lax.axis_size(axis)
    bits = count.bit_length() - 1
    rest = mine.shape[1:]
    mine = mine.reshape((2,) * (bits - 1) + rest)
    other = other.reshape(mine.shape)
    for i in range(bits):
        upper = (lax.axis_index(axis) >> i) % 2 == 1
        if i:
            first = lax.index_in_dim(blocks, 0, bits - 1, keepdims=False)
            second = lax.index_in_dim(blocks, 1, bits - 1, keepdims=False)
            mine = jnp.where(upper, second, first)
            other = jnp.where(upper, first, second)
        other = flip(other, axis, 1 << i)
        blocks = ordered(mine, other, upper, 0)
    return blocks.reshape((count,) + rest)


def spread_blocks(blocks, axis, order):
    count = lax.axis_size(axis)
    lead, rest = blocks.shape[0], blocks.shape[1:]
    done = []
    for bit in order:
        upper = lax.axis_index(axis) & (1 << bit) != 0
        other = flip(blocks, axis, 1 << bit)
        blocks = ordered(blocks, other, upper, 1 + sum(b > bit for b in done))
        done.append(bit)
    return blocks.reshape((lead, count) + rest)


def exchange(blocks):
    return lax.all_to_all(blocks, ("section", "ctx"), 0, 0, tiled=True)


def compute(block_order, queries, cache_keys, cache_values, attention_out, output_grad):
    sections = lax.axis_size("section")
    ctx_count = lax.axis_size("ctx")
    assert ctx_count & (ctx_count - 1) == 0
    assert sections & (sections - 1) == 0 and sections > 1
    layers, rows, _ = queries.shape
    assert layers == 1
    key_count, here = cache_keys.shape
    row_count = rows * ctx_count
    key_total = key_count * ctx_count
    peers = sections * ctx_count

    ctx_bits = ctx_count.bit_length() - 1
    down = list(range(ctx_bits))[::-1]

    packed = pack(
        block_order,
        cache_keys,
        cache_values,
        queries[0],
        output_grad[0],
        attention_out[0],
        sections,
    )
    start, keys, values = packed[4:]
    query_all = swap_blocks(packed[0], packed[1], "section")
    query_all = spread_blocks(query_all, "ctx", down)
    query_all = query_all.reshape(peers * rows, here)
    grad_all = swap_blocks(packed[2], packed[3], "section")
    grad_all = spread_blocks(grad_all, "ctx", down[:1] + down[1:][::-1])
    grad_all = grad_all.reshape(peers * rows, here + LANES)

    own = stats_kernel(start, query_all, keys, row_count, key_total)
    merged = merge_stats(own, "ctx", down[-1:] + down[:-1])
    part, probs, score_grads = query_kernel(
        start, query_all, grad_all, keys, values, own, row_count, key_total
    )
    part = exchange(part.reshape(peers, rows, here + LANES))
    grad_keys, grad_values = cache_kernel(query_all, grad_all, probs, score_grads, own, merged)
    grad_queries = combine_kernel(part.reshape(sections, ctx_count, rows, here + LANES))
    return (grad_queries[None], grad_keys, grad_values)


def solution(mesh):
    in_specs = (
        P(),
        P("section", "ctx", None),
        P("ctx", "section"),
        P("ctx", "section"),
        P("section", "ctx", None),
        P("section", "ctx", None),
    )
    out_specs = (P("section", "ctx", None), P("ctx", "section"), P("ctx", "section"))
    return jax.shard_map(compute, mesh=mesh, in_specs=in_specs, out_specs=out_specs, check_vma=False)
```

```python
import math

import jax
import jax.numpy as jnp
from jax import lax
from jax.experimental import pallas as pl
from jax.experimental.pallas import tpu as pltpu
from jax.sharding import PartitionSpec as P


HEAD_DIM = 128
LANES = 128
ON_CHIP_BYTES = 1 << 20
masked_score = -1e30
BF = jnp.bfloat16
F32 = jnp.float32


def nt(a, b):
    return lax.dot_general(a, b, (((1,), (1,)), ((), ())), preferred_element_type=F32)


def nn(a, b):
    return lax.dot_general(a, b, (((1,), (0,)), ((), ())), preferred_element_type=F32)


def tn(a, b):
    return lax.dot_general(a, b, (((0,), (0,)), ((), ())), preferred_element_type=F32)


def split3(x):
    hi = x.astype(BF)
    rest = x - hi.astype(F32)
    mid = rest.astype(BF)
    low = (rest - mid.astype(F32)).astype(BF)
    return hi, mid, low


def in_vmem(count):
    return [pl.BlockSpec(memory_space=pltpu.VMEM) for _ in range(count)]


def small(shape, dtype):
    return math.prod(shape) * jnp.dtype(dtype).itemsize <= ON_CHIP_BYTES


def vmem(value):
    if small(value.shape, value.dtype):
        return pltpu.with_memory_space_constraint(value, pltpu.VMEM)
    return value


def held(shape, dtype):
    if small(shape, dtype):
        return pltpu.VMEM(shape, dtype)
    return jax.ShapeDtypeStruct(shape, dtype)


def head_of(h):
    return pl.ds(h * HEAD_DIM, HEAD_DIM)


def pack(block_order, keys, values, queries, grads, outs, sections):
    rows, features = grads.shape
    here = features // sections
    heads = here // HEAD_DIM
    key_count = keys.shape[0]
    half = sections // 2

    def body(order_hbm, k_hbm, v_hbm, q_hbm, g_hbm, o_hbm, *refs):
        q_mine, q_other, g_mine, g_other, start_ref, k_ref, v_ref = refs[:7]
        q_ref, g_ref, o_ref, order_ref, sems = refs[7:]
        pairs = [
            (q_hbm, q_ref),
            (g_hbm, g_ref),
            (o_hbm, o_ref),
            (order_hbm, order_ref),
            (k_hbm, k_ref),
            (v_hbm, v_ref),
        ]
        copies = [pltpu.make_async_copy(*pair, sems.at[i]) for i, pair in enumerate(pairs)]
        for copy in copies:
            copy.start()
        odd = lax.axis_index("section") % 2
        lane = lax.broadcasted_iota(jnp.int32, (rows, LANES), 1)

        def at(s, h):
            return pl.ds(pl.multiple_of(s * here + h * HEAD_DIM, HEAD_DIM), HEAD_DIM)

        for i in range(3):
            copies[i].wait()
        for q_out, g_out, bit in ((q_mine, g_mine, odd), (q_other, g_other, 1 - odd)):
            for j in range(half):
                extra = jnp.zeros((rows, LANES), F32)
                for h in range(heads):
                    g = g_ref[:, at(2 * j + bit, h)]
                    terms = g.astype(F32) * o_ref[:, at(2 * j + bit, h)].astype(F32)
                    delta = jnp.sum(terms, axis=1, keepdims=True)
                    for part, value in enumerate(split3(delta)):
                        extra = jnp.where(lane == part * heads + h, value.astype(F32), extra)
                    g_out[j, :, head_of(h)] = g
                    q_out[j, :, head_of(h)] = q_ref[:, at(2 * j + bit, h)]
                q_out[j, :, pl.ds(here, LANES)] = extra.astype(BF)
        copies[3].wait()
        block = order_ref[lax.axis_index("ctx")]
        start_ref[...] = jnp.full(start_ref.shape, block * key_count, jnp.int32)
        copies[4].wait()
        copies[5].wait()

    query_half = held((half, rows, here + LANES), BF)
    grad_half = held((half, rows, here), BF)
    return pl.pallas_call(
        body,
        in_specs=[pl.BlockSpec(memory_space=pl.ANY)] * 6,
        out_specs=in_vmem(7),
        out_shape=[
            query_half,
            query_half,
            grad_half,
            grad_half,
            held((8, LANES), jnp.int32),
            held(keys.shape, BF),
            held(values.shape, BF),
        ],
        scratch_shapes=[
            pltpu.VMEM((rows, features), BF),
            pltpu.VMEM((rows, features), BF),
            pltpu.VMEM((rows, features), BF),
            pltpu.SMEM(block_order.shape, jnp.int32),
            pltpu.SemaphoreType.DMA((6,)),
        ],
        name="pack",
    )(block_order, keys, values, queries, grads, outs)


def visible_of(start_ref, shape, row_count, key_total):
    key_pos = start_ref[0:1, 0:1] + lax.broadcasted_iota(jnp.int32, shape, 0)
    row = lax.broadcasted_iota(jnp.int32, shape, 1) % row_count
    return key_pos <= key_total - row_count + row


def stats_kernel(start, queries, keys, row_count, key_total):
    m = queries.shape[0]
    key_count, here = keys.shape
    heads = here // HEAD_DIM
    slots = -(-heads // 8) * 8
    scaling = HEAD_DIM ** (-0.5)

    def body(start_ref, q_ref, k_ref, out_ref):
        visible = visible_of(start_ref, (key_count, m), row_count, key_total)
        out_ref[...] = jnp.ones_like(out_ref)
        for h in range(heads):
            at = head_of(h)
            s = jnp.where(visible, nt(k_ref[:, at], q_ref[:, at]) * scaling, masked_score)
            top = jnp.max(s, axis=0, keepdims=True)
            total = jnp.sum(jnp.where(visible, jnp.exp(s - top), 0.0), axis=0, keepdims=True)
            out_ref[0, pl.ds(h, 1), :] = top
            out_ref[1, pl.ds(h, 1), :] = total

    return pl.pallas_call(
        body,
        in_specs=in_vmem(3),
        out_specs=in_vmem(1)[0],
        out_shape=held((2, slots, m), F32),
        name="stats",
    )(vmem(start), vmem(queries), vmem(keys))


def query_kernel(start, queries, grads, keys, values, stats, row_count, key_total):
    m = queries.shape[0]
    key_count, here = keys.shape
    heads = here // HEAD_DIM
    slots = stats.shape[1]
    scaling = HEAD_DIM ** (-0.5)

    def body(start_ref, q_ref, g_ref, k_ref, v_ref, l_ref, u_ref, p_ref, ds_ref):
        visible = visible_of(start_ref, (key_count, m), row_count, key_total)
        extra = q_ref[:, pl.ds(here, LANES)]
        slot = lax.broadcasted_iota(jnp.int32, (slots, LANES), 0)
        lane = lax.broadcasted_iota(jnp.int32, (slots, LANES), 1)
        pick = (lane % heads == slot) & (lane < 3 * heads)
        delta = nt(jnp.where(pick, 1.0, 0.0).astype(BF), extra)
        tops = l_ref[0]
        for h in range(heads):
            at = head_of(h)
            k = k_ref[:, at]
            s = nt(k, q_ref[:, at]) * scaling
            prob = jnp.where(visible, jnp.exp(s - tops[h : h + 1, :]), 0.0)
            ds = prob * (nt(v_ref[:, at], g_ref[:, at]) - delta[h : h + 1, :]) * scaling
            ds = ds.astype(BF)
            u_ref[:, at] = tn(ds, k).astype(BF)
            p_ref[h] = prob.astype(BF)
            ds_ref[h] = ds
        sent = jnp.zeros((m, LANES), F32)
        for i in range(2):
            for part, value in enumerate(split3(l_ref[i])):
                at = (3 * i + part) * heads
                place = (lane == at + slot) & (slot < heads)
                sent += tn(value, jnp.where(place, 1.0, 0.0).astype(BF))
        u_ref[:, pl.ds(here, LANES)] = sent.astype(BF)

    return pl.pallas_call(
        body,
        in_specs=in_vmem(6),
        out_specs=in_vmem(3),
        out_shape=[
            jax.ShapeDtypeStruct((m, here + LANES), BF),
            held((heads, key_count, m), BF),
            held((heads, key_count, m), BF),
        ],
        name="query_gradients",
    )(vmem(start), vmem(queries), vmem(grads), vmem(keys), vmem(values), vmem(stats))


def cache_kernel(queries, grads, probs, score_grads, own, merged):
    here = grads.shape[1]
    heads, key_count, _ = probs.shape

    def body(q_ref, g_ref, p_ref, ds_ref, own_ref, all_ref, dk_ref, dv_ref):
        share = jnp.exp(own_ref[0] - all_ref[0]) / all_ref[1]
        for h in range(heads):
            at = head_of(h)
            row = share[h : h + 1, :]
            ds = (ds_ref[h].astype(F32) * row).astype(BF)
            prob = (p_ref[h].astype(F32) * row).astype(BF)
            dk_ref[:, at] = nn(ds, q_ref[:, at]).astype(BF)
            dv_ref[:, at] = nn(prob, g_ref[:, at]).astype(BF)

    return pl.pallas_call(
        body,
        in_specs=in_vmem(6),
        out_specs=in_vmem(2),
        out_shape=[jax.ShapeDtypeStruct((key_count, here), BF)] * 2,
        name="cache_gradients",
    )(vmem(queries), vmem(grads), vmem(probs), vmem(score_grads), vmem(own), vmem(merged))


def combine_kernel(parts):
    sections, holders, rows, width = parts.shape
    here = width - LANES
    heads = here // HEAD_DIM

    def body(p_ref, out_ref):
        def stats_of(s, c):
            e = p_ref[s, c, :, pl.ds(here, LANES)].astype(F32)
            e += pltpu.roll(e, LANES - heads, 1) + pltpu.roll(e, LANES - 2 * heads, 1)
            return e, pltpu.roll(e, LANES - 3 * heads, 1)

        for s in range(sections):
            top = jnp.full((rows, LANES), -jnp.inf, F32)
            for c in range(holders):
                top = jnp.maximum(top, stats_of(s, c)[0])
            total = jnp.zeros((rows, LANES), F32)
            for c in range(holders):
                own, count = stats_of(s, c)
                total += jnp.exp(own - top) * count
            sums = [jnp.zeros((rows, HEAD_DIM), F32) for _ in range(heads)]
            for c in range(holders):
                share = jnp.exp(stats_of(s, c)[0] - top) / total
                for h in range(heads):
                    value = p_ref[s, c, :, head_of(h)].astype(F32)
                    sums[h] += share[:, h : h + 1] * value
            for h in range(heads):
                out_ref[:, head_of(s * heads + h)] = sums[h].astype(BF)

    return pl.pallas_call(
        body,
        in_specs=in_vmem(1),
        out_specs=in_vmem(1)[0],
        out_shape=jax.ShapeDtypeStruct((rows, sections * here), BF),
        name="combine",
    )(vmem(parts))


def merge_stats(stats, axis, order):
    for bit in order:
        other = flip(stats, axis, 1 << bit)
        top = jnp.maximum(stats[0], other[0])
        total = stats[1] * jnp.exp(stats[0] - top) + other[1] * jnp.exp(other[0] - top)
        stats = jnp.stack([top, total])
    return stats


def flip(value, axis, bit):
    count = lax.axis_size(axis)
    return lax.ppermute(value, axis, [(i, i ^ bit) for i in range(count)])


def ordered(mine, other, upper, axis):
    first = jnp.where(upper, other, mine)
    second = jnp.where(upper, mine, other)
    return jnp.stack([first, second], axis)


def swap_blocks(mine, other, axis):
    count = lax.axis_size(axis)
    bits = count.bit_length() - 1
    rest = mine.shape[1:]
    mine = mine.reshape((2,) * (bits - 1) + rest)
    other = other.reshape(mine.shape)
    for i in range(bits):
        upper = (lax.axis_index(axis) >> i) % 2 == 1
        if i:
            first = lax.index_in_dim(blocks, 0, bits - 1, keepdims=False)
            second = lax.index_in_dim(blocks, 1, bits - 1, keepdims=False)
            mine = jnp.where(upper, second, first)
            other = jnp.where(upper, first, second)
        other = flip(other, axis, 1 << i)
        blocks = ordered(mine, other, upper, 0)
    return blocks.reshape((count,) + rest)


def spread_blocks(blocks, axis, order):
    count = lax.axis_size(axis)
    lead, rest = blocks.shape[0], blocks.shape[1:]
    done = []
    for bit in order:
        upper = lax.axis_index(axis) & (1 << bit) != 0
        other = flip(blocks, axis, 1 << bit)
        blocks = ordered(blocks, other, upper, 1 + sum(b > bit for b in done))
        done.append(bit)
    return blocks.reshape((lead, count) + rest)


def exchange(blocks):
    return lax.all_to_all(blocks, ("section", "ctx"), 0, 0, tiled=True)


def compute(block_order, queries, cache_keys, cache_values, attention_out, output_grad):
    sections = lax.axis_size("section")
    ctx_count = lax.axis_size("ctx")
    assert ctx_count & (ctx_count - 1) == 0
    assert sections & (sections - 1) == 0 and sections > 1
    layers, rows, _ = queries.shape
    assert layers == 1
    key_count, here = cache_keys.shape
    row_count = rows * ctx_count
    key_total = key_count * ctx_count
    peers = sections * ctx_count

    ctx_bits = ctx_count.bit_length() - 1
    down = list(range(ctx_bits))[::-1]

    packed = pack(
        block_order,
        cache_keys,
        cache_values,
        queries[0],
        output_grad[0],
        attention_out[0],
        sections,
    )
    start, keys, values = packed[4:]
    query_all = swap_blocks(packed[0], packed[1], "section")
    query_all = spread_blocks(query_all, "ctx", down)
    query_all = query_all.reshape(peers * rows, here + LANES)
    grad_all = swap_blocks(packed[2], packed[3], "section")
    grad_all = spread_blocks(grad_all, "ctx", down[:1] + down[1:][::-1])
    grad_all = grad_all.reshape(peers * rows, here)

    own = stats_kernel(start, query_all, keys, row_count, key_total)
    merged = merge_stats(own, "ctx", down[::-1])
    part, probs, score_grads = query_kernel(
        start, query_all, grad_all, keys, values, own, row_count, key_total
    )
    part = exchange(part.reshape(peers, rows, here + LANES))
    grad_keys, grad_values = cache_kernel(query_all, grad_all, probs, score_grads, own, merged)
    grad_queries = combine_kernel(part.reshape(sections, ctx_count, rows, here + LANES))
    return (grad_queries[None], grad_keys, grad_values)


def solution(mesh):
    in_specs = (
        P(),
        P("section", "ctx", None),
        P("ctx", "section"),
        P("ctx", "section"),
        P("section", "ctx", None),
        P("section", "ctx", None),
    )
    out_specs = (P("section", "ctx", None), P("ctx", "section"), P("ctx", "section"))
    return jax.shard_map(compute, mesh=mesh, in_specs=in_specs, out_specs=out_specs, check_vma=False)
```

```python
import math

import jax
import jax.numpy as jnp
from jax import lax
from jax.experimental import pallas as pl
from jax.experimental.pallas import tpu as pltpu
from jax.sharding import PartitionSpec as P


HEAD_DIM = 128
LANES = 128
ON_CHIP_BYTES = 1 << 20
masked_score = -1e30
BF = jnp.bfloat16
F32 = jnp.float32


def nt(a, b):
    return lax.dot_general(a, b, (((1,), (1,)), ((), ())), preferred_element_type=F32)


def nn(a, b):
    return lax.dot_general(a, b, (((1,), (0,)), ((), ())), preferred_element_type=F32)


def tn(a, b):
    return lax.dot_general(a, b, (((0,), (0,)), ((), ())), preferred_element_type=F32)


def split3(x):
    hi = x.astype(BF)
    rest = x - hi.astype(F32)
    mid = rest.astype(BF)
    low = (rest - mid.astype(F32)).astype(BF)
    return hi, mid, low


def in_vmem(count):
    return [pl.BlockSpec(memory_space=pltpu.VMEM) for _ in range(count)]


def small(shape, dtype):
    return math.prod(shape) * jnp.dtype(dtype).itemsize <= ON_CHIP_BYTES


def vmem(value):
    if small(value.shape, value.dtype):
        return pltpu.with_memory_space_constraint(value, pltpu.VMEM)
    return value


def held(shape, dtype):
    if small(shape, dtype):
        return pltpu.VMEM(shape, dtype)
    return jax.ShapeDtypeStruct(shape, dtype)


def head_of(h):
    return pl.ds(h * HEAD_DIM, HEAD_DIM)


def pack(block_order, keys, values, queries, grads, outs, sections):
    rows, features = grads.shape
    here = features // sections
    heads = here // HEAD_DIM
    key_count = keys.shape[0]
    half = sections // 2

    def body(order_hbm, k_hbm, v_hbm, q_hbm, g_hbm, o_hbm, *refs):
        q_mine, q_other, g_mine, g_other, start_ref, k_ref, v_ref = refs[:7]
        q_ref, g_ref, o_ref, order_ref, sems = refs[7:]
        pairs = [
            (q_hbm, q_ref),
            (g_hbm, g_ref),
            (o_hbm, o_ref),
            (order_hbm, order_ref),
            (k_hbm, k_ref),
            (v_hbm, v_ref),
        ]
        copies = [pltpu.make_async_copy(*pair, sems.at[i]) for i, pair in enumerate(pairs)]
        for copy in copies:
            copy.start()
        odd = lax.axis_index("section") % 2
        lane = lax.broadcasted_iota(jnp.int32, (rows, LANES), 1)

        def at(s, h):
            return pl.ds(pl.multiple_of(s * here + h * HEAD_DIM, HEAD_DIM), HEAD_DIM)

        for i in range(3):
            copies[i].wait()
        for q_out, g_out, bit in ((q_mine, g_mine, odd), (q_other, g_other, 1 - odd)):
            for j in range(half):
                extra = jnp.zeros((rows, LANES), F32)
                for h in range(heads):
                    g = g_ref[:, at(2 * j + bit, h)]
                    terms = g.astype(F32) * o_ref[:, at(2 * j + bit, h)].astype(F32)
                    delta = jnp.sum(terms, axis=1, keepdims=True)
                    for part, value in enumerate(split3(delta)):
                        extra = jnp.where(lane == part * heads + h, value.astype(F32), extra)
                    g_out[j, :, head_of(h)] = g
                    q_out[j, :, head_of(h)] = q_ref[:, at(2 * j + bit, h)]
                q_out[j, :, pl.ds(here, LANES)] = extra.astype(BF)
        copies[3].wait()
        block = order_ref[lax.axis_index("ctx")]
        start_ref[...] = jnp.full(start_ref.shape, block * key_count, jnp.int32)
        copies[4].wait()
        copies[5].wait()

    query_half = held((half, rows, here + LANES), BF)
    grad_half = held((half, rows, here), BF)
    return pl.pallas_call(
        body,
        in_specs=[pl.BlockSpec(memory_space=pl.ANY)] * 6,
        out_specs=in_vmem(7),
        out_shape=[
            query_half,
            query_half,
            grad_half,
            grad_half,
            held((8, LANES), jnp.int32),
            held(keys.shape, BF),
            held(values.shape, BF),
        ],
        scratch_shapes=[
            pltpu.VMEM((rows, features), BF),
            pltpu.VMEM((rows, features), BF),
            pltpu.VMEM((rows, features), BF),
            pltpu.SMEM(block_order.shape, jnp.int32),
            pltpu.SemaphoreType.DMA((6,)),
        ],
        name="pack",
    )(block_order, keys, values, queries, grads, outs)


def visible_of(start_ref, shape, row_count, key_total):
    key_pos = start_ref[0:1, 0:1] + lax.broadcasted_iota(jnp.int32, shape, 0)
    row = lax.broadcasted_iota(jnp.int32, shape, 1) % row_count
    return key_pos <= key_total - row_count + row


def stats_kernel(start, queries, keys, row_count, key_total):
    m = queries.shape[0]
    key_count, here = keys.shape
    heads = here // HEAD_DIM
    slots = -(-heads // 8) * 8
    scaling = HEAD_DIM ** (-0.5)

    def body(start_ref, q_ref, k_ref, out_ref):
        visible = visible_of(start_ref, (key_count, m), row_count, key_total)
        out_ref[...] = jnp.ones_like(out_ref)
        for h in range(heads):
            at = head_of(h)
            s = jnp.where(visible, nt(k_ref[:, at], q_ref[:, at]) * scaling, masked_score)
            top = jnp.max(s, axis=0, keepdims=True)
            total = jnp.sum(jnp.where(visible, jnp.exp(s - top), 0.0), axis=0, keepdims=True)
            out_ref[0, pl.ds(h, 1), :] = top
            out_ref[1, pl.ds(h, 1), :] = total

    return pl.pallas_call(
        body,
        in_specs=in_vmem(3),
        out_specs=in_vmem(1)[0],
        out_shape=held((2, slots, m), F32),
        name="stats",
    )(vmem(start), vmem(queries), vmem(keys))


def query_kernel(start, queries, grads, keys, values, stats, row_count, key_total):
    m = queries.shape[0]
    key_count, here = keys.shape
    heads = here // HEAD_DIM
    slots = stats.shape[1]
    scaling = HEAD_DIM ** (-0.5)

    def body(start_ref, q_ref, g_ref, k_ref, v_ref, l_ref, *refs):
        u_hbm, p_ref, ds_ref, u_ref, sems = refs

        def copy_of(h, width):
            at = pl.ds(h * HEAD_DIM, width)
            return pltpu.make_async_copy(u_ref.at[:, at], u_hbm.at[:, at], sems.at[h])

        visible = visible_of(start_ref, (key_count, m), row_count, key_total)
        extra = q_ref[:, pl.ds(here, LANES)]
        slot = lax.broadcasted_iota(jnp.int32, (slots, LANES), 0)
        lane = lax.broadcasted_iota(jnp.int32, (slots, LANES), 1)
        pick = (lane % heads == slot) & (lane < 3 * heads)
        delta = nt(jnp.where(pick, 1.0, 0.0).astype(BF), extra)
        tops = l_ref[0]
        sent = jnp.zeros((m, LANES), F32)
        for i in range(2):
            for part, value in enumerate(split3(l_ref[i])):
                at = (3 * i + part) * heads
                place = (lane == at + slot) & (slot < heads)
                sent += tn(value, jnp.where(place, 1.0, 0.0).astype(BF))
        u_ref[:, pl.ds(here, LANES)] = sent.astype(BF)
        copy_of(heads, LANES).start()
        for h in range(heads):
            at = head_of(h)
            k = k_ref[:, at]
            s = nt(k, q_ref[:, at]) * scaling
            prob = jnp.where(visible, jnp.exp(s - tops[h : h + 1, :]), 0.0)
            ds = prob * (nt(v_ref[:, at], g_ref[:, at]) - delta[h : h + 1, :]) * scaling
            ds = ds.astype(BF)
            u_ref[:, at] = tn(ds, k).astype(BF)
            copy_of(h, HEAD_DIM).start()
            p_ref[h] = prob.astype(BF)
            ds_ref[h] = ds
        for h in range(heads):
            copy_of(h, HEAD_DIM).wait()
        copy_of(heads, LANES).wait()

    return pl.pallas_call(
        body,
        in_specs=in_vmem(6),
        out_specs=[pl.BlockSpec(memory_space=pl.ANY), *in_vmem(2)],
        out_shape=[
            jax.ShapeDtypeStruct((m, here + LANES), BF),
            held((heads, key_count, m), BF),
            held((heads, key_count, m), BF),
        ],
        scratch_shapes=[
            pltpu.VMEM((m, here + LANES), BF),
            pltpu.SemaphoreType.DMA((heads + 1,)),
        ],
        name="query_gradients",
    )(vmem(start), vmem(queries), vmem(grads), vmem(keys), vmem(values), vmem(stats))


def cache_kernel(queries, grads, probs, score_grads, own, merged):
    here = grads.shape[1]
    heads, key_count, _ = probs.shape

    def body(q_ref, g_ref, p_ref, ds_ref, own_ref, all_ref, dk_ref, dv_ref):
        share = jnp.exp(own_ref[0] - all_ref[0]) / all_ref[1]
        for h in range(heads):
            at = head_of(h)
            row = share[h : h + 1, :]
            ds = (ds_ref[h].astype(F32) * row).astype(BF)
            prob = (p_ref[h].astype(F32) * row).astype(BF)
            dk_ref[:, at] = nn(ds, q_ref[:, at]).astype(BF)
            dv_ref[:, at] = nn(prob, g_ref[:, at]).astype(BF)

    return pl.pallas_call(
        body,
        in_specs=in_vmem(6),
        out_specs=in_vmem(2),
        out_shape=[jax.ShapeDtypeStruct((key_count, here), BF)] * 2,
        name="cache_gradients",
    )(vmem(queries), vmem(grads), vmem(probs), vmem(score_grads), vmem(own), vmem(merged))


def combine_kernel(parts):
    sections, holders, rows, width = parts.shape
    here = width - LANES
    heads = here // HEAD_DIM

    def body(p_ref, out_ref):
        def stats_of(s, c):
            e = p_ref[s, c, :, pl.ds(here, LANES)].astype(F32)
            e += pltpu.roll(e, LANES - heads, 1) + pltpu.roll(e, LANES - 2 * heads, 1)
            return e, pltpu.roll(e, LANES - 3 * heads, 1)

        for s in range(sections):
            top = jnp.full((rows, LANES), -jnp.inf, F32)
            for c in range(holders):
                top = jnp.maximum(top, stats_of(s, c)[0])
            total = jnp.zeros((rows, LANES), F32)
            for c in range(holders):
                own, count = stats_of(s, c)
                total += jnp.exp(own - top) * count
            sums = [jnp.zeros((rows, HEAD_DIM), F32) for _ in range(heads)]
            for c in range(holders):
                share = jnp.exp(stats_of(s, c)[0] - top) / total
                for h in range(heads):
                    value = p_ref[s, c, :, head_of(h)].astype(F32)
                    sums[h] += share[:, h : h + 1] * value
            for h in range(heads):
                out_ref[:, head_of(s * heads + h)] = sums[h].astype(BF)

    return pl.pallas_call(
        body,
        in_specs=in_vmem(1),
        out_specs=in_vmem(1)[0],
        out_shape=jax.ShapeDtypeStruct((rows, sections * here), BF),
        name="combine",
    )(vmem(parts))


def merge_stats(stats, axis, order):
    for bit in order:
        other = flip(stats, axis, 1 << bit)
        top = jnp.maximum(stats[0], other[0])
        total = stats[1] * jnp.exp(stats[0] - top) + other[1] * jnp.exp(other[0] - top)
        stats = jnp.stack([top, total])
    return stats


def flip(value, axis, bit):
    count = lax.axis_size(axis)
    return lax.ppermute(value, axis, [(i, i ^ bit) for i in range(count)])


def ordered(mine, other, upper, axis):
    first = jnp.where(upper, other, mine)
    second = jnp.where(upper, mine, other)
    return jnp.stack([first, second], axis)


def swap_blocks(mine, other, axis):
    count = lax.axis_size(axis)
    bits = count.bit_length() - 1
    rest = mine.shape[1:]
    mine = mine.reshape((2,) * (bits - 1) + rest)
    other = other.reshape(mine.shape)
    for i in range(bits):
        upper = (lax.axis_index(axis) >> i) % 2 == 1
        if i:
            first = lax.index_in_dim(blocks, 0, bits - 1, keepdims=False)
            second = lax.index_in_dim(blocks, 1, bits - 1, keepdims=False)
            mine = jnp.where(upper, second, first)
            other = jnp.where(upper, first, second)
        other = flip(other, axis, 1 << i)
        blocks = ordered(mine, other, upper, 0)
    return blocks.reshape((count,) + rest)


def spread_blocks(blocks, axis, order):
    count = lax.axis_size(axis)
    lead, rest = blocks.shape[0], blocks.shape[1:]
    done = []
    for bit in order:
        upper = lax.axis_index(axis) & (1 << bit) != 0
        other = flip(blocks, axis, 1 << bit)
        blocks = ordered(blocks, other, upper, 1 + sum(b > bit for b in done))
        done.append(bit)
    return blocks.reshape((lead, count) + rest)


def exchange(blocks):
    return lax.all_to_all(blocks, ("section", "ctx"), 0, 0, tiled=True)


def compute(block_order, queries, cache_keys, cache_values, attention_out, output_grad):
    sections = lax.axis_size("section")
    ctx_count = lax.axis_size("ctx")
    assert ctx_count & (ctx_count - 1) == 0
    assert sections & (sections - 1) == 0 and sections > 1
    layers, rows, _ = queries.shape
    assert layers == 1
    key_count, here = cache_keys.shape
    row_count = rows * ctx_count
    key_total = key_count * ctx_count
    peers = sections * ctx_count

    ctx_bits = ctx_count.bit_length() - 1
    down = list(range(ctx_bits))[::-1]

    packed = pack(
        block_order,
        cache_keys,
        cache_values,
        queries[0],
        output_grad[0],
        attention_out[0],
        sections,
    )
    start, keys, values = packed[4:]
    query_all = swap_blocks(packed[0], packed[1], "section")
    query_all = spread_blocks(query_all, "ctx", down)
    query_all = query_all.reshape(peers * rows, here + LANES)
    grad_all = swap_blocks(packed[2], packed[3], "section")
    grad_all = spread_blocks(grad_all, "ctx", down[:1] + down[1:][::-1])
    grad_all = grad_all.reshape(peers * rows, here)

    own = stats_kernel(start, query_all, keys, row_count, key_total)
    merged = merge_stats(own, "ctx", down[::-1])
    part, probs, score_grads = query_kernel(
        start, query_all, grad_all, keys, values, own, row_count, key_total
    )
    part = exchange(part.reshape(peers, rows, here + LANES))
    grad_keys, grad_values = cache_kernel(query_all, grad_all, probs, score_grads, own, merged)
    grad_queries = combine_kernel(part.reshape(sections, ctx_count, rows, here + LANES))
    return (grad_queries[None], grad_keys, grad_values)


def solution(mesh):
    in_specs = (
        P(),
        P("section", "ctx", None),
        P("ctx", "section"),
        P("ctx", "section"),
        P("section", "ctx", None),
        P("section", "ctx", None),
    )
    out_specs = (P("section", "ctx", None), P("ctx", "section"), P("ctx", "section"))
    return jax.shard_map(compute, mesh=mesh, in_specs=in_specs, out_specs=out_specs, check_vma=False)
```

```python
import math

import jax
import jax.numpy as jnp
from jax import lax
from jax.experimental import pallas as pl
from jax.experimental.pallas import tpu as pltpu
from jax.sharding import PartitionSpec as P


HEAD_DIM = 128
LANES = 128
ON_CHIP_BYTES = 1 << 20
masked_score = -1e30
BF = jnp.bfloat16
F32 = jnp.float32


def nt(a, b):
    return lax.dot_general(a, b, (((1,), (1,)), ((), ())), preferred_element_type=F32)


def nn(a, b):
    return lax.dot_general(a, b, (((1,), (0,)), ((), ())), preferred_element_type=F32)


def tn(a, b):
    return lax.dot_general(a, b, (((0,), (0,)), ((), ())), preferred_element_type=F32)


def split3(x):
    hi = x.astype(BF)
    rest = x - hi.astype(F32)
    mid = rest.astype(BF)
    low = (rest - mid.astype(F32)).astype(BF)
    return hi, mid, low


def in_vmem(count):
    return [pl.BlockSpec(memory_space=pltpu.VMEM) for _ in range(count)]


def small(shape, dtype):
    return math.prod(shape) * jnp.dtype(dtype).itemsize <= ON_CHIP_BYTES


def vmem(value):
    if small(value.shape, value.dtype):
        return pltpu.with_memory_space_constraint(value, pltpu.VMEM)
    return value


def held(shape, dtype):
    if small(shape, dtype):
        return pltpu.VMEM(shape, dtype)
    return jax.ShapeDtypeStruct(shape, dtype)


def head_of(h):
    return pl.ds(h * HEAD_DIM, HEAD_DIM)


def pack(block_order, keys, values, queries, grads, outs, sections):
    rows, features = grads.shape
    here = features // sections
    heads = here // HEAD_DIM
    key_count = keys.shape[0]

    def body(order_hbm, k_hbm, v_hbm, q_hbm, g_hbm, o_hbm, *refs):
        blocks = refs[:sections]
        start_ref, k_ref, v_ref, q_ref, g_ref, o_ref, order_ref, sems = refs[sections:]
        pairs = [
            (q_hbm, q_ref),
            (g_hbm, g_ref),
            (o_hbm, o_ref),
            (order_hbm, order_ref),
            (k_hbm, k_ref),
            (v_hbm, v_ref),
        ]
        copies = [pltpu.make_async_copy(*pair, sems.at[i]) for i, pair in enumerate(pairs)]
        for copy in copies:
            copy.start()
        section = lax.axis_index("section")
        lane = lax.broadcasted_iota(jnp.int32, (rows, LANES), 1)

        def at(s, h):
            return pl.ds(pl.multiple_of(s * here + h * HEAD_DIM, HEAD_DIM), HEAD_DIM)

        for i in range(3):
            copies[i].wait()
        for step, out_ref in enumerate(blocks):
            to = section ^ step
            extra = jnp.zeros((rows, LANES), F32)
            for h in range(heads):
                g = g_ref[:, at(to, h)]
                terms = g.astype(F32) * o_ref[:, at(to, h)].astype(F32)
                delta = jnp.sum(terms, axis=1, keepdims=True)
                for part, value in enumerate(split3(delta)):
                    extra = jnp.where(lane == part * heads + h, value.astype(F32), extra)
                out_ref[:, head_of(h)] = q_ref[:, at(to, h)]
                out_ref[:, head_of(heads + 1 + h)] = g
            out_ref[:, head_of(heads)] = extra.astype(BF)
        copies[3].wait()
        block = order_ref[lax.axis_index("ctx")]
        start_ref[...] = jnp.full(start_ref.shape, block * key_count, jnp.int32)
        copies[4].wait()
        copies[5].wait()

    return pl.pallas_call(
        body,
        in_specs=[pl.BlockSpec(memory_space=pl.ANY)] * 6,
        out_specs=in_vmem(sections + 3),
        out_shape=[
            *[held((rows, 2 * here + LANES), BF)] * sections,
            held((8, LANES), jnp.int32),
            held(keys.shape, BF),
            held(values.shape, BF),
        ],
        scratch_shapes=[
            pltpu.VMEM((rows, features), BF),
            pltpu.VMEM((rows, features), BF),
            pltpu.VMEM((rows, features), BF),
            pltpu.SMEM(block_order.shape, jnp.int32),
            pltpu.SemaphoreType.DMA((6,)),
        ],
        name="pack",
    )(block_order, keys, values, queries, grads, outs)


def visible_of(start_ref, shape, row_count, key_total):
    key_pos = start_ref[0:1, 0:1] + lax.broadcasted_iota(jnp.int32, shape, 0)
    row = lax.broadcasted_iota(jnp.int32, shape, 1) % row_count
    return key_pos <= key_total - row_count + row


def stats_kernel(start, queries, keys, row_count, key_total):
    m = queries.shape[0]
    key_count, here = keys.shape
    heads = here // HEAD_DIM
    slots = -(-heads // 8) * 8
    scaling = HEAD_DIM ** (-0.5)

    def body(start_ref, q_ref, k_ref, out_ref):
        visible = visible_of(start_ref, (key_count, m), row_count, key_total)
        out_ref[...] = jnp.ones_like(out_ref)
        for h in range(heads):
            at = head_of(h)
            s = jnp.where(visible, nt(k_ref[:, at], q_ref[:, at]) * scaling, masked_score)
            top = jnp.max(s, axis=0, keepdims=True)
            total = jnp.sum(jnp.where(visible, jnp.exp(s - top), 0.0), axis=0, keepdims=True)
            out_ref[0, pl.ds(h, 1), :] = top
            out_ref[1, pl.ds(h, 1), :] = total

    return pl.pallas_call(
        body,
        in_specs=in_vmem(3),
        out_specs=in_vmem(1)[0],
        out_shape=held((2, slots, m), F32),
        name="stats",
    )(vmem(start), vmem(queries), vmem(keys))


def query_kernel(start, queries, grads, keys, values, stats, row_count, key_total):
    m = queries.shape[0]
    key_count, here = keys.shape
    heads = here // HEAD_DIM
    slots = stats.shape[1]
    scaling = HEAD_DIM ** (-0.5)

    def body(start_ref, q_ref, g_ref, k_ref, v_ref, l_ref, *refs):
        u_hbm, p_ref, ds_ref, u_ref, sems = refs

        def copy_of(h, width):
            at = pl.ds(h * HEAD_DIM, width)
            return pltpu.make_async_copy(u_ref.at[:, at], u_hbm.at[:, at], sems.at[h])

        visible = visible_of(start_ref, (key_count, m), row_count, key_total)
        extra = q_ref[:, pl.ds(here, LANES)]
        slot = lax.broadcasted_iota(jnp.int32, (slots, LANES), 0)
        lane = lax.broadcasted_iota(jnp.int32, (slots, LANES), 1)
        pick = (lane % heads == slot) & (lane < 3 * heads)
        delta = nt(jnp.where(pick, 1.0, 0.0).astype(BF), extra)
        tops = l_ref[0]
        sent = jnp.zeros((m, LANES), F32)
        for i in range(2):
            for part, value in enumerate(split3(l_ref[i])):
                at = (3 * i + part) * heads
                place = (lane == at + slot) & (slot < heads)
                sent += tn(value, jnp.where(place, 1.0, 0.0).astype(BF))
        u_ref[:, pl.ds(here, LANES)] = sent.astype(BF)
        copy_of(heads, LANES).start()
        for h in range(heads):
            at = head_of(h)
            k = k_ref[:, at]
            s = nt(k, q_ref[:, at]) * scaling
            prob = jnp.where(visible, jnp.exp(s - tops[h : h + 1, :]), 0.0)
            ds = prob * (nt(v_ref[:, at], g_ref[:, at]) - delta[h : h + 1, :]) * scaling
            ds = ds.astype(BF)
            u_ref[:, at] = tn(ds, k).astype(BF)
            copy_of(h, HEAD_DIM).start()
            p_ref[h] = prob.astype(BF)
            ds_ref[h] = ds
        for h in range(heads):
            copy_of(h, HEAD_DIM).wait()
        copy_of(heads, LANES).wait()

    return pl.pallas_call(
        body,
        in_specs=in_vmem(6),
        out_specs=[pl.BlockSpec(memory_space=pl.ANY), *in_vmem(2)],
        out_shape=[
            jax.ShapeDtypeStruct((m, here + LANES), BF),
            held((heads, key_count, m), BF),
            held((heads, key_count, m), BF),
        ],
        scratch_shapes=[
            pltpu.VMEM((m, here + LANES), BF),
            pltpu.SemaphoreType.DMA((heads + 1,)),
        ],
        name="query_gradients",
    )(vmem(start), vmem(queries), vmem(grads), vmem(keys), vmem(values), vmem(stats))


def cache_kernel(queries, grads, probs, score_grads, own, merged):
    here = grads.shape[1]
    heads, key_count, _ = probs.shape

    def body(q_ref, g_ref, p_ref, ds_ref, own_ref, all_ref, dk_ref, dv_ref):
        share = jnp.exp(own_ref[0] - all_ref[0]) / all_ref[1]
        for h in range(heads):
            at = head_of(h)
            row = share[h : h + 1, :]
            ds = (ds_ref[h].astype(F32) * row).astype(BF)
            prob = (p_ref[h].astype(F32) * row).astype(BF)
            dk_ref[:, at] = nn(ds, q_ref[:, at]).astype(BF)
            dv_ref[:, at] = nn(prob, g_ref[:, at]).astype(BF)

    return pl.pallas_call(
        body,
        in_specs=in_vmem(6),
        out_specs=in_vmem(2),
        out_shape=[jax.ShapeDtypeStruct((key_count, here), BF)] * 2,
        name="cache_gradients",
    )(vmem(queries), vmem(grads), vmem(probs), vmem(score_grads), vmem(own), vmem(merged))


def combine_kernel(parts):
    sections, holders, rows, width = parts.shape
    here = width - LANES
    heads = here // HEAD_DIM

    def body(p_ref, out_ref):
        def stats_of(s, c):
            e = p_ref[s, c, :, pl.ds(here, LANES)].astype(F32)
            e += pltpu.roll(e, LANES - heads, 1) + pltpu.roll(e, LANES - 2 * heads, 1)
            return e, pltpu.roll(e, LANES - 3 * heads, 1)

        for s in range(sections):
            top = jnp.full((rows, LANES), -jnp.inf, F32)
            for c in range(holders):
                top = jnp.maximum(top, stats_of(s, c)[0])
            total = jnp.zeros((rows, LANES), F32)
            for c in range(holders):
                own, count = stats_of(s, c)
                total += jnp.exp(own - top) * count
            sums = [jnp.zeros((rows, HEAD_DIM), F32) for _ in range(heads)]
            for c in range(holders):
                share = jnp.exp(stats_of(s, c)[0] - top) / total
                for h in range(heads):
                    value = p_ref[s, c, :, head_of(h)].astype(F32)
                    sums[h] += share[:, h : h + 1] * value
            for h in range(heads):
                out_ref[:, head_of(s * heads + h)] = sums[h].astype(BF)

    return pl.pallas_call(
        body,
        in_specs=in_vmem(1),
        out_specs=in_vmem(1)[0],
        out_shape=jax.ShapeDtypeStruct((rows, sections * here), BF),
        name="combine",
    )(vmem(parts))


def merge_stats(stats, axis, order):
    for bit in order:
        other = flip(stats, axis, 1 << bit)
        top = jnp.maximum(stats[0], other[0])
        total = stats[1] * jnp.exp(stats[0] - top) + other[1] * jnp.exp(other[0] - top)
        stats = jnp.stack([top, total])
    return stats


def flip(value, axis, bit):
    count = lax.axis_size(axis)
    return lax.ppermute(value, axis, [(i, i ^ bit) for i in range(count)])


def ordered(mine, other, upper, axis):
    first = jnp.where(upper, other, mine)
    second = jnp.where(upper, mine, other)
    return jnp.stack([first, second], axis)


def swap_blocks(blocks, axis):
    count = lax.axis_size(axis)
    here = lax.axis_index(axis)
    got = [blocks[0]]
    for step in range(1, count):
        got.append(flip(blocks[step], axis, step))
    bit = 1
    while bit < count:
        upper = here & bit != 0
        got = [jnp.where(upper, got[i ^ bit], got[i]) for i in range(count)]
        bit *= 2
    return jnp.stack(got)


def spread_blocks(blocks, axis, order):
    count = lax.axis_size(axis)
    lead, rest = blocks.shape[0], blocks.shape[1:]
    done = []
    for bit in order:
        upper = lax.axis_index(axis) & (1 << bit) != 0
        other = flip(blocks, axis, 1 << bit)
        blocks = ordered(blocks, other, upper, 1 + sum(b > bit for b in done))
        done.append(bit)
    return blocks.reshape((lead, count) + rest)


def exchange(blocks):
    return lax.all_to_all(blocks, ("section", "ctx"), 0, 0, tiled=True)


def compute(block_order, queries, cache_keys, cache_values, attention_out, output_grad):
    sections = lax.axis_size("section")
    ctx_count = lax.axis_size("ctx")
    assert ctx_count & (ctx_count - 1) == 0
    assert sections & (sections - 1) == 0 and sections > 1
    layers, rows, _ = queries.shape
    assert layers == 1
    key_count, here = cache_keys.shape
    row_count = rows * ctx_count
    key_total = key_count * ctx_count
    peers = sections * ctx_count

    ctx_bits = ctx_count.bit_length() - 1
    down = list(range(ctx_bits))[::-1]

    packed = pack(
        block_order,
        cache_keys,
        cache_values,
        queries[0],
        output_grad[0],
        attention_out[0],
        sections,
    )
    start, keys, values = packed[sections:]
    swapped = swap_blocks(packed[:sections], "section")
    query_all, grad_all = swapped[..., : here + LANES], swapped[..., here + LANES :]
    query_all = spread_blocks(query_all, "ctx", down)
    query_all = query_all.reshape(peers * rows, here + LANES)
    grad_all = spread_blocks(grad_all, "ctx", down[:1] + down[1:][::-1])
    grad_all = grad_all.reshape(peers * rows, here)

    own = stats_kernel(start, query_all, keys, row_count, key_total)
    merged = merge_stats(own, "ctx", down[-1:] + down[:-1])
    part, probs, score_grads = query_kernel(
        start, query_all, grad_all, keys, values, own, row_count, key_total
    )
    part = exchange(part.reshape(peers, rows, here + LANES))
    grad_keys, grad_values = cache_kernel(query_all, grad_all, probs, score_grads, own, merged)
    grad_queries = combine_kernel(part.reshape(sections, ctx_count, rows, here + LANES))
    return (grad_queries[None], grad_keys, grad_values)


def solution(mesh):
    in_specs = (
        P(),
        P("section", "ctx", None),
        P("ctx", "section"),
        P("ctx", "section"),
        P("section", "ctx", None),
        P("section", "ctx", None),
    )
    out_specs = (P("section", "ctx", None), P("ctx", "section"), P("ctx", "section"))
    return jax.shard_map(compute, mesh=mesh, in_specs=in_specs, out_specs=out_specs, check_vma=False)
```

```python
import math

import jax
import jax.numpy as jnp
from jax import lax
from jax.experimental import pallas as pl
from jax.experimental.pallas import tpu as pltpu
from jax.sharding import PartitionSpec as P


HEAD_DIM = 128
LANES = 128
ON_CHIP_BYTES = 1 << 20
masked_score = -1e30
BF = jnp.bfloat16
F32 = jnp.float32


def nt(a, b):
    return lax.dot_general(a, b, (((1,), (1,)), ((), ())), preferred_element_type=F32)


def nn(a, b):
    return lax.dot_general(a, b, (((1,), (0,)), ((), ())), preferred_element_type=F32)


def tn(a, b):
    return lax.dot_general(a, b, (((0,), (0,)), ((), ())), preferred_element_type=F32)


def split3(x):
    hi = x.astype(BF)
    rest = x - hi.astype(F32)
    mid = rest.astype(BF)
    low = (rest - mid.astype(F32)).astype(BF)
    return hi, mid, low


def in_vmem(count):
    return [pl.BlockSpec(memory_space=pltpu.VMEM) for _ in range(count)]


def small(shape, dtype):
    return math.prod(shape) * jnp.dtype(dtype).itemsize <= ON_CHIP_BYTES


def vmem(value):
    if small(value.shape, value.dtype):
        return pltpu.with_memory_space_constraint(value, pltpu.VMEM)
    return value


def held(shape, dtype):
    if small(shape, dtype):
        return pltpu.VMEM(shape, dtype)
    return jax.ShapeDtypeStruct(shape, dtype)


def head_of(h):
    return pl.ds(h * HEAD_DIM, HEAD_DIM)


def pack(block_order, keys, values, queries, grads, outs, sections):
    rows, features = grads.shape
    here = features // sections
    heads = here // HEAD_DIM
    key_count = keys.shape[0]

    def body(order_hbm, k_hbm, v_hbm, q_hbm, g_hbm, o_hbm, *refs):
        blocks = refs[:sections]
        start_ref, k_ref, v_ref, q_ref, g_ref, o_ref, order_ref, sems = refs[sections:]
        pairs = [
            (q_hbm, q_ref),
            (g_hbm, g_ref),
            (o_hbm, o_ref),
            (order_hbm, order_ref),
            (k_hbm, k_ref),
            (v_hbm, v_ref),
        ]
        copies = [pltpu.make_async_copy(*pair, sems.at[i]) for i, pair in enumerate(pairs)]
        for copy in copies:
            copy.start()
        section = lax.axis_index("section")
        lane = lax.broadcasted_iota(jnp.int32, (rows, LANES), 1)

        def at(s, h):
            return pl.ds(pl.multiple_of(s * here + h * HEAD_DIM, HEAD_DIM), HEAD_DIM)

        for i in range(3):
            copies[i].wait()
        for step, out_ref in enumerate(blocks):
            to = section ^ step
            extra = jnp.zeros((rows, LANES), F32)
            for h in range(heads):
                g = g_ref[:, at(to, h)]
                terms = g.astype(F32) * o_ref[:, at(to, h)].astype(F32)
                delta = jnp.sum(terms, axis=1, keepdims=True)
                for part, value in enumerate(split3(delta)):
                    extra = jnp.where(lane == part * heads + h, value.astype(F32), extra)
                out_ref[:, head_of(h)] = q_ref[:, at(to, h)]
                out_ref[:, head_of(heads + 1 + h)] = g
            out_ref[:, head_of(heads)] = extra.astype(BF)
        copies[3].wait()
        block = order_ref[lax.axis_index("ctx")]
        start_ref[...] = jnp.full(start_ref.shape, block * key_count, jnp.int32)
        copies[4].wait()
        copies[5].wait()

    return pl.pallas_call(
        body,
        in_specs=[pl.BlockSpec(memory_space=pl.ANY)] * 6,
        out_specs=in_vmem(sections + 3),
        out_shape=[
            *[held((rows, 2 * here + LANES), BF)] * sections,
            held((8, LANES), jnp.int32),
            held(keys.shape, BF),
            held(values.shape, BF),
        ],
        scratch_shapes=[
            pltpu.VMEM((rows, features), BF),
            pltpu.VMEM((rows, features), BF),
            pltpu.VMEM((rows, features), BF),
            pltpu.SMEM(block_order.shape, jnp.int32),
            pltpu.SemaphoreType.DMA((6,)),
        ],
        name="pack",
    )(block_order, keys, values, queries, grads, outs)


def visible_of(start_ref, shape, row_count, key_total):
    key_pos = start_ref[0:1, 0:1] + lax.broadcasted_iota(jnp.int32, shape, 0)
    row = lax.broadcasted_iota(jnp.int32, shape, 1) % row_count
    return key_pos <= key_total - row_count + row


def stats_kernel(start, queries, keys, row_count, key_total):
    m = queries.shape[0]
    key_count, here = keys.shape
    heads = here // HEAD_DIM
    slots = -(-heads // 8) * 8
    scaling = HEAD_DIM ** (-0.5)

    def body(start_ref, q_ref, k_ref, out_ref, prob_ref, delta_ref, sent_ref):
        visible = visible_of(start_ref, (key_count, m), row_count, key_total)
        out_ref[...] = jnp.ones_like(out_ref)
        for h in range(heads):
            at = head_of(h)
            s = jnp.where(visible, nt(k_ref[:, at], q_ref[:, at]) * scaling, masked_score)
            top = jnp.max(s, axis=0, keepdims=True)
            prob = jnp.where(visible, jnp.exp(s - top), 0.0)
            prob_ref[h] = prob
            out_ref[0, pl.ds(h, 1), :] = top
            out_ref[1, pl.ds(h, 1), :] = jnp.sum(prob, axis=0, keepdims=True)
        slot = lax.broadcasted_iota(jnp.int32, (slots, LANES), 0)
        lane = lax.broadcasted_iota(jnp.int32, (slots, LANES), 1)
        pick = (lane % heads == slot) & (lane < 3 * heads)
        delta_ref[...] = nt(jnp.where(pick, 1.0, 0.0).astype(BF), q_ref[:, pl.ds(here, LANES)])
        sent = jnp.zeros((m, LANES), F32)
        for i in range(2):
            for part, value in enumerate(split3(out_ref[i])):
                at = (3 * i + part) * heads
                place = (lane == at + slot) & (slot < heads)
                sent += tn(value, jnp.where(place, 1.0, 0.0).astype(BF))
        sent_ref[...] = sent.astype(BF)

    return pl.pallas_call(
        body,
        in_specs=in_vmem(3),
        out_specs=in_vmem(4),
        out_shape=[
            held((2, slots, m), F32),
            held((heads, key_count, m), F32),
            held((slots, m), F32),
            held((m, LANES), BF),
        ],
        name="stats",
    )(vmem(start), vmem(queries), vmem(keys))


def query_kernel(grads, keys, values, probs, deltas, sent):
    m = grads.shape[0]
    key_count, here = keys.shape
    heads = here // HEAD_DIM
    scaling = HEAD_DIM ** (-0.5)

    def body(g_ref, k_ref, v_ref, p_ref, d_ref, sent_ref, u_hbm, ds_ref, u_ref, sems):
        def copy_of(h):
            return pltpu.make_async_copy(
                u_ref.at[:, head_of(h)], u_hbm.at[:, head_of(h)], sems.at[h]
            )

        last = pltpu.make_async_copy(sent_ref, u_hbm.at[:, head_of(heads)], sems.at[heads])
        last.start()
        for h in range(heads):
            at = head_of(h)
            ds = p_ref[h] * (nt(v_ref[:, at], g_ref[:, at]) - d_ref[h : h + 1, :]) * scaling
            ds = ds.astype(BF)
            u_ref[:, at] = tn(ds, k_ref[:, at]).astype(BF)
            copy_of(h).start()
            ds_ref[h] = ds
        for h in range(heads):
            copy_of(h).wait()
        last.wait()

    return pl.pallas_call(
        body,
        in_specs=in_vmem(6),
        out_specs=[pl.BlockSpec(memory_space=pl.ANY), in_vmem(1)[0]],
        out_shape=[
            jax.ShapeDtypeStruct((m, here + LANES), BF),
            held((heads, key_count, m), BF),
        ],
        scratch_shapes=[
            pltpu.VMEM((m, here), BF),
            pltpu.SemaphoreType.DMA((heads + 1,)),
        ],
        name="query_gradients",
    )(vmem(grads), vmem(keys), vmem(values), vmem(probs), vmem(deltas), vmem(sent))


def cache_kernel(queries, grads, probs, score_grads, own, merged):
    here = grads.shape[1]
    heads, key_count, _ = probs.shape

    def body(q_ref, g_ref, p_ref, ds_ref, own_ref, all_ref, dk_ref, dv_ref):
        share = jnp.exp(own_ref[0] - all_ref[0]) / all_ref[1]
        for h in range(heads):
            at = head_of(h)
            row = share[h : h + 1, :]
            ds = (ds_ref[h].astype(F32) * row).astype(BF)
            prob = (p_ref[h] * row).astype(BF)
            dk_ref[:, at] = nn(ds, q_ref[:, at]).astype(BF)
            dv_ref[:, at] = nn(prob, g_ref[:, at]).astype(BF)

    return pl.pallas_call(
        body,
        in_specs=in_vmem(6),
        out_specs=in_vmem(2),
        out_shape=[jax.ShapeDtypeStruct((key_count, here), BF)] * 2,
        name="cache_gradients",
    )(vmem(queries), vmem(grads), vmem(probs), vmem(score_grads), vmem(own), vmem(merged))


def combine_kernel(parts):
    sections, holders, rows, width = parts.shape
    here = width - LANES
    heads = here // HEAD_DIM

    def body(p_ref, out_ref):
        def stats_of(s, c):
            e = p_ref[s, c, :, pl.ds(here, LANES)].astype(F32)
            e += pltpu.roll(e, LANES - heads, 1) + pltpu.roll(e, LANES - 2 * heads, 1)
            return e, pltpu.roll(e, LANES - 3 * heads, 1)

        for s in range(sections):
            top = jnp.full((rows, LANES), -jnp.inf, F32)
            for c in range(holders):
                top = jnp.maximum(top, stats_of(s, c)[0])
            total = jnp.zeros((rows, LANES), F32)
            for c in range(holders):
                own, count = stats_of(s, c)
                total += jnp.exp(own - top) * count
            sums = [jnp.zeros((rows, HEAD_DIM), F32) for _ in range(heads)]
            for c in range(holders):
                share = jnp.exp(stats_of(s, c)[0] - top) / total
                for h in range(heads):
                    value = p_ref[s, c, :, head_of(h)].astype(F32)
                    sums[h] += share[:, h : h + 1] * value
            for h in range(heads):
                out_ref[:, head_of(s * heads + h)] = sums[h].astype(BF)

    return pl.pallas_call(
        body,
        in_specs=in_vmem(1),
        out_specs=in_vmem(1)[0],
        out_shape=jax.ShapeDtypeStruct((rows, sections * here), BF),
        name="combine",
    )(vmem(parts))


def merge_stats(stats, axis, order):
    for bit in order:
        other = flip(stats, axis, 1 << bit)
        top = jnp.maximum(stats[0], other[0])
        total = stats[1] * jnp.exp(stats[0] - top) + other[1] * jnp.exp(other[0] - top)
        stats = jnp.stack([top, total])
    return stats


def flip(value, axis, bit):
    count = lax.axis_size(axis)
    return lax.ppermute(value, axis, [(i, i ^ bit) for i in range(count)])


def ordered(mine, other, upper, axis):
    first = jnp.where(upper, other, mine)
    second = jnp.where(upper, mine, other)
    return jnp.stack([first, second], axis)


def swap_blocks(blocks, axis):
    count = lax.axis_size(axis)
    here = lax.axis_index(axis)
    got = [blocks[0]]
    for step in range(1, count):
        got.append(flip(blocks[step], axis, step))
    bit = 1
    while bit < count:
        upper = here & bit != 0
        got = [jnp.where(upper, got[i ^ bit], got[i]) for i in range(count)]
        bit *= 2
    return jnp.stack(got)


def spread_blocks(blocks, axis, order):
    count = lax.axis_size(axis)
    lead, rest = blocks.shape[0], blocks.shape[1:]
    done = []
    for bit in order:
        upper = lax.axis_index(axis) & (1 << bit) != 0
        other = flip(blocks, axis, 1 << bit)
        blocks = ordered(blocks, other, upper, 1 + sum(b > bit for b in done))
        done.append(bit)
    return blocks.reshape((lead, count) + rest)


def exchange(blocks):
    return lax.all_to_all(blocks, ("section", "ctx"), 0, 0, tiled=True)


def compute(block_order, queries, cache_keys, cache_values, attention_out, output_grad):
    sections = lax.axis_size("section")
    ctx_count = lax.axis_size("ctx")
    assert ctx_count & (ctx_count - 1) == 0
    assert sections & (sections - 1) == 0 and sections > 1
    layers, rows, _ = queries.shape
    assert layers == 1
    key_count, here = cache_keys.shape
    row_count = rows * ctx_count
    key_total = key_count * ctx_count
    peers = sections * ctx_count

    ctx_bits = ctx_count.bit_length() - 1
    down = list(range(ctx_bits))[::-1]

    packed = pack(
        block_order,
        cache_keys,
        cache_values,
        queries[0],
        output_grad[0],
        attention_out[0],
        sections,
    )
    start, keys, values = packed[sections:]
    swapped = swap_blocks(packed[:sections], "section")
    query_all, grad_all = swapped[..., : here + LANES], swapped[..., here + LANES :]
    query_all = spread_blocks(query_all, "ctx", down)
    query_all = query_all.reshape(peers * rows, here + LANES)
    grad_all = spread_blocks(grad_all, "ctx", down[:1] + down[1:][::-1])
    grad_all = grad_all.reshape(peers * rows, here)

    own, probs, deltas, row_stats = stats_kernel(start, query_all, keys, row_count, key_total)
    merged = merge_stats(own, "ctx", down[-1:] + down[:-1])
    part, score_grads = query_kernel(grad_all, keys, values, probs, deltas, row_stats)
    part = exchange(part.reshape(peers, rows, here + LANES))
    grad_keys, grad_values = cache_kernel(query_all, grad_all, probs, score_grads, own, merged)
    grad_queries = combine_kernel(part.reshape(sections, ctx_count, rows, here + LANES))
    return (grad_queries[None], grad_keys, grad_values)


def solution(mesh):
    in_specs = (
        P(),
        P("section", "ctx", None),
        P("ctx", "section"),
        P("ctx", "section"),
        P("section", "ctx", None),
        P("section", "ctx", None),
    )
    out_specs = (P("section", "ctx", None), P("ctx", "section"), P("ctx", "section"))
    return jax.shard_map(compute, mesh=mesh, in_specs=in_specs, out_specs=out_specs, check_vma=False)
```

```python
import math

import jax
import jax.numpy as jnp
from jax import lax
from jax.experimental import pallas as pl
from jax.experimental.pallas import tpu as pltpu
from jax.sharding import PartitionSpec as P


HEAD_DIM = 128
LANES = 128
ON_CHIP_BYTES = 1 << 20
masked_score = -1e30
BF = jnp.bfloat16
F32 = jnp.float32


def nt(a, b):
    return lax.dot_general(a, b, (((1,), (1,)), ((), ())), preferred_element_type=F32)


def nn(a, b):
    return lax.dot_general(a, b, (((1,), (0,)), ((), ())), preferred_element_type=F32)


def tn(a, b):
    return lax.dot_general(a, b, (((0,), (0,)), ((), ())), preferred_element_type=F32)


def split3(x):
    hi = x.astype(BF)
    rest = x - hi.astype(F32)
    mid = rest.astype(BF)
    low = (rest - mid.astype(F32)).astype(BF)
    return hi, mid, low


def in_vmem(count):
    return [pl.BlockSpec(memory_space=pltpu.VMEM) for _ in range(count)]


def small(shape, dtype):
    return math.prod(shape) * jnp.dtype(dtype).itemsize <= ON_CHIP_BYTES


def vmem(value):
    if small(value.shape, value.dtype):
        return pltpu.with_memory_space_constraint(value, pltpu.VMEM)
    return value


def held(shape, dtype):
    if small(shape, dtype):
        return pltpu.VMEM(shape, dtype)
    return jax.ShapeDtypeStruct(shape, dtype)


def head_of(h):
    return pl.ds(h * HEAD_DIM, HEAD_DIM)


def pack(block_order, keys, values, queries, grads, outs, sections):
    rows, features = grads.shape
    here = features // sections
    heads = here // HEAD_DIM
    key_count = keys.shape[0]

    def body(order_hbm, k_hbm, v_hbm, q_hbm, g_hbm, o_hbm, *refs):
        blocks = refs[:sections]
        start_ref, k_ref, v_ref, q_ref, g_ref, o_ref, order_ref, sems = refs[sections:]
        pairs = [
            (q_hbm, q_ref),
            (g_hbm, g_ref),
            (o_hbm, o_ref),
            (order_hbm, order_ref),
            (k_hbm, k_ref),
            (v_hbm, v_ref),
        ]
        copies = [pltpu.make_async_copy(*pair, sems.at[i]) for i, pair in enumerate(pairs)]
        for copy in copies:
            copy.start()
        section = lax.axis_index("section")
        lane = lax.broadcasted_iota(jnp.int32, (rows, LANES), 1)

        def at(s, h):
            return pl.ds(pl.multiple_of(s * here + h * HEAD_DIM, HEAD_DIM), HEAD_DIM)

        for i in range(3):
            copies[i].wait()
        for step, out_ref in enumerate(blocks):
            to = section ^ step
            extra = jnp.zeros((rows, LANES), F32)
            for h in range(heads):
                g = g_ref[:, at(to, h)]
                terms = g.astype(F32) * o_ref[:, at(to, h)].astype(F32)
                delta = jnp.sum(terms, axis=1, keepdims=True)
                for part, value in enumerate(split3(delta)):
                    extra = jnp.where(lane == part * heads + h, value.astype(F32), extra)
                out_ref[:, head_of(h)] = q_ref[:, at(to, h)]
                out_ref[:, head_of(heads + 1 + h)] = g
            out_ref[:, head_of(heads)] = extra.astype(BF)
        copies[3].wait()
        block = order_ref[lax.axis_index("ctx")]
        start_ref[...] = jnp.full(start_ref.shape, block * key_count, jnp.int32)
        copies[4].wait()
        copies[5].wait()

    return pl.pallas_call(
        body,
        in_specs=[pl.BlockSpec(memory_space=pl.ANY)] * 6,
        out_specs=in_vmem(sections + 3),
        out_shape=[
            *[held((rows, 2 * here + LANES), BF)] * sections,
            held((8, LANES), jnp.int32),
            held(keys.shape, BF),
            held(values.shape, BF),
        ],
        scratch_shapes=[
            pltpu.VMEM((rows, features), BF),
            pltpu.VMEM((rows, features), BF),
            pltpu.VMEM((rows, features), BF),
            pltpu.SMEM(block_order.shape, jnp.int32),
            pltpu.SemaphoreType.DMA((6,)),
        ],
        name="pack",
    )(block_order, keys, values, queries, grads, outs)


def visible_of(start_ref, shape, row_count, key_total):
    key_pos = start_ref[0:1, 0:1] + lax.broadcasted_iota(jnp.int32, shape, 0)
    row = lax.broadcasted_iota(jnp.int32, shape, 1) % row_count
    return key_pos <= key_total - row_count + row


def stats_kernel(start, queries, keys, row_count, key_total):
    m = queries.shape[0]
    key_count, here = keys.shape
    heads = here // HEAD_DIM
    slots = -(-heads // 8) * 8
    scaling = HEAD_DIM ** (-0.5)

    def body(start_ref, q_ref, k_ref, out_ref, prob_ref, delta_ref, sent_ref):
        visible = visible_of(start_ref, (key_count, m), row_count, key_total)
        out_ref[...] = jnp.ones_like(out_ref)
        for h in range(heads):
            at = head_of(h)
            s = jnp.where(visible, nt(k_ref[:, at], q_ref[:, at]) * scaling, masked_score)
            top = jnp.max(s, axis=0, keepdims=True)
            prob = jnp.where(visible, jnp.exp(s - top), 0.0)
            prob_ref[h] = prob
            out_ref[0, pl.ds(h, 1), :] = top
            out_ref[1, pl.ds(h, 1), :] = jnp.sum(prob, axis=0, keepdims=True)
        slot = lax.broadcasted_iota(jnp.int32, (slots, LANES), 0)
        lane = lax.broadcasted_iota(jnp.int32, (slots, LANES), 1)
        pick = (lane % heads == slot) & (lane < 3 * heads)
        delta_ref[...] = nt(jnp.where(pick, 1.0, 0.0).astype(BF), q_ref[:, pl.ds(here, LANES)])
        sent = jnp.zeros((m, LANES), F32)
        for i in range(2):
            for part, value in enumerate(split3(out_ref[i])):
                at = (3 * i + part) * heads
                place = (lane == at + slot) & (slot < heads)
                sent += tn(value, jnp.where(place, 1.0, 0.0).astype(BF))
        sent_ref[...] = sent.astype(BF)

    return pl.pallas_call(
        body,
        in_specs=in_vmem(3),
        out_specs=in_vmem(4),
        out_shape=[
            held((2, slots, m), F32),
            held((heads, key_count, m), F32),
            held((slots, m), F32),
            held((m, LANES), BF),
        ],
        name="stats",
    )(vmem(start), vmem(queries), vmem(keys))


def query_kernel(grads, keys, values, probs, deltas, sent):
    m = grads.shape[0]
    key_count, here = keys.shape
    heads = here // HEAD_DIM
    scaling = HEAD_DIM ** (-0.5)

    def body(g_ref, k_ref, v_ref, p_ref, d_ref, sent_ref, u_hbm, ds_ref, u_ref, sems):
        def copy_of(h):
            return pltpu.make_async_copy(
                u_ref.at[:, head_of(h)], u_hbm.at[:, head_of(h)], sems.at[h]
            )

        last = pltpu.make_async_copy(sent_ref, u_hbm.at[:, head_of(heads)], sems.at[heads])
        last.start()
        for h in range(heads):
            at = head_of(h)
            ds = p_ref[h] * (nt(v_ref[:, at], g_ref[:, at]) - d_ref[h : h + 1, :]) * scaling
            ds = ds.astype(BF)
            u_ref[:, at] = tn(ds, k_ref[:, at]).astype(BF)
            copy_of(h).start()
            ds_ref[h] = ds
        for h in range(heads):
            copy_of(h).wait()
        last.wait()

    return pl.pallas_call(
        body,
        in_specs=in_vmem(6),
        out_specs=[pl.BlockSpec(memory_space=pl.ANY), in_vmem(1)[0]],
        out_shape=[
            jax.ShapeDtypeStruct((m, here + LANES), BF),
            held((heads, key_count, m), BF),
        ],
        scratch_shapes=[
            pltpu.VMEM((m, here), BF),
            pltpu.SemaphoreType.DMA((heads + 1,)),
        ],
        name="query_gradients",
    )(vmem(grads), vmem(keys), vmem(values), vmem(probs), vmem(deltas), vmem(sent))


def cache_kernel(queries, grads, probs, score_grads, own, merged):
    here = grads.shape[1]
    heads, key_count, _ = probs.shape

    def body(q_ref, g_ref, p_ref, ds_ref, own_ref, all_ref, dk_ref, dv_ref):
        share = jnp.exp(own_ref[0] - all_ref[0]) / all_ref[1]
        for h in range(heads):
            at = head_of(h)
            row = share[h : h + 1, :]
            ds = (ds_ref[h].astype(F32) * row).astype(BF)
            prob = (p_ref[h] * row).astype(BF)
            dk_ref[:, at] = nn(ds, q_ref[:, at]).astype(BF)
            dv_ref[:, at] = nn(prob, g_ref[:, at]).astype(BF)

    return pl.pallas_call(
        body,
        in_specs=in_vmem(6),
        out_specs=in_vmem(2),
        out_shape=[jax.ShapeDtypeStruct((key_count, here), BF)] * 2,
        name="cache_gradients",
    )(vmem(queries), vmem(grads), vmem(probs), vmem(score_grads), vmem(own), vmem(merged))


def combine_kernel(parts):
    sections, holders, rows, width = parts.shape
    here = width - LANES
    heads = here // HEAD_DIM

    def body(p_ref, out_ref):
        def stats_of(s, c):
            e = p_ref[s, c, :, pl.ds(here, LANES)].astype(F32)
            e += pltpu.roll(e, LANES - heads, 1) + pltpu.roll(e, LANES - 2 * heads, 1)
            return e, pltpu.roll(e, LANES - 3 * heads, 1)

        for s in range(sections):
            top = jnp.full((rows, LANES), -jnp.inf, F32)
            for c in range(holders):
                top = jnp.maximum(top, stats_of(s, c)[0])
            total = jnp.zeros((rows, LANES), F32)
            for c in range(holders):
                own, count = stats_of(s, c)
                total += jnp.exp(own - top) * count
            sums = [jnp.zeros((rows, HEAD_DIM), F32) for _ in range(heads)]
            for c in range(holders):
                share = jnp.exp(stats_of(s, c)[0] - top) / total
                for h in range(heads):
                    value = p_ref[s, c, :, head_of(h)].astype(F32)
                    sums[h] += share[:, h : h + 1] * value
            for h in range(heads):
                out_ref[:, head_of(s * heads + h)] = sums[h].astype(BF)

    return pl.pallas_call(
        body,
        in_specs=in_vmem(1),
        out_specs=in_vmem(1)[0],
        out_shape=jax.ShapeDtypeStruct((rows, sections * here), BF),
        name="combine",
    )(vmem(parts))


def merge_stats(stats, axis, order):
    for bit in order:
        other = flip(stats, axis, 1 << bit)
        top = jnp.maximum(stats[0], other[0])
        total = stats[1] * jnp.exp(stats[0] - top) + other[1] * jnp.exp(other[0] - top)
        stats = jnp.stack([top, total])
    return stats


def flip(value, axis, bit):
    count = lax.axis_size(axis)
    return lax.ppermute(value, axis, [(i, i ^ bit) for i in range(count)])


def ordered(mine, other, upper, axis):
    first = jnp.where(upper, other, mine)
    second = jnp.where(upper, mine, other)
    return jnp.stack([first, second], axis)


def swap_blocks(blocks, axis):
    count = lax.axis_size(axis)
    here = lax.axis_index(axis)
    got = [blocks[0]]
    for step in range(1, count):
        got.append(flip(blocks[step], axis, step))
    bit = 1
    while bit < count:
        upper = here & bit != 0
        got = [jnp.where(upper, got[i ^ bit], got[i]) for i in range(count)]
        bit *= 2
    return jnp.stack(got)


def flip_by_parity(value, bits):
    sections, count = lax.axis_size("section"), lax.axis_size("ctx")
    pairs = []
    for section in range(sections):
        for at in range(count):
            to = at ^ (1 << bits[section % 2])
            pairs.append((section * count + at, section * count + to))
    return lax.ppermute(value, ("section", "ctx"), pairs)


def spread_blocks(blocks, first_bits, last_bits):
    count = lax.axis_size("ctx")
    at = lax.axis_index("ctx")
    odd = lax.axis_index("section") % 2 == 1
    lead, rest = blocks.shape[0], blocks.shape[1:]
    pairs = [(bit, bit) for bit in first_bits] + [last_bits, last_bits[::-1]]
    for i, (even_bit, odd_bit) in enumerate(pairs):
        upper = at >> jnp.where(odd, odd_bit, even_bit) & 1 == 1
        other = flip_by_parity(blocks, (even_bit, odd_bit))
        blocks = ordered(blocks, other, upper, 1 + i)
    turned = odd if last_bits[0] > last_bits[1] else ~odd
    blocks = jnp.where(turned, jnp.swapaxes(blocks, i, i + 1), blocks)
    return blocks.reshape((lead, count) + rest)


def exchange(blocks):
    return lax.all_to_all(blocks, ("section", "ctx"), 0, 0, tiled=True)


def compute(block_order, queries, cache_keys, cache_values, attention_out, output_grad):
    sections = lax.axis_size("section")
    ctx_count = lax.axis_size("ctx")
    assert ctx_count & (ctx_count - 1) == 0 and ctx_count > 2
    assert sections & (sections - 1) == 0 and sections > 1
    layers, rows, _ = queries.shape
    assert layers == 1
    key_count, here = cache_keys.shape
    row_count = rows * ctx_count
    key_total = key_count * ctx_count
    peers = sections * ctx_count

    ctx_bits = ctx_count.bit_length() - 1
    down = list(range(ctx_bits))[::-1]

    packed = pack(
        block_order,
        cache_keys,
        cache_values,
        queries[0],
        output_grad[0],
        attention_out[0],
        sections,
    )
    start, keys, values = packed[sections:]
    swapped = swap_blocks(packed[:sections], "section")
    query_all, grad_all = swapped[..., : here + LANES], swapped[..., here + LANES :]
    last = (down[-2], down[-1])
    query_all = spread_blocks(query_all, down[:-2], last)
    query_all = query_all.reshape(peers * rows, here + LANES)
    grad_all = spread_blocks(grad_all, down[:-2], last[::-1])
    grad_all = grad_all.reshape(peers * rows, here)

    own, probs, deltas, row_stats = stats_kernel(start, query_all, keys, row_count, key_total)
    merged = merge_stats(own, "ctx", down[-1:] + down[:-1])
    part, score_grads = query_kernel(grad_all, keys, values, probs, deltas, row_stats)
    part = exchange(part.reshape(peers, rows, here + LANES))
    grad_keys, grad_values = cache_kernel(query_all, grad_all, probs, score_grads, own, merged)
    grad_queries = combine_kernel(part.reshape(sections, ctx_count, rows, here + LANES))
    return (grad_queries[None], grad_keys, grad_values)


def solution(mesh):
    in_specs = (
        P(),
        P("section", "ctx", None),
        P("ctx", "section"),
        P("ctx", "section"),
        P("section", "ctx", None),
        P("section", "ctx", None),
    )
    out_specs = (P("section", "ctx", None), P("ctx", "section"), P("ctx", "section"))
    return jax.shard_map(compute, mesh=mesh, in_specs=in_specs, out_specs=out_specs, check_vma=False)
```

```python
import math

import jax
import jax.numpy as jnp
from jax import lax
from jax.experimental import pallas as pl
from jax.experimental.pallas import tpu as pltpu
from jax.sharding import PartitionSpec as P


HEAD_DIM = 128
LANES = 128
ON_CHIP_BYTES = 1 << 20
masked_score = -1e30
BF = jnp.bfloat16
F32 = jnp.float32


def nt(a, b):
    return lax.dot_general(a, b, (((1,), (1,)), ((), ())), preferred_element_type=F32)


def nn(a, b):
    return lax.dot_general(a, b, (((1,), (0,)), ((), ())), preferred_element_type=F32)


def tn(a, b):
    return lax.dot_general(a, b, (((0,), (0,)), ((), ())), preferred_element_type=F32)


def split3(x):
    hi = x.astype(BF)
    rest = x - hi.astype(F32)
    mid = rest.astype(BF)
    low = (rest - mid.astype(F32)).astype(BF)
    return hi, mid, low


def in_vmem(count):
    return [pl.BlockSpec(memory_space=pltpu.VMEM) for _ in range(count)]


def small(shape, dtype):
    return math.prod(shape) * jnp.dtype(dtype).itemsize <= ON_CHIP_BYTES


def vmem(value):
    if small(value.shape, value.dtype):
        return pltpu.with_memory_space_constraint(value, pltpu.VMEM)
    return value


def held(shape, dtype):
    if small(shape, dtype):
        return pltpu.VMEM(shape, dtype)
    return jax.ShapeDtypeStruct(shape, dtype)


def head_of(h):
    return pl.ds(h * HEAD_DIM, HEAD_DIM)


def pack(block_order, keys, values, queries, grads, outs, sections):
    rows, features = grads.shape
    here = features // sections
    heads = here // HEAD_DIM
    key_count = keys.shape[0]

    def body(order_hbm, k_hbm, v_hbm, q_hbm, g_hbm, o_hbm, *refs):
        blocks = refs[:sections]
        start_ref, k_ref, v_ref, q_ref, g_ref, o_ref, order_ref, sems = refs[sections:]
        pairs = [
            (q_hbm, q_ref),
            (g_hbm, g_ref),
            (o_hbm, o_ref),
            (order_hbm, order_ref),
            (k_hbm, k_ref),
            (v_hbm, v_ref),
        ]
        copies = [pltpu.make_async_copy(*pair, sems.at[i]) for i, pair in enumerate(pairs)]
        for copy in copies:
            copy.start()
        section = lax.axis_index("section")
        lane = lax.broadcasted_iota(jnp.int32, (rows, LANES), 1)

        def at(s, h):
            return pl.ds(pl.multiple_of(s * here + h * HEAD_DIM, HEAD_DIM), HEAD_DIM)

        for i in range(3):
            copies[i].wait()
        for step, out_ref in enumerate(blocks):
            to = section ^ step
            extra = jnp.zeros((rows, LANES), F32)
            for h in range(heads):
                g = g_ref[:, at(to, h)]
                terms = g.astype(F32) * o_ref[:, at(to, h)].astype(F32)
                delta = jnp.sum(terms, axis=1, keepdims=True)
                for part, value in enumerate(split3(delta)):
                    extra = jnp.where(lane == part * heads + h, value.astype(F32), extra)
                out_ref[:, head_of(h)] = q_ref[:, at(to, h)]
                out_ref[:, head_of(heads + 1 + h)] = g
            out_ref[:, head_of(heads)] = extra.astype(BF)
        copies[3].wait()
        block = order_ref[lax.axis_index("ctx")]
        start_ref[...] = jnp.full(start_ref.shape, block * key_count, jnp.int32)
        copies[4].wait()
        copies[5].wait()

    return pl.pallas_call(
        body,
        in_specs=[pl.BlockSpec(memory_space=pl.ANY)] * 6,
        out_specs=in_vmem(sections + 3),
        out_shape=[
            *[held((rows, 2 * here + LANES), BF)] * sections,
            held((8, LANES), jnp.int32),
            held(keys.shape, BF),
            held(values.shape, BF),
        ],
        scratch_shapes=[
            pltpu.VMEM((rows, features), BF),
            pltpu.VMEM((rows, features), BF),
            pltpu.VMEM((rows, features), BF),
            pltpu.SMEM(block_order.shape, jnp.int32),
            pltpu.SemaphoreType.DMA((6,)),
        ],
        name="pack",
    )(block_order, keys, values, queries, grads, outs)


def visible_of(start_ref, shape, row_count, key_total):
    key_pos = start_ref[0:1, 0:1] + lax.broadcasted_iota(jnp.int32, shape, 0)
    row = lax.broadcasted_iota(jnp.int32, shape, 1) % row_count
    return key_pos <= key_total - row_count + row


def stats_kernel(start, queries, keys, row_count, key_total):
    m = queries.shape[0]
    key_count, here = keys.shape
    heads = here // HEAD_DIM
    slots = -(-heads // 8) * 8
    scaling = HEAD_DIM ** (-0.5)

    def body(start_ref, q_ref, k_ref, out_ref, prob_ref, delta_ref, sent_ref):
        visible = visible_of(start_ref, (key_count, m), row_count, key_total)
        out_ref[...] = jnp.ones_like(out_ref)
        for h in range(heads):
            at = head_of(h)
            s = jnp.where(visible, nt(k_ref[:, at], q_ref[:, at]) * scaling, masked_score)
            top = jnp.max(s, axis=0, keepdims=True)
            prob = jnp.where(visible, jnp.exp(s - top), 0.0)
            prob_ref[h] = prob
            out_ref[0, pl.ds(h, 1), :] = top
            out_ref[1, pl.ds(h, 1), :] = jnp.sum(prob, axis=0, keepdims=True)
        slot = lax.broadcasted_iota(jnp.int32, (slots, LANES), 0)
        lane = lax.broadcasted_iota(jnp.int32, (slots, LANES), 1)
        pick = (lane % heads == slot) & (lane < 3 * heads)
        delta_ref[...] = nt(jnp.where(pick, 1.0, 0.0).astype(BF), q_ref[:, pl.ds(here, LANES)])
        sent = jnp.zeros((m, LANES), F32)
        for i in range(2):
            for part, value in enumerate(split3(out_ref[i])):
                at = (3 * i + part) * heads
                place = (lane == at + slot) & (slot < heads)
                sent += tn(value, jnp.where(place, 1.0, 0.0).astype(BF))
        sent_ref[...] = sent.astype(BF)

    return pl.pallas_call(
        body,
        in_specs=in_vmem(3),
        out_specs=in_vmem(4),
        out_shape=[
            held((2, slots, m), F32),
            held((heads, key_count, m), F32),
            held((slots, m), F32),
            held((m, LANES), BF),
        ],
        name="stats",
    )(vmem(start), vmem(queries), vmem(keys))


def query_kernel(grads, keys, values, probs, deltas, sent):
    m = grads.shape[0]
    key_count, here = keys.shape
    heads = here // HEAD_DIM
    scaling = HEAD_DIM ** (-0.5)

    def body(g_ref, k_ref, v_ref, p_ref, d_ref, sent_ref, u_hbm, ds_ref, u_ref, sems):
        def copy_of(h):
            return pltpu.make_async_copy(
                u_ref.at[:, head_of(h)], u_hbm.at[:, head_of(h)], sems.at[h]
            )

        last = pltpu.make_async_copy(sent_ref, u_hbm.at[:, head_of(heads)], sems.at[heads])
        last.start()
        for h in range(heads):
            at = head_of(h)
            ds = p_ref[h] * (nt(v_ref[:, at], g_ref[:, at]) - d_ref[h : h + 1, :]) * scaling
            ds = ds.astype(BF)
            u_ref[:, at] = tn(ds, k_ref[:, at]).astype(BF)
            copy_of(h).start()
            ds_ref[h] = ds
        for h in range(heads):
            copy_of(h).wait()
        last.wait()

    return pl.pallas_call(
        body,
        in_specs=in_vmem(6),
        out_specs=[pl.BlockSpec(memory_space=pl.ANY), in_vmem(1)[0]],
        out_shape=[
            jax.ShapeDtypeStruct((m, here + LANES), BF),
            held((heads, key_count, m), BF),
        ],
        scratch_shapes=[
            pltpu.VMEM((m, here), BF),
            pltpu.SemaphoreType.DMA((heads + 1,)),
        ],
        name="query_gradients",
    )(vmem(grads), vmem(keys), vmem(values), vmem(probs), vmem(deltas), vmem(sent))


def cache_kernel(queries, grads, probs, score_grads, own, merged):
    here = grads.shape[1]
    heads, key_count, _ = probs.shape

    def body(q_ref, g_ref, p_ref, ds_ref, own_ref, all_ref, dk_ref, dv_ref):
        share = jnp.exp(own_ref[0] - all_ref[0]) / all_ref[1]
        for h in range(heads):
            at = head_of(h)
            row = share[h : h + 1, :]
            ds = (ds_ref[h].astype(F32) * row).astype(BF)
            prob = (p_ref[h] * row).astype(BF)
            dk_ref[:, at] = nn(ds, q_ref[:, at]).astype(BF)
            dv_ref[:, at] = nn(prob, g_ref[:, at]).astype(BF)

    return pl.pallas_call(
        body,
        in_specs=in_vmem(6),
        out_specs=in_vmem(2),
        out_shape=[jax.ShapeDtypeStruct((key_count, here), BF)] * 2,
        name="cache_gradients",
    )(vmem(queries), vmem(grads), vmem(probs), vmem(score_grads), vmem(own), vmem(merged))


def combine_kernel(parts):
    sections, holders, rows, width = parts.shape
    here = width - LANES
    heads = here // HEAD_DIM

    def body(p_ref, out_ref):
        def stats_of(s, c):
            e = p_ref[s, c, :, pl.ds(here, LANES)].astype(F32)
            e += pltpu.roll(e, LANES - heads, 1) + pltpu.roll(e, LANES - 2 * heads, 1)
            return e, pltpu.roll(e, LANES - 3 * heads, 1)

        for s in range(sections):
            top = jnp.full((rows, LANES), -jnp.inf, F32)
            for c in range(holders):
                top = jnp.maximum(top, stats_of(s, c)[0])
            total = jnp.zeros((rows, LANES), F32)
            for c in range(holders):
                own, count = stats_of(s, c)
                total += jnp.exp(own - top) * count
            sums = [jnp.zeros((rows, HEAD_DIM), F32) for _ in range(heads)]
            for c in range(holders):
                share = jnp.exp(stats_of(s, c)[0] - top) / total
                for h in range(heads):
                    value = p_ref[s, c, :, head_of(h)].astype(F32)
                    sums[h] += share[:, h : h + 1] * value
            for h in range(heads):
                out_ref[:, head_of(s * heads + h)] = sums[h].astype(BF)

    return pl.pallas_call(
        body,
        in_specs=in_vmem(1),
        out_specs=in_vmem(1)[0],
        out_shape=jax.ShapeDtypeStruct((rows, sections * here), BF),
        name="combine",
    )(vmem(parts))


def merge_stats(stats, axis, order):
    for bit in order:
        other = flip(stats, axis, 1 << bit)
        top = jnp.maximum(stats[0], other[0])
        total = stats[1] * jnp.exp(stats[0] - top) + other[1] * jnp.exp(other[0] - top)
        stats = jnp.stack([top, total])
    return stats


def flip(value, axis, bit):
    count = lax.axis_size(axis)
    return lax.ppermute(value, axis, [(i, i ^ bit) for i in range(count)])


def ordered(mine, other, upper, axis):
    first = jnp.where(upper, other, mine)
    second = jnp.where(upper, mine, other)
    return jnp.stack([first, second], axis)


def swap_blocks(blocks, axis):
    count = lax.axis_size(axis)
    here = lax.axis_index(axis)
    got = [blocks[0]]
    for step in range(1, count):
        got.append(flip(blocks[step], axis, step))
    bit = 1
    while bit < count:
        upper = here & bit != 0
        got = [jnp.where(upper, got[i ^ bit], got[i]) for i in range(count)]
        bit *= 2
    return jnp.stack(got)


def flip_by_parity(value, bits):
    sections, count = lax.axis_size("section"), lax.axis_size("ctx")
    pairs = []
    for section in range(sections):
        for at in range(count):
            to = at ^ (1 << bits[section % 2])
            pairs.append((section * count + at, section * count + to))
    return lax.ppermute(value, ("section", "ctx"), pairs)


def spread_blocks(blocks, even_bits, odd_bits):
    count = lax.axis_size("ctx")
    at = lax.axis_index("ctx")
    odd = lax.axis_index("section") % 2 == 1
    lead, rest = blocks.shape[0], blocks.shape[1:]
    for i, (even_bit, odd_bit) in enumerate(zip(even_bits, odd_bits)):
        upper = at >> jnp.where(odd, odd_bit, even_bit) & 1 == 1
        other = flip_by_parity(blocks, (even_bit, odd_bit))
        blocks = ordered(blocks, other, upper, 1 + i)
    turned = [bits[-2] < bits[-1] for bits in (even_bits, odd_bits)]
    if any(turned):
        other = jnp.swapaxes(blocks, i, i + 1)
        blocks = jnp.where(jnp.where(odd, turned[1], turned[0]), other, blocks)
    return blocks.reshape((lead, count) + rest)


def exchange(blocks):
    return lax.all_to_all(blocks, ("section", "ctx"), 0, 0, tiled=True)


def compute(block_order, queries, cache_keys, cache_values, attention_out, output_grad):
    sections = lax.axis_size("section")
    ctx_count = lax.axis_size("ctx")
    assert ctx_count & (ctx_count - 1) == 0 and ctx_count > 2
    assert sections & (sections - 1) == 0 and sections > 1
    layers, rows, _ = queries.shape
    assert layers == 1
    key_count, here = cache_keys.shape
    row_count = rows * ctx_count
    key_total = key_count * ctx_count
    peers = sections * ctx_count

    ctx_bits = ctx_count.bit_length() - 1
    down = list(range(ctx_bits))[::-1]

    packed = pack(
        block_order,
        cache_keys,
        cache_values,
        queries[0],
        output_grad[0],
        attention_out[0],
        sections,
    )
    start, keys, values = packed[sections:]
    swapped = swap_blocks(packed[:sections], "section")
    query_all, grad_all = swapped[..., : here + LANES], swapped[..., here + LANES :]
    turned = down[:-2] + [down[-1], down[-2]]
    query_all = spread_blocks(query_all, down, down)
    query_all = query_all.reshape(peers * rows, here + LANES)
    grad_all = spread_blocks(grad_all, turned, down)
    grad_all = grad_all.reshape(peers * rows, here)

    own, probs, deltas, row_stats = stats_kernel(start, query_all, keys, row_count, key_total)
    merged = merge_stats(own, "ctx", down[-1:] + down[:-1])
    part, score_grads = query_kernel(grad_all, keys, values, probs, deltas, row_stats)
    part = exchange(part.reshape(peers, rows, here + LANES))
    grad_keys, grad_values = cache_kernel(query_all, grad_all, probs, score_grads, own, merged)
    grad_queries = combine_kernel(part.reshape(sections, ctx_count, rows, here + LANES))
    return (grad_queries[None], grad_keys, grad_values)


def solution(mesh):
    in_specs = (
        P(),
        P("section", "ctx", None),
        P("ctx", "section"),
        P("ctx", "section"),
        P("section", "ctx", None),
        P("section", "ctx", None),
    )
    out_specs = (P("section", "ctx", None), P("ctx", "section"), P("ctx", "section"))
    return jax.shard_map(compute, mesh=mesh, in_specs=in_specs, out_specs=out_specs, check_vma=False)
```

```python
import math

import jax
import jax.numpy as jnp
from jax import lax
from jax.experimental import pallas as pl
from jax.experimental.pallas import tpu as pltpu
from jax.sharding import PartitionSpec as P


HEAD_DIM = 128
LANES = 128
ON_CHIP_BYTES = 1 << 20
masked_score = -1e30
BF = jnp.bfloat16
F32 = jnp.float32


def nt(a, b):
    return lax.dot_general(a, b, (((1,), (1,)), ((), ())), preferred_element_type=F32)


def nn(a, b):
    return lax.dot_general(a, b, (((1,), (0,)), ((), ())), preferred_element_type=F32)


def tn(a, b):
    return lax.dot_general(a, b, (((0,), (0,)), ((), ())), preferred_element_type=F32)


def split3(x):
    hi = x.astype(BF)
    rest = x - hi.astype(F32)
    mid = rest.astype(BF)
    low = (rest - mid.astype(F32)).astype(BF)
    return hi, mid, low


def in_vmem(count):
    return [pl.BlockSpec(memory_space=pltpu.VMEM) for _ in range(count)]


def small(shape, dtype):
    return math.prod(shape) * jnp.dtype(dtype).itemsize <= ON_CHIP_BYTES


def vmem(value):
    if small(value.shape, value.dtype):
        return pltpu.with_memory_space_constraint(value, pltpu.VMEM)
    return value


def held(shape, dtype):
    if small(shape, dtype):
        return pltpu.VMEM(shape, dtype)
    return jax.ShapeDtypeStruct(shape, dtype)


def head_of(h):
    return pl.ds(h * HEAD_DIM, HEAD_DIM)


def pack(block_order, keys, values, queries, grads, outs, sections):
    rows, features = grads.shape
    here = features // sections
    heads = here // HEAD_DIM
    key_count = keys.shape[0]

    def body(order_hbm, k_hbm, v_hbm, q_hbm, g_hbm, o_hbm, *refs):
        blocks = refs[:sections]
        start_ref, k_ref, v_ref, q_ref, g_ref, o_ref, order_ref, sems = refs[sections:]
        pairs = [
            (q_hbm, q_ref),
            (g_hbm, g_ref),
            (o_hbm, o_ref),
            (order_hbm, order_ref),
            (k_hbm, k_ref),
            (v_hbm, v_ref),
        ]
        copies = [pltpu.make_async_copy(*pair, sems.at[i]) for i, pair in enumerate(pairs)]
        for copy in copies:
            copy.start()
        section = lax.axis_index("section")
        lane = lax.broadcasted_iota(jnp.int32, (rows, LANES), 1)

        def at(s, h):
            return pl.ds(pl.multiple_of(s * here + h * HEAD_DIM, HEAD_DIM), HEAD_DIM)

        for i in range(3):
            copies[i].wait()
        for step, out_ref in enumerate(blocks):
            to = section ^ step
            extra = jnp.zeros((rows, LANES), F32)
            for h in range(heads):
                g = g_ref[:, at(to, h)]
                terms = g.astype(F32) * o_ref[:, at(to, h)].astype(F32)
                delta = jnp.sum(terms, axis=1, keepdims=True)
                for part, value in enumerate(split3(delta)):
                    extra = jnp.where(lane == part * heads + h, value.astype(F32), extra)
                out_ref[:, head_of(h)] = q_ref[:, at(to, h)]
                out_ref[:, head_of(heads + 1 + h)] = g
            out_ref[:, head_of(heads)] = extra.astype(BF)
        copies[3].wait()
        block = order_ref[lax.axis_index("ctx")]
        start_ref[...] = jnp.full(start_ref.shape, block * key_count, jnp.int32)
        copies[4].wait()
        copies[5].wait()

    return pl.pallas_call(
        body,
        in_specs=[pl.BlockSpec(memory_space=pl.ANY)] * 6,
        out_specs=in_vmem(sections + 3),
        out_shape=[
            *[held((rows, 2 * here + LANES), BF)] * sections,
            held((8, LANES), jnp.int32),
            held(keys.shape, BF),
            held(values.shape, BF),
        ],
        scratch_shapes=[
            pltpu.VMEM((rows, features), BF),
            pltpu.VMEM((rows, features), BF),
            pltpu.VMEM((rows, features), BF),
            pltpu.SMEM(block_order.shape, jnp.int32),
            pltpu.SemaphoreType.DMA((6,)),
        ],
        name="pack",
    )(block_order, keys, values, queries, grads, outs)


def visible_of(start_ref, shape, row_count, key_total):
    key_pos = start_ref[0:1, 0:1] + lax.broadcasted_iota(jnp.int32, shape, 0)
    row = lax.broadcasted_iota(jnp.int32, shape, 1) % row_count
    return key_pos <= key_total - row_count + row


def stats_kernel(start, queries, keys, row_count, key_total):
    m = queries.shape[0]
    key_count, here = keys.shape
    heads = here // HEAD_DIM
    slots = -(-heads // 8) * 8
    scaling = HEAD_DIM ** (-0.5)

    def body(start_ref, q_ref, k_ref, out_ref, prob_ref, delta_ref, sent_ref):
        visible = visible_of(start_ref, (key_count, m), row_count, key_total)
        out_ref[...] = jnp.ones_like(out_ref)
        for h in range(heads):
            at = head_of(h)
            s = jnp.where(visible, nt(k_ref[:, at], q_ref[:, at]) * scaling, masked_score)
            top = jnp.max(s, axis=0, keepdims=True)
            prob = jnp.where(visible, jnp.exp(s - top), 0.0)
            prob_ref[h] = prob
            out_ref[0, pl.ds(h, 1), :] = top
            out_ref[1, pl.ds(h, 1), :] = jnp.sum(prob, axis=0, keepdims=True)
        slot = lax.broadcasted_iota(jnp.int32, (slots, LANES), 0)
        lane = lax.broadcasted_iota(jnp.int32, (slots, LANES), 1)
        pick = (lane % heads == slot) & (lane < 3 * heads)
        delta_ref[...] = nt(jnp.where(pick, 1.0, 0.0).astype(BF), q_ref[:, pl.ds(here, LANES)])
        sent = jnp.zeros((m, LANES), F32)
        for i in range(2):
            for part, value in enumerate(split3(out_ref[i])):
                at = (3 * i + part) * heads
                place = (lane == at + slot) & (slot < heads)
                sent += tn(value, jnp.where(place, 1.0, 0.0).astype(BF))
        sent_ref[...] = sent.astype(BF)

    return pl.pallas_call(
        body,
        in_specs=in_vmem(3),
        out_specs=in_vmem(4),
        out_shape=[
            held((2, slots, m), F32),
            held((heads, key_count, m), F32),
            held((slots, m), F32),
            held((m, LANES), BF),
        ],
        name="stats",
    )(vmem(start), vmem(queries), vmem(keys))


def query_kernel(grads, keys, values, probs, deltas, sent):
    m = grads.shape[0]
    key_count, here = keys.shape
    heads = here // HEAD_DIM
    scaling = HEAD_DIM ** (-0.5)

    def body(g_ref, k_ref, v_ref, p_ref, d_ref, sent_ref, u_hbm, ds_ref, u_ref, sems):
        def copy_of(h):
            return pltpu.make_async_copy(
                u_ref.at[:, head_of(h)], u_hbm.at[:, head_of(h)], sems.at[h]
            )

        last = pltpu.make_async_copy(sent_ref, u_hbm.at[:, head_of(heads)], sems.at[heads])
        last.start()
        for h in range(heads):
            at = head_of(h)
            ds = p_ref[h] * (nt(v_ref[:, at], g_ref[:, at]) - d_ref[h : h + 1, :]) * scaling
            ds = ds.astype(BF)
            u_ref[:, at] = tn(ds, k_ref[:, at]).astype(BF)
            copy_of(h).start()
            ds_ref[h] = ds
        for h in range(heads):
            copy_of(h).wait()
        last.wait()

    return pl.pallas_call(
        body,
        in_specs=in_vmem(6),
        out_specs=[pl.BlockSpec(memory_space=pl.ANY), in_vmem(1)[0]],
        out_shape=[
            jax.ShapeDtypeStruct((m, here + LANES), BF),
            held((heads, key_count, m), BF),
        ],
        scratch_shapes=[
            pltpu.VMEM((m, here), BF),
            pltpu.SemaphoreType.DMA((heads + 1,)),
        ],
        name="query_gradients",
    )(vmem(grads), vmem(keys), vmem(values), vmem(probs), vmem(deltas), vmem(sent))


def cache_kernel(queries, grads, probs, score_grads, own, merged):
    here = grads.shape[1]
    heads, key_count, _ = probs.shape

    def body(q_ref, g_ref, p_ref, ds_ref, own_ref, all_ref, dk_ref, dv_ref):
        share = jnp.exp(own_ref[0] - all_ref[0]) / all_ref[1]
        for h in range(heads):
            at = head_of(h)
            row = share[h : h + 1, :]
            ds = (ds_ref[h].astype(F32) * row).astype(BF)
            prob = (p_ref[h] * row).astype(BF)
            dk_ref[:, at] = nn(ds, q_ref[:, at]).astype(BF)
            dv_ref[:, at] = nn(prob, g_ref[:, at]).astype(BF)

    return pl.pallas_call(
        body,
        in_specs=in_vmem(6),
        out_specs=in_vmem(2),
        out_shape=[jax.ShapeDtypeStruct((key_count, here), BF)] * 2,
        name="cache_gradients",
    )(vmem(queries), vmem(grads), vmem(probs), vmem(score_grads), vmem(own), vmem(merged))


def combine_kernel(parts, sections, holders):
    width = parts.shape[1]
    rows = parts.shape[0] // (sections * holders)
    here = width - LANES
    heads = here // HEAD_DIM
    shape = (sections, holders, rows, HEAD_DIM)

    def body(p_ref, out_ref):
        stats = p_ref[:, pl.ds(here, LANES)]
        lane = lax.broadcasted_iota(jnp.int32, (LANES, HEAD_DIM), 0)
        for h in range(heads):
            mine = lane % heads == h
            first = mine & (lane < 3 * heads)
            second = mine & (lane >= 3 * heads) & (lane < 6 * heads)
            own = nn(stats, jnp.where(first, 1.0, 0.0).astype(BF)).reshape(shape)
            count = nn(stats, jnp.where(second, 1.0, 0.0).astype(BF)).reshape(shape)
            share = jnp.exp(own - jnp.max(own, axis=1, keepdims=True))
            total = jnp.sum(share * count, axis=1)
            value = p_ref[:, head_of(h)].astype(F32).reshape(shape)
            result = jnp.sum(share * value, axis=1) / total
            for s in range(sections):
                out_ref[:, head_of(s * heads + h)] = result[s].astype(BF)

    return pl.pallas_call(
        body,
        in_specs=in_vmem(1),
        out_specs=in_vmem(1)[0],
        out_shape=jax.ShapeDtypeStruct((rows, sections * here), BF),
        name="combine",
    )(vmem(parts))


def merge_stats(stats, axis, order):
    for bit in order:
        other = flip(stats, axis, 1 << bit)
        top = jnp.maximum(stats[0], other[0])
        total = stats[1] * jnp.exp(stats[0] - top) + other[1] * jnp.exp(other[0] - top)
        stats = jnp.stack([top, total])
    return stats


def flip(value, axis, bit):
    count = lax.axis_size(axis)
    return lax.ppermute(value, axis, [(i, i ^ bit) for i in range(count)])


def ordered(mine, other, upper, axis):
    first = jnp.where(upper, other, mine)
    second = jnp.where(upper, mine, other)
    return jnp.stack([first, second], axis)


def swap_blocks(blocks, axis):
    count = lax.axis_size(axis)
    here = lax.axis_index(axis)
    got = [blocks[0]]
    for step in range(1, count):
        got.append(flip(blocks[step], axis, step))
    bit = 1
    while bit < count:
        upper = here & bit != 0
        got = [jnp.where(upper, got[i ^ bit], got[i]) for i in range(count)]
        bit *= 2
    return jnp.stack(got)


def spread_blocks(blocks, axis, order):
    count = lax.axis_size(axis)
    lead, rest = blocks.shape[0], blocks.shape[1:]
    done = []
    for bit in order:
        upper = lax.axis_index(axis) & (1 << bit) != 0
        other = flip(blocks, axis, 1 << bit)
        blocks = ordered(blocks, other, upper, 1 + sum(b > bit for b in done))
        done.append(bit)
    return blocks.reshape((lead, count) + rest)


def exchange(blocks):
    return lax.all_to_all(blocks, ("section", "ctx"), 0, 0, tiled=True)


def compute(block_order, queries, cache_keys, cache_values, attention_out, output_grad):
    sections = lax.axis_size("section")
    ctx_count = lax.axis_size("ctx")
    assert ctx_count & (ctx_count - 1) == 0
    assert sections & (sections - 1) == 0 and sections > 1
    layers, rows, _ = queries.shape
    assert layers == 1
    key_count, here = cache_keys.shape
    row_count = rows * ctx_count
    key_total = key_count * ctx_count
    peers = sections * ctx_count

    ctx_bits = ctx_count.bit_length() - 1
    down = list(range(ctx_bits))[::-1]

    packed = pack(
        block_order,
        cache_keys,
        cache_values,
        queries[0],
        output_grad[0],
        attention_out[0],
        sections,
    )
    start, keys, values = packed[sections:]
    swapped = swap_blocks(packed[:sections], "section")
    query_all, grad_all = swapped[..., : here + LANES], swapped[..., here + LANES :]
    query_all = spread_blocks(query_all, "ctx", down)
    query_all = query_all.reshape(peers * rows, here + LANES)
    grad_all = spread_blocks(grad_all, "ctx", down[:1] + down[1:][::-1])
    grad_all = grad_all.reshape(peers * rows, here)

    own, probs, deltas, row_stats = stats_kernel(start, query_all, keys, row_count, key_total)
    merged = merge_stats(own, "ctx", down[-1:] + down[:-1])
    part, score_grads = query_kernel(grad_all, keys, values, probs, deltas, row_stats)
    part = exchange(part.reshape(peers, rows, here + LANES))
    grad_keys, grad_values = cache_kernel(query_all, grad_all, probs, score_grads, own, merged)
    part = part.reshape(peers * rows, here + LANES)
    grad_queries = combine_kernel(part, sections, ctx_count)
    return (grad_queries[None], grad_keys, grad_values)


def solution(mesh):
    in_specs = (
        P(),
        P("section", "ctx", None),
        P("ctx", "section"),
        P("ctx", "section"),
        P("section", "ctx", None),
        P("section", "ctx", None),
    )
    out_specs = (P("section", "ctx", None), P("ctx", "section"), P("ctx", "section"))
    return jax.shard_map(compute, mesh=mesh, in_specs=in_specs, out_specs=out_specs, check_vma=False)
```

```python
import math

import jax
import jax.numpy as jnp
from jax import lax
from jax.experimental import pallas as pl
from jax.experimental.pallas import tpu as pltpu
from jax.sharding import PartitionSpec as P


HEAD_DIM = 128
LANES = 128
ON_CHIP_BYTES = 1 << 20
masked_score = -1e30
BF = jnp.bfloat16
F32 = jnp.float32


def nt(a, b):
    return lax.dot_general(a, b, (((1,), (1,)), ((), ())), preferred_element_type=F32)


def nn(a, b):
    return lax.dot_general(a, b, (((1,), (0,)), ((), ())), preferred_element_type=F32)


def tn(a, b):
    return lax.dot_general(a, b, (((0,), (0,)), ((), ())), preferred_element_type=F32)


def split3(x):
    hi = x.astype(BF)
    rest = x - hi.astype(F32)
    mid = rest.astype(BF)
    low = (rest - mid.astype(F32)).astype(BF)
    return hi, mid, low


def in_vmem(count):
    return [pl.BlockSpec(memory_space=pltpu.VMEM) for _ in range(count)]


def small(shape, dtype):
    return math.prod(shape) * jnp.dtype(dtype).itemsize <= ON_CHIP_BYTES


def vmem(value):
    if small(value.shape, value.dtype):
        return pltpu.with_memory_space_constraint(value, pltpu.VMEM)
    return value


def held(shape, dtype):
    if small(shape, dtype):
        return pltpu.VMEM(shape, dtype)
    return jax.ShapeDtypeStruct(shape, dtype)


def head_of(h):
    return pl.ds(h * HEAD_DIM, HEAD_DIM)


def pack(block_order, keys, values, queries, grads, outs, sections):
    rows, features = grads.shape
    here = features // sections
    heads = here // HEAD_DIM
    key_count = keys.shape[0]

    def body(order_hbm, k_hbm, v_hbm, q_hbm, g_hbm, o_hbm, *refs):
        blocks = refs[:sections]
        start_ref, k_ref, v_ref, q_ref, g_ref, o_ref, order_ref, sems = refs[sections:]
        pairs = [
            (q_hbm, q_ref),
            (g_hbm, g_ref),
            (o_hbm, o_ref),
            (order_hbm, order_ref),
            (k_hbm, k_ref),
            (v_hbm, v_ref),
        ]
        copies = [pltpu.make_async_copy(*pair, sems.at[i]) for i, pair in enumerate(pairs)]
        for copy in copies:
            copy.start()
        section = lax.axis_index("section")
        lane = lax.broadcasted_iota(jnp.int32, (rows, LANES), 1)

        def at(s, h):
            return pl.ds(pl.multiple_of(s * here + h * HEAD_DIM, HEAD_DIM), HEAD_DIM)

        for i in range(3):
            copies[i].wait()
        for step, out_ref in enumerate(blocks):
            to = section ^ step
            extra = jnp.zeros((rows, LANES), F32)
            for h in range(heads):
                g = g_ref[:, at(to, h)]
                terms = g.astype(F32) * o_ref[:, at(to, h)].astype(F32)
                delta = jnp.sum(terms, axis=1, keepdims=True)
                for part, value in enumerate(split3(delta)):
                    extra = jnp.where(lane == part * heads + h, value.astype(F32), extra)
                out_ref[:, head_of(h)] = q_ref[:, at(to, h)]
                out_ref[:, head_of(heads + 1 + h)] = g
            out_ref[:, head_of(heads)] = extra.astype(BF)
        copies[3].wait()
        block = order_ref[lax.axis_index("ctx")]
        start_ref[...] = jnp.full(start_ref.shape, block * key_count, jnp.int32)
        copies[4].wait()
        copies[5].wait()

    return pl.pallas_call(
        body,
        in_specs=[pl.BlockSpec(memory_space=pl.ANY)] * 6,
        out_specs=in_vmem(sections + 3),
        out_shape=[
            *[held((rows, 2 * here + LANES), BF)] * sections,
            held((8, LANES), jnp.int32),
            held(keys.shape, BF),
            held(values.shape, BF),
        ],
        scratch_shapes=[
            pltpu.VMEM((rows, features), BF),
            pltpu.VMEM((rows, features), BF),
            pltpu.VMEM((rows, features), BF),
            pltpu.SMEM(block_order.shape, jnp.int32),
            pltpu.SemaphoreType.DMA((6,)),
        ],
        name="pack",
    )(block_order, keys, values, queries, grads, outs)


def visible_of(start_ref, shape, row_count, key_total):
    key_pos = start_ref[0:1, 0:1] + lax.broadcasted_iota(jnp.int32, shape, 0)
    row = lax.broadcasted_iota(jnp.int32, shape, 1) % row_count
    return key_pos <= key_total - row_count + row


def stats_kernel(start, queries, keys, row_count, key_total):
    m = queries.shape[0]
    key_count, here = keys.shape
    heads = here // HEAD_DIM
    slots = -(-heads // 8) * 8
    scaling = HEAD_DIM ** (-0.5)

    def body(start_ref, q_ref, k_ref, out_ref, prob_ref):
        visible = visible_of(start_ref, (key_count, m), row_count, key_total)
        out_ref[...] = jnp.ones_like(out_ref)
        for h in range(heads):
            at = head_of(h)
            s = jnp.where(visible, nt(k_ref[:, at], q_ref[:, at]) * scaling, masked_score)
            top = jnp.max(s, axis=0, keepdims=True)
            prob = jnp.where(visible, jnp.exp(s - top), 0.0)
            prob_ref[h] = prob
            out_ref[0, pl.ds(h, 1), :] = top
            out_ref[1, pl.ds(h, 1), :] = jnp.sum(prob, axis=0, keepdims=True)

    return pl.pallas_call(
        body,
        in_specs=in_vmem(3),
        out_specs=in_vmem(2),
        out_shape=[
            held((2, slots, m), F32),
            held((heads, key_count, m), F32),
        ],
        name="stats",
    )(vmem(start), vmem(queries), vmem(keys))


def query_kernel(queries, grads, keys, values, probs, own):
    m = grads.shape[0]
    key_count, here = keys.shape
    heads = here // HEAD_DIM
    slots = own.shape[1]
    scaling = HEAD_DIM ** (-0.5)

    def body(q_ref, g_ref, k_ref, v_ref, p_ref, own_ref, u_hbm, ds_ref, u_ref, sems):
        def copy_of(h):
            return pltpu.make_async_copy(
                u_ref.at[:, head_of(h)], u_hbm.at[:, head_of(h)], sems.at[h]
            )

        slot = lax.broadcasted_iota(jnp.int32, (slots, LANES), 0)
        lane = lax.broadcasted_iota(jnp.int32, (slots, LANES), 1)
        pick = (lane % heads == slot) & (lane < 3 * heads)
        deltas = nt(jnp.where(pick, 1.0, 0.0).astype(BF), q_ref[:, pl.ds(here, LANES)])
        sent = jnp.zeros((m, LANES), F32)
        for i in range(2):
            for part, value in enumerate(split3(own_ref[i])):
                at = (3 * i + part) * heads
                place = (lane == at + slot) & (slot < heads)
                sent += tn(value, jnp.where(place, 1.0, 0.0).astype(BF))
        u_ref[:, head_of(heads)] = sent.astype(BF)
        copy_of(heads).start()
        for h in range(heads):
            at = head_of(h)
            ds = p_ref[h] * (nt(v_ref[:, at], g_ref[:, at]) - deltas[h : h + 1, :]) * scaling
            ds = ds.astype(BF)
            u_ref[:, at] = tn(ds, k_ref[:, at]).astype(BF)
            copy_of(h).start()
            ds_ref[h] = ds
        for h in range(heads + 1):
            copy_of(h).wait()

    return pl.pallas_call(
        body,
        in_specs=in_vmem(6),
        out_specs=[pl.BlockSpec(memory_space=pl.ANY), in_vmem(1)[0]],
        out_shape=[
            jax.ShapeDtypeStruct((m, here + LANES), BF),
            held((heads, key_count, m), BF),
        ],
        scratch_shapes=[
            pltpu.VMEM((m, here + LANES), BF),
            pltpu.SemaphoreType.DMA((heads + 1,)),
        ],
        name="query_gradients",
    )(vmem(queries), vmem(grads), vmem(keys), vmem(values), vmem(probs), vmem(own))


def cache_kernel(queries, grads, probs, score_grads, own, merged):
    here = grads.shape[1]
    heads, key_count, _ = probs.shape

    def body(q_ref, g_ref, p_ref, ds_ref, own_ref, all_ref, dk_ref, dv_ref):
        share = jnp.exp(own_ref[0] - all_ref[0]) / all_ref[1]
        for h in range(heads):
            at = head_of(h)
            row = share[h : h + 1, :]
            ds = (ds_ref[h].astype(F32) * row).astype(BF)
            prob = (p_ref[h] * row).astype(BF)
            dk_ref[:, at] = nn(ds, q_ref[:, at]).astype(BF)
            dv_ref[:, at] = nn(prob, g_ref[:, at]).astype(BF)

    return pl.pallas_call(
        body,
        in_specs=in_vmem(6),
        out_specs=in_vmem(2),
        out_shape=[jax.ShapeDtypeStruct((key_count, here), BF)] * 2,
        name="cache_gradients",
    )(vmem(queries), vmem(grads), vmem(probs), vmem(score_grads), vmem(own), vmem(merged))


def combine_kernel(parts, sections, holders):
    width = parts.shape[1]
    rows = parts.shape[0] // (sections * holders)
    here = width - LANES
    heads = here // HEAD_DIM
    shape = (sections, holders, rows, HEAD_DIM)

    def body(p_ref, out_ref):
        stats = p_ref[:, pl.ds(here, LANES)]
        lane = lax.broadcasted_iota(jnp.int32, (LANES, HEAD_DIM), 0)
        for h in range(heads):
            mine = lane % heads == h
            first = mine & (lane < 3 * heads)
            second = mine & (lane >= 3 * heads) & (lane < 6 * heads)
            own = nn(stats, jnp.where(first, 1.0, 0.0).astype(BF)).reshape(shape)
            count = nn(stats, jnp.where(second, 1.0, 0.0).astype(BF)).reshape(shape)
            share = jnp.exp(own - jnp.max(own, axis=1, keepdims=True))
            total = jnp.sum(share * count, axis=1)
            value = p_ref[:, head_of(h)].astype(F32).reshape(shape)
            result = jnp.sum(share * value, axis=1) / total
            for s in range(sections):
                out_ref[:, head_of(s * heads + h)] = result[s].astype(BF)

    return pl.pallas_call(
        body,
        in_specs=in_vmem(1),
        out_specs=in_vmem(1)[0],
        out_shape=jax.ShapeDtypeStruct((rows, sections * here), BF),
        name="combine",
    )(vmem(parts))


def merge_stats(stats, axis, order):
    for bit in order:
        other = flip(stats, axis, 1 << bit)
        top = jnp.maximum(stats[0], other[0])
        total = stats[1] * jnp.exp(stats[0] - top) + other[1] * jnp.exp(other[0] - top)
        stats = jnp.stack([top, total])
    return stats


def flip(value, axis, bit):
    count = lax.axis_size(axis)
    return lax.ppermute(value, axis, [(i, i ^ bit) for i in range(count)])


def ordered(mine, other, upper, axis):
    first = jnp.where(upper, other, mine)
    second = jnp.where(upper, mine, other)
    return jnp.stack([first, second], axis)


def swap_blocks(blocks, axis):
    count = lax.axis_size(axis)
    here = lax.axis_index(axis)
    got = [blocks[0]]
    for step in range(1, count):
        got.append(flip(blocks[step], axis, step))
    bit = 1
    while bit < count:
        upper = here & bit != 0
        got = [jnp.where(upper, got[i ^ bit], got[i]) for i in range(count)]
        bit *= 2
    return jnp.stack(got)


def spread_blocks(blocks, axis, order):
    count = lax.axis_size(axis)
    lead, rest = blocks.shape[0], blocks.shape[1:]
    done = []
    for bit in order:
        upper = lax.axis_index(axis) & (1 << bit) != 0
        other = flip(blocks, axis, 1 << bit)
        blocks = ordered(blocks, other, upper, 1 + sum(b > bit for b in done))
        done.append(bit)
    return blocks.reshape((lead, count) + rest)


def exchange(blocks):
    return lax.all_to_all(blocks, ("section", "ctx"), 0, 0, tiled=True)


def compute(block_order, queries, cache_keys, cache_values, attention_out, output_grad):
    sections = lax.axis_size("section")
    ctx_count = lax.axis_size("ctx")
    assert ctx_count & (ctx_count - 1) == 0
    assert sections & (sections - 1) == 0 and sections > 1
    layers, rows, _ = queries.shape
    assert layers == 1
    key_count, here = cache_keys.shape
    row_count = rows * ctx_count
    key_total = key_count * ctx_count
    peers = sections * ctx_count

    ctx_bits = ctx_count.bit_length() - 1
    down = list(range(ctx_bits))[::-1]

    packed = pack(
        block_order,
        cache_keys,
        cache_values,
        queries[0],
        output_grad[0],
        attention_out[0],
        sections,
    )
    start, keys, values = packed[sections:]
    swapped = swap_blocks(packed[:sections], "section")
    query_all, grad_all = swapped[..., : here + LANES], swapped[..., here + LANES :]
    query_all = spread_blocks(query_all, "ctx", down)
    query_all = query_all.reshape(peers * rows, here + LANES)
    grad_all = spread_blocks(grad_all, "ctx", down[:1] + down[1:][::-1])
    grad_all = grad_all.reshape(peers * rows, here)

    own, probs = stats_kernel(start, query_all, keys, row_count, key_total)
    merged = merge_stats(own, "ctx", down[-1:] + down[:-1])
    part, score_grads = query_kernel(query_all, grad_all, keys, values, probs, own)
    part = exchange(part.reshape(peers, rows, here + LANES))
    grad_keys, grad_values = cache_kernel(query_all, grad_all, probs, score_grads, own, merged)
    part = part.reshape(peers * rows, here + LANES)
    grad_queries = combine_kernel(part, sections, ctx_count)
    return (grad_queries[None], grad_keys, grad_values)


def solution(mesh):
    in_specs = (
        P(),
        P("section", "ctx", None),
        P("ctx", "section"),
        P("ctx", "section"),
        P("section", "ctx", None),
        P("section", "ctx", None),
    )
    out_specs = (P("section", "ctx", None), P("ctx", "section"), P("ctx", "section"))
    return jax.shard_map(compute, mesh=mesh, in_specs=in_specs, out_specs=out_specs, check_vma=False)
```

```python
import math

import jax
import jax.numpy as jnp
from jax import lax
from jax.experimental import pallas as pl
from jax.experimental.pallas import tpu as pltpu
from jax.sharding import PartitionSpec as P


HEAD_DIM = 128
LANES = 128
ON_CHIP_BYTES = 1 << 20
masked_score = -1e30
BF = jnp.bfloat16
F32 = jnp.float32


def nt(a, b):
    return lax.dot_general(a, b, (((1,), (1,)), ((), ())), preferred_element_type=F32)


def nn(a, b):
    return lax.dot_general(a, b, (((1,), (0,)), ((), ())), preferred_element_type=F32)


def tn(a, b):
    return lax.dot_general(a, b, (((0,), (0,)), ((), ())), preferred_element_type=F32)


def split3(x):
    hi = x.astype(BF)
    rest = x - hi.astype(F32)
    mid = rest.astype(BF)
    low = (rest - mid.astype(F32)).astype(BF)
    return hi, mid, low


def in_vmem(count):
    return [pl.BlockSpec(memory_space=pltpu.VMEM) for _ in range(count)]


def small(shape, dtype):
    return math.prod(shape) * jnp.dtype(dtype).itemsize <= ON_CHIP_BYTES


def vmem(value):
    if small(value.shape, value.dtype):
        return pltpu.with_memory_space_constraint(value, pltpu.VMEM)
    return value


def held(shape, dtype):
    if small(shape, dtype):
        return pltpu.VMEM(shape, dtype)
    return jax.ShapeDtypeStruct(shape, dtype)


def head_of(h):
    return pl.ds(h * HEAD_DIM, HEAD_DIM)


def pack(block_order, keys, values, queries, grads, outs, sections):
    rows, features = grads.shape
    here = features // sections
    heads = here // HEAD_DIM
    key_count = keys.shape[0]

    def body(order_hbm, k_hbm, v_hbm, q_hbm, g_hbm, o_hbm, *refs):
        blocks = refs[:sections]
        start_ref, k_ref, v_ref, q_ref, g_ref, o_ref, order_ref, sems = refs[sections:]
        pairs = [
            (q_hbm, q_ref),
            (g_hbm, g_ref),
            (o_hbm, o_ref),
            (order_hbm, order_ref),
            (k_hbm, k_ref),
            (v_hbm, v_ref),
        ]
        copies = [pltpu.make_async_copy(*pair, sems.at[i]) for i, pair in enumerate(pairs)]
        for copy in copies:
            copy.start()
        section = lax.axis_index("section")
        lane = lax.broadcasted_iota(jnp.int32, (rows, LANES), 1)

        def at(s, h):
            return pl.ds(pl.multiple_of(s * here + h * HEAD_DIM, HEAD_DIM), HEAD_DIM)

        for i in range(3):
            copies[i].wait()
        for step, out_ref in enumerate(blocks):
            to = section ^ step
            extra = jnp.zeros((rows, LANES), F32)
            for h in range(heads):
                g = g_ref[:, at(to, h)]
                terms = g.astype(F32) * o_ref[:, at(to, h)].astype(F32)
                delta = jnp.sum(terms, axis=1, keepdims=True)
                for part, value in enumerate(split3(delta)):
                    mine = lane == (3 * section + part) * heads + h
                    extra = jnp.where(mine, value.astype(F32), extra)
                out_ref[:, head_of(h)] = q_ref[:, at(to, h)]
                out_ref[:, head_of(heads + 1 + h)] = g
            out_ref[:, head_of(heads)] = extra.astype(BF)
        copies[3].wait()
        block = order_ref[lax.axis_index("ctx")]
        start_ref[...] = jnp.full(start_ref.shape, block * key_count, jnp.int32)
        copies[4].wait()
        copies[5].wait()

    return pl.pallas_call(
        body,
        in_specs=[pl.BlockSpec(memory_space=pl.ANY)] * 6,
        out_specs=in_vmem(sections + 3),
        out_shape=[
            *[held((rows, 2 * here + LANES), BF)] * sections,
            held((8, LANES), jnp.int32),
            held(keys.shape, BF),
            held(values.shape, BF),
        ],
        scratch_shapes=[
            pltpu.VMEM((rows, features), BF),
            pltpu.VMEM((rows, features), BF),
            pltpu.VMEM((rows, features), BF),
            pltpu.SMEM(block_order.shape, jnp.int32),
            pltpu.SemaphoreType.DMA((6,)),
        ],
        name="pack",
    )(block_order, keys, values, queries, grads, outs)


def visible_of(start_ref, shape, row_count, key_total):
    key_pos = start_ref[0:1, 0:1] + lax.broadcasted_iota(jnp.int32, shape, 0)
    row = lax.broadcasted_iota(jnp.int32, shape, 1) % row_count
    return key_pos <= key_total - row_count + row


def query_head(q_ref, h, here):
    layers = (q_ref.shape[1] - LANES) // here
    parts = [q_ref[:, pl.ds(i * here + h * HEAD_DIM, HEAD_DIM)] for i in range(layers)]
    return jnp.concatenate(parts, axis=0)


def stats_kernel(start, queries, keys, row_count, key_total):
    key_count, here = keys.shape
    m = queries.shape[0] * ((queries.shape[1] - LANES) // here)
    heads = here // HEAD_DIM
    slots = -(-heads // 8) * 8
    scaling = HEAD_DIM ** (-0.5)

    def body(start_ref, q_ref, k_ref, out_ref, prob_ref):
        visible = visible_of(start_ref, (key_count, m), row_count, key_total)
        out_ref[...] = jnp.ones_like(out_ref)
        for h in range(heads):
            at = head_of(h)
            s = jnp.where(visible, nt(k_ref[:, at], query_head(q_ref, h, here)) * scaling, masked_score)
            top = jnp.max(s, axis=0, keepdims=True)
            prob = jnp.where(visible, jnp.exp(s - top), 0.0)
            prob_ref[h] = prob
            out_ref[0, pl.ds(h, 1), :] = top
            out_ref[1, pl.ds(h, 1), :] = jnp.sum(prob, axis=0, keepdims=True)

    return pl.pallas_call(
        body,
        in_specs=in_vmem(3),
        out_specs=in_vmem(2),
        out_shape=[
            held((2, slots, m), F32),
            held((heads, key_count, m), F32),
        ],
        name="stats",
    )(vmem(start), vmem(queries), vmem(keys))


def query_kernel(queries, grads, keys, values, probs, own):
    m = grads.shape[0]
    key_count, here = keys.shape
    heads = here // HEAD_DIM
    slots = own.shape[1]
    scaling = HEAD_DIM ** (-0.5)

    def body(q_ref, g_ref, k_ref, v_ref, p_ref, own_ref, u_hbm, ds_ref, u_ref, sems):
        def copy_of(h):
            return pltpu.make_async_copy(
                u_ref.at[:, head_of(h)], u_hbm.at[:, head_of(h)], sems.at[h]
            )

        slot = lax.broadcasted_iota(jnp.int32, (slots, LANES), 0)
        lane = lax.broadcasted_iota(jnp.int32, (slots, LANES), 1)
        width = 3 * heads
        layers = m // q_ref.shape[0]
        extra = q_ref[:, pl.ds(layers * here, LANES)]
        spot = lax.broadcasted_iota(jnp.int32, extra.shape, 1)
        parts = [jnp.where(spot // width == i, extra, jnp.zeros_like(extra)) for i in range(layers)]
        pick = (lane % heads == slot) & (lane < layers * width)
        pick = jnp.where(pick, 1.0, 0.0).astype(BF)
        deltas = nt(pick, jnp.concatenate(parts, axis=0))
        sent = jnp.zeros((m, LANES), F32)
        for i in range(2):
            for part, value in enumerate(split3(own_ref[i])):
                at = (3 * i + part) * heads
                place = (lane == at + slot) & (slot < heads)
                sent += tn(value, jnp.where(place, 1.0, 0.0).astype(BF))
        u_ref[:, head_of(heads)] = sent.astype(BF)
        copy_of(heads).start()
        for h in range(heads):
            at = head_of(h)
            ds = p_ref[h] * (nt(v_ref[:, at], g_ref[:, at]) - deltas[h : h + 1, :]) * scaling
            ds = ds.astype(BF)
            u_ref[:, at] = tn(ds, k_ref[:, at]).astype(BF)
            copy_of(h).start()
            ds_ref[h] = ds
        for h in range(heads + 1):
            copy_of(h).wait()

    return pl.pallas_call(
        body,
        in_specs=in_vmem(6),
        out_specs=[pl.BlockSpec(memory_space=pl.ANY), in_vmem(1)[0]],
        out_shape=[
            jax.ShapeDtypeStruct((m, here + LANES), BF),
            held((heads, key_count, m), BF),
        ],
        scratch_shapes=[
            pltpu.VMEM((m, here + LANES), BF),
            pltpu.SemaphoreType.DMA((heads + 1,)),
        ],
        name="query_gradients",
    )(vmem(queries), vmem(grads), vmem(keys), vmem(values), vmem(probs), vmem(own))


def cache_kernel(queries, grads, probs, score_grads, own, merged):
    here = grads.shape[1]
    heads, key_count, _ = probs.shape

    def body(q_ref, g_ref, p_ref, ds_ref, own_ref, all_ref, dk_ref, dv_ref):
        share = jnp.exp(own_ref[0] - all_ref[0]) / all_ref[1]
        for h in range(heads):
            at = head_of(h)
            row = share[h : h + 1, :]
            ds = (ds_ref[h].astype(F32) * row).astype(BF)
            prob = (p_ref[h] * row).astype(BF)
            dk_ref[:, at] = nn(ds, query_head(q_ref, h, here)).astype(BF)
            dv_ref[:, at] = nn(prob, g_ref[:, at]).astype(BF)

    return pl.pallas_call(
        body,
        in_specs=in_vmem(6),
        out_specs=in_vmem(2),
        out_shape=[jax.ShapeDtypeStruct((key_count, here), BF)] * 2,
        name="cache_gradients",
    )(vmem(queries), vmem(grads), vmem(probs), vmem(score_grads), vmem(own), vmem(merged))


def combine_kernel(parts, sections, holders):
    width = parts.shape[1]
    rows = parts.shape[0] // (sections * holders)
    here = width - LANES
    heads = here // HEAD_DIM
    shape = (sections, holders, rows, HEAD_DIM)

    def body(p_ref, out_ref):
        stats = p_ref[:, pl.ds(here, LANES)]
        lane = lax.broadcasted_iota(jnp.int32, (LANES, HEAD_DIM), 0)
        for h in range(heads):
            mine = lane % heads == h
            first = mine & (lane < 3 * heads)
            second = mine & (lane >= 3 * heads) & (lane < 6 * heads)
            own = nn(stats, jnp.where(first, 1.0, 0.0).astype(BF)).reshape(shape)
            count = nn(stats, jnp.where(second, 1.0, 0.0).astype(BF)).reshape(shape)
            share = jnp.exp(own - jnp.max(own, axis=1, keepdims=True))
            total = jnp.sum(share * count, axis=1)
            value = p_ref[:, head_of(h)].astype(F32).reshape(shape)
            result = jnp.sum(share * value, axis=1) / total
            for s in range(sections):
                out_ref[:, head_of(s * heads + h)] = result[s].astype(BF)

    return pl.pallas_call(
        body,
        in_specs=in_vmem(1),
        out_specs=in_vmem(1)[0],
        out_shape=jax.ShapeDtypeStruct((rows, sections * here), BF),
        name="combine",
    )(vmem(parts))


def merge_stats(stats, axis, order):
    for bit in order:
        other = flip(stats, axis, 1 << bit)
        top = jnp.maximum(stats[0], other[0])
        total = stats[1] * jnp.exp(stats[0] - top) + other[1] * jnp.exp(other[0] - top)
        stats = jnp.stack([top, total])
    return stats


def flip(value, axis, bit):
    count = lax.axis_size(axis)
    return lax.ppermute(value, axis, [(i, i ^ bit) for i in range(count)])


def ordered(mine, other, upper, axis):
    first = jnp.where(upper, other, mine)
    second = jnp.where(upper, mine, other)
    return jnp.stack([first, second], axis)


def swap_blocks(blocks, axis):
    count = lax.axis_size(axis)
    here = lax.axis_index(axis)
    got = [blocks[0]]
    for step in range(1, count):
        got.append(flip(blocks[step], axis, step))
    bit = 1
    while bit < count:
        upper = here & bit != 0
        got = [jnp.where(upper, got[i ^ bit], got[i]) for i in range(count)]
        bit *= 2
    return jnp.stack(got)


def spread_blocks(blocks, axis, order):
    count = lax.axis_size(axis)
    lead, rest = blocks.shape[0], blocks.shape[1:]
    done = []
    for bit in order:
        upper = lax.axis_index(axis) & (1 << bit) != 0
        other = flip(blocks, axis, 1 << bit)
        blocks = ordered(blocks, other, upper, 1 + sum(b > bit for b in done))
        done.append(bit)
    return blocks.reshape((lead, count) + rest)


def exchange(blocks):
    return lax.all_to_all(blocks, ("section", "ctx"), 0, 0, tiled=True)


def compute(block_order, queries, cache_keys, cache_values, attention_out, output_grad):
    sections = lax.axis_size("section")
    ctx_count = lax.axis_size("ctx")
    assert ctx_count & (ctx_count - 1) == 0
    assert sections & (sections - 1) == 0 and sections > 1
    layers, rows, features = queries.shape
    assert layers == 1 and 3 * features // HEAD_DIM <= LANES
    key_count, here = cache_keys.shape
    row_count = rows * ctx_count
    key_total = key_count * ctx_count
    peers = sections * ctx_count

    ctx_bits = ctx_count.bit_length() - 1
    down = list(range(ctx_bits))[::-1]

    packed = pack(
        block_order,
        cache_keys,
        cache_values,
        queries[0],
        output_grad[0],
        attention_out[0],
        sections,
    )
    start, keys, values = packed[sections:]
    swapped = swap_blocks(packed[:sections], "section")
    deltas = sum(block[:, here : here + LANES] for block in swapped)
    sent = jnp.concatenate([*(block[:, :here] for block in swapped), deltas], axis=1)
    query_all = spread_blocks(sent[None], "ctx", down)
    query_all = query_all.reshape(row_count, -1)
    sent = jnp.stack([block[:, here + LANES :] for block in swapped])
    grad_all = spread_blocks(sent, "ctx", down[:1] + down[1:][::-1])
    grad_all = grad_all.reshape(peers * rows, here)

    own, probs = stats_kernel(start, query_all, keys, row_count, key_total)
    merged = merge_stats(own, "ctx", down[-1:] + down[:-1])
    part, score_grads = query_kernel(query_all, grad_all, keys, values, probs, own)
    part = exchange(part.reshape(peers, rows, here + LANES))
    grad_keys, grad_values = cache_kernel(query_all, grad_all, probs, score_grads, own, merged)
    part = part.reshape(peers * rows, here + LANES)
    grad_queries = combine_kernel(part, sections, ctx_count)
    return (grad_queries[None], grad_keys, grad_values)


def solution(mesh):
    in_specs = (
        P(),
        P("section", "ctx", None),
        P("ctx", "section"),
        P("ctx", "section"),
        P("section", "ctx", None),
        P("section", "ctx", None),
    )
    out_specs = (P("section", "ctx", None), P("ctx", "section"), P("ctx", "section"))
    return jax.shard_map(compute, mesh=mesh, in_specs=in_specs, out_specs=out_specs, check_vma=False)
```

```python
import math

import jax
import jax.numpy as jnp
from jax import lax
from jax.experimental import pallas as pl
from jax.experimental.pallas import tpu as pltpu
from jax.sharding import PartitionSpec as P


HEAD_DIM = 128
LANES = 128
ON_CHIP_BYTES = 1 << 20
masked_score = -1e30
BF = jnp.bfloat16
F32 = jnp.float32


def nt(a, b):
    return lax.dot_general(a, b, (((1,), (1,)), ((), ())), preferred_element_type=F32)


def nn(a, b):
    return lax.dot_general(a, b, (((1,), (0,)), ((), ())), preferred_element_type=F32)


def tn(a, b):
    return lax.dot_general(a, b, (((0,), (0,)), ((), ())), preferred_element_type=F32)


def split3(x):
    hi = x.astype(BF)
    rest = x - hi.astype(F32)
    mid = rest.astype(BF)
    low = (rest - mid.astype(F32)).astype(BF)
    return hi, mid, low


def in_vmem(count):
    return [pl.BlockSpec(memory_space=pltpu.VMEM) for _ in range(count)]


def small(shape, dtype):
    return math.prod(shape) * jnp.dtype(dtype).itemsize <= ON_CHIP_BYTES


def vmem(value):
    if small(value.shape, value.dtype):
        return pltpu.with_memory_space_constraint(value, pltpu.VMEM)
    return value


def held(shape, dtype):
    if small(shape, dtype):
        return pltpu.VMEM(shape, dtype)
    return jax.ShapeDtypeStruct(shape, dtype)


def head_of(h):
    return pl.ds(h * HEAD_DIM, HEAD_DIM)


def pack(queries, grads, outs, sections):
    rows, features = grads.shape
    here = features // sections
    heads = here // HEAD_DIM

    def body(q_hbm, g_hbm, o_hbm, *refs):
        blocks = refs[:sections]
        q_ref, g_ref, o_ref, sems = refs[sections:]
        pairs = [(q_hbm, q_ref), (g_hbm, g_ref), (o_hbm, o_ref)]
        copies = [pltpu.make_async_copy(*pair, sems.at[i]) for i, pair in enumerate(pairs)]
        for copy in copies:
            copy.start()
        section = lax.axis_index("section")
        lane = lax.broadcasted_iota(jnp.int32, (rows, LANES), 1)

        def at(s, h):
            return pl.ds(pl.multiple_of(s * here + h * HEAD_DIM, HEAD_DIM), HEAD_DIM)

        for copy in copies:
            copy.wait()
        for step, out_ref in enumerate(blocks):
            to = section ^ step
            extra = jnp.zeros((rows, LANES), F32)
            for h in range(heads):
                g = g_ref[:, at(to, h)]
                terms = g.astype(F32) * o_ref[:, at(to, h)].astype(F32)
                delta = jnp.sum(terms, axis=1, keepdims=True)
                for part, value in enumerate(split3(delta)):
                    mine = lane == (3 * section + part) * heads + h
                    extra = jnp.where(mine, value.astype(F32), extra)
                out_ref[:, head_of(h)] = q_ref[:, at(to, h)]
                out_ref[:, head_of(heads + 1 + h)] = g
            out_ref[:, head_of(heads)] = extra.astype(BF)

    return pl.pallas_call(
        body,
        in_specs=[pl.BlockSpec(memory_space=pl.ANY)] * 3,
        out_specs=in_vmem(sections),
        out_shape=[held((rows, 2 * here + LANES), BF)] * sections,
        scratch_shapes=[
            pltpu.VMEM((rows, features), BF),
            pltpu.VMEM((rows, features), BF),
            pltpu.VMEM((rows, features), BF),
            pltpu.SemaphoreType.DMA((3,)),
        ],
        name="pack",
    )(queries, grads, outs)


def fetch(block_order, keys, values):
    def body(order_hbm, k_hbm, v_hbm, start_ref, k_ref, v_ref, order_ref, sems):
        pairs = [(order_hbm, order_ref), (k_hbm, k_ref), (v_hbm, v_ref)]
        copies = [pltpu.make_async_copy(*pair, sems.at[i]) for i, pair in enumerate(pairs)]
        for copy in copies:
            copy.start()
        copies[0].wait()
        block = order_ref[lax.axis_index("ctx")]
        start_ref[...] = jnp.full(start_ref.shape, block * keys.shape[0], jnp.int32)
        copies[1].wait()
        copies[2].wait()

    return pl.pallas_call(
        body,
        in_specs=[pl.BlockSpec(memory_space=pl.ANY)] * 3,
        out_specs=in_vmem(3),
        out_shape=[
            held((8, LANES), jnp.int32),
            held(keys.shape, BF),
            held(values.shape, BF),
        ],
        scratch_shapes=[
            pltpu.SMEM(block_order.shape, jnp.int32),
            pltpu.SemaphoreType.DMA((3,)),
        ],
        name="fetch",
    )(block_order, keys, values)


def visible_of(start_ref, shape, row_count, key_total):
    key_pos = start_ref[0:1, 0:1] + lax.broadcasted_iota(jnp.int32, shape, 0)
    row = lax.broadcasted_iota(jnp.int32, shape, 1) % row_count
    return key_pos <= key_total - row_count + row


def query_head(q_ref, h, here):
    layers = (q_ref.shape[1] - LANES) // here
    parts = [q_ref[:, pl.ds(i * here + h * HEAD_DIM, HEAD_DIM)] for i in range(layers)]
    return jnp.concatenate(parts, axis=0)


def stats_kernel(start, queries, keys, row_count, key_total):
    key_count, here = keys.shape
    m = queries.shape[0] * ((queries.shape[1] - LANES) // here)
    heads = here // HEAD_DIM
    slots = -(-heads // 8) * 8
    scaling = HEAD_DIM ** (-0.5)

    def body(start_ref, q_ref, k_ref, out_ref, prob_ref):
        visible = visible_of(start_ref, (key_count, m), row_count, key_total)
        out_ref[...] = jnp.ones_like(out_ref)
        for h in range(heads):
            at = head_of(h)
            s = jnp.where(visible, nt(k_ref[:, at], query_head(q_ref, h, here)) * scaling, masked_score)
            top = jnp.max(s, axis=0, keepdims=True)
            prob = jnp.where(visible, jnp.exp(s - top), 0.0)
            prob_ref[h] = prob
            out_ref[0, pl.ds(h, 1), :] = top
            out_ref[1, pl.ds(h, 1), :] = jnp.sum(prob, axis=0, keepdims=True)

    return pl.pallas_call(
        body,
        in_specs=in_vmem(3),
        out_specs=in_vmem(2),
        out_shape=[
            held((2, slots, m), F32),
            held((heads, key_count, m), F32),
        ],
        name="stats",
    )(vmem(start), vmem(queries), vmem(keys))


def query_kernel(queries, grads, keys, values, probs, own):
    m = grads.shape[0]
    key_count, here = keys.shape
    heads = here // HEAD_DIM
    slots = own.shape[1]
    scaling = HEAD_DIM ** (-0.5)

    def body(q_ref, g_ref, k_ref, v_ref, p_ref, own_ref, u_hbm, ds_ref, u_ref, sems):
        def copy_of(h):
            return pltpu.make_async_copy(
                u_ref.at[:, head_of(h)], u_hbm.at[:, head_of(h)], sems.at[h]
            )

        slot = lax.broadcasted_iota(jnp.int32, (slots, LANES), 0)
        lane = lax.broadcasted_iota(jnp.int32, (slots, LANES), 1)
        width = 3 * heads
        layers = m // q_ref.shape[0]
        extra = q_ref[:, pl.ds(layers * here, LANES)]
        spot = lax.broadcasted_iota(jnp.int32, extra.shape, 1)
        parts = [jnp.where(spot // width == i, extra, jnp.zeros_like(extra)) for i in range(layers)]
        pick = (lane % heads == slot) & (lane < layers * width)
        pick = jnp.where(pick, 1.0, 0.0).astype(BF)
        deltas = nt(pick, jnp.concatenate(parts, axis=0))
        sent = jnp.zeros((m, LANES), F32)
        for i in range(2):
            for part, value in enumerate(split3(own_ref[i])):
                at = (3 * i + part) * heads
                place = (lane == at + slot) & (slot < heads)
                sent += tn(value, jnp.where(place, 1.0, 0.0).astype(BF))
        u_ref[:, head_of(heads)] = sent.astype(BF)
        copy_of(heads).start()
        for h in range(heads):
            at = head_of(h)
            ds = p_ref[h] * (nt(v_ref[:, at], g_ref[:, at]) - deltas[h : h + 1, :]) * scaling
            ds = ds.astype(BF)
            u_ref[:, at] = tn(ds, k_ref[:, at]).astype(BF)
            copy_of(h).start()
            ds_ref[h] = ds
        for h in range(heads + 1):
            copy_of(h).wait()

    return pl.pallas_call(
        body,
        in_specs=in_vmem(6),
        out_specs=[pl.BlockSpec(memory_space=pl.ANY), in_vmem(1)[0]],
        out_shape=[
            jax.ShapeDtypeStruct((m, here + LANES), BF),
            held((heads, key_count, m), BF),
        ],
        scratch_shapes=[
            pltpu.VMEM((m, here + LANES), BF),
            pltpu.SemaphoreType.DMA((heads + 1,)),
        ],
        name="query_gradients",
    )(vmem(queries), vmem(grads), vmem(keys), vmem(values), vmem(probs), vmem(own))


def cache_kernel(queries, grads, probs, score_grads, own, merged):
    here = grads.shape[1]
    heads, key_count, _ = probs.shape

    def body(q_ref, g_ref, p_ref, ds_ref, own_ref, all_ref, dk_ref, dv_ref):
        share = jnp.exp(own_ref[0] - all_ref[0]) / all_ref[1]
        for h in range(heads):
            at = head_of(h)
            row = share[h : h + 1, :]
            ds = (ds_ref[h].astype(F32) * row).astype(BF)
            prob = (p_ref[h] * row).astype(BF)
            dk_ref[:, at] = nn(ds, query_head(q_ref, h, here)).astype(BF)
            dv_ref[:, at] = nn(prob, g_ref[:, at]).astype(BF)

    return pl.pallas_call(
        body,
        in_specs=in_vmem(6),
        out_specs=in_vmem(2),
        out_shape=[jax.ShapeDtypeStruct((key_count, here), BF)] * 2,
        name="cache_gradients",
    )(vmem(queries), vmem(grads), vmem(probs), vmem(score_grads), vmem(own), vmem(merged))


def combine_kernel(parts, sections, holders):
    width = parts.shape[1]
    rows = parts.shape[0] // (sections * holders)
    here = width - LANES
    heads = here // HEAD_DIM
    shape = (sections, holders, rows, HEAD_DIM)

    def body(p_ref, out_ref):
        stats = p_ref[:, pl.ds(here, LANES)]
        lane = lax.broadcasted_iota(jnp.int32, (LANES, HEAD_DIM), 0)
        for h in range(heads):
            mine = lane % heads == h
            first = mine & (lane < 3 * heads)
            second = mine & (lane >= 3 * heads) & (lane < 6 * heads)
            own = nn(stats, jnp.where(first, 1.0, 0.0).astype(BF)).reshape(shape)
            count = nn(stats, jnp.where(second, 1.0, 0.0).astype(BF)).reshape(shape)
            share = jnp.exp(own - jnp.max(own, axis=1, keepdims=True))
            total = jnp.sum(share * count, axis=1)
            value = p_ref[:, head_of(h)].astype(F32).reshape(shape)
            result = jnp.sum(share * value, axis=1) / total
            for s in range(sections):
                out_ref[:, head_of(s * heads + h)] = result[s].astype(BF)

    return pl.pallas_call(
        body,
        in_specs=in_vmem(1),
        out_specs=in_vmem(1)[0],
        out_shape=jax.ShapeDtypeStruct((rows, sections * here), BF),
        name="combine",
    )(vmem(parts))


def merge_stats(stats, axis, order):
    for bit in order:
        other = flip(stats, axis, 1 << bit)
        top = jnp.maximum(stats[0], other[0])
        total = stats[1] * jnp.exp(stats[0] - top) + other[1] * jnp.exp(other[0] - top)
        stats = jnp.stack([top, total])
    return stats


def flip(value, axis, bit):
    count = lax.axis_size(axis)
    return lax.ppermute(value, axis, [(i, i ^ bit) for i in range(count)])


def ordered(mine, other, upper, axis):
    first = jnp.where(upper, other, mine)
    second = jnp.where(upper, mine, other)
    return jnp.stack([first, second], axis)


def swap_blocks(blocks, axis):
    count = lax.axis_size(axis)
    here = lax.axis_index(axis)
    got = [blocks[0]]
    for step in range(1, count):
        got.append(flip(blocks[step], axis, step))
    bit = 1
    while bit < count:
        upper = here & bit != 0
        got = [jnp.where(upper, got[i ^ bit], got[i]) for i in range(count)]
        bit *= 2
    return jnp.stack(got)


def spread_blocks(blocks, axis, order):
    count = lax.axis_size(axis)
    lead, rest = blocks.shape[0], blocks.shape[1:]
    done = []
    for bit in order:
        upper = lax.axis_index(axis) & (1 << bit) != 0
        other = flip(blocks, axis, 1 << bit)
        blocks = ordered(blocks, other, upper, 1 + sum(b > bit for b in done))
        done.append(bit)
    return blocks.reshape((lead, count) + rest)


def exchange(blocks):
    return lax.all_to_all(blocks, ("section", "ctx"), 0, 0, tiled=True)


def compute(block_order, queries, cache_keys, cache_values, attention_out, output_grad):
    sections = lax.axis_size("section")
    ctx_count = lax.axis_size("ctx")
    assert ctx_count & (ctx_count - 1) == 0
    assert sections & (sections - 1) == 0 and sections > 1
    layers, rows, features = queries.shape
    assert layers == 1 and 3 * features // HEAD_DIM <= LANES
    key_count, here = cache_keys.shape
    row_count = rows * ctx_count
    key_total = key_count * ctx_count
    peers = sections * ctx_count

    ctx_bits = ctx_count.bit_length() - 1
    down = list(range(ctx_bits))[::-1]

    packed = pack(queries[0], output_grad[0], attention_out[0], sections)
    start, keys, values = fetch(block_order, cache_keys, cache_values)
    swapped = swap_blocks(packed, "section")
    deltas = sum(block[:, here : here + LANES] for block in swapped)
    sent = jnp.concatenate([*(block[:, :here] for block in swapped), deltas], axis=1)
    query_all = spread_blocks(sent[None], "ctx", down)
    query_all = query_all.reshape(row_count, -1)
    sent = jnp.stack([block[:, here + LANES :] for block in swapped])
    grad_all = spread_blocks(sent, "ctx", down[:1] + down[1:][::-1])
    grad_all = grad_all.reshape(peers * rows, here)

    own, probs = stats_kernel(start, query_all, keys, row_count, key_total)
    merged = merge_stats(own, "ctx", down[-1:] + down[:-1])
    part, score_grads = query_kernel(query_all, grad_all, keys, values, probs, own)
    part = exchange(part.reshape(peers, rows, here + LANES))
    grad_keys, grad_values = cache_kernel(query_all, grad_all, probs, score_grads, own, merged)
    part = part.reshape(peers * rows, here + LANES)
    grad_queries = combine_kernel(part, sections, ctx_count)
    return (grad_queries[None], grad_keys, grad_values)


def solution(mesh):
    in_specs = (
        P(),
        P("section", "ctx", None),
        P("ctx", "section"),
        P("ctx", "section"),
        P("section", "ctx", None),
        P("section", "ctx", None),
    )
    out_specs = (P("section", "ctx", None), P("ctx", "section"), P("ctx", "section"))
    return jax.shard_map(compute, mesh=mesh, in_specs=in_specs, out_specs=out_specs, check_vma=False)
```
